128 devices in a mesh: grp: 4 (over y), cand: 32 (over x, z, core).
Axes of the slice: x: 4, y: 4, z: 4, core: 2. Of those that a mesh axis runs over, the one named last changes fastest.
Arguments:
- node_emb: bfloat16 [32, 512, 512], P('cand'), may hold values from -6 to 6
- rel_emb: float32 [900, 512], P('grp'), may hold values from -6 to 6
- w_in: bfloat16 [512, 512], replicated, may hold values from -0.25 to 0.25
- w_self: bfloat16 [512, 512], replicated, may hold values from -1 to 1
- rel_score: float32 [900, 512], replicated, may hold values from -7 to 7
- mirror_blocks: int32 [4, 32, 32, 1], P('grp', 'cand'), may hold values from 0 to 3
- adj_values: bfloat16 [4, 32, 192, 128, 128], P('grp', 'cand'), may hold values from -0.0390625 to 0.0390625
- adj_source: int32 [4, 32, 192], P('grp', 'cand'), may hold values from 0 to 31
- adj_target: int32 [4, 32, 192], P('grp', 'cand'), may hold values from 0 to 3
- adj_relation: int32 [4, 32, 192], P('grp', 'cand'), may hold values from 0 to 224
- live_blocks: int32 [4, 32], P('grp', 'cand'), may hold values from 48 to 192, as said below
- query_head: int32 [1024], replicated, may hold values from 0 to 16383
- query_rel: int32 [1024], replicated, may hold values from 0 to 899
- allowed: int32 [1024, 8], replicated, may hold values from 0 to 127, as said below
- true_tail: int32 [1024], replicated, may hold values from 0 to 16383, as said below
Outputs:
- h_out: bfloat16 [32, 512, 512], P('cand', 'grp')
- loss: float32 [1024], replicated
- grad_h: float32 [32, 512, 512], P('cand', 'grp')
- grad_rel: float32 [900, 512], P('grp')
- grad_w_in: float32 [512, 512], replicated
- grad_w_self: float32 [512, 512], replicated
The draws below stay inside these ranges and needn't reach their ends.
Inputs may be any that keep to these rules, and one draw needn't show every extreme that they name: `live_blocks`: blocks from this count on are padding; on some device all 192 blocks are live. `allowed`: ids of blocks of 128 concepts; a query may name a block twice. `true_tail`: lies in one of the query's allowed blocks.
All inputs are finite; a program needn't handle non-finite values.
Results may differ from the reference program's by a relative error of at most 0.011.
Values may be sent and summed in bfloat16 or wider, within the bound.
A program may use at most 128 MiB of HBM per device.

```python
import math
import jax
import jax.numpy as jnp
import numpy as np
from jax import lax

D = 512
REL = 900
BLOCK = 128
SLOT = 1
K_ALLOW = 8
NODE_DEV = 512
ADJ_BLK = 192
QUERIES = 1024
NODES = 16384
N_GRP = 4
N_CAND = 32


def sign_pattern(key):
    return jnp.where(jax.random.uniform(jax.random.fold_in(key, 77), (D,), jnp.float32) < 0.5, -1.0, 1.0)


def draw_w_self(key, part):
    rough = jnp.clip(jax.random.normal(jax.random.fold_in(key, 31), (D, D), jnp.float32), -4.0, 4.0) * D ** (-0.5)
    along = jnp.clip(jax.random.normal(jax.random.fold_in(key, 32), (D,), jnp.float32), -3.0, 3.0) * D ** (-0.5)
    value = rough + 2.0 * along[:, None] * sign_pattern(key)[None, :]
    return jnp.clip(value, -1.0, 1.0).astype(jnp.bfloat16)


def draw_rel_score(key, part):
    signs = jnp.where(jax.random.uniform(jax.random.fold_in(key, 1), (REL, D), jnp.float32) < 0.5, -1.0, 1.0)
    level = jnp.exp(jax.random.uniform(jax.random.fold_in(key, 4), (REL, 1), jnp.float32, jnp.log(5.5), jnp.log(7.5)))
    rough = jax.random.uniform(jax.random.fold_in(key, 5), (REL, D), jnp.float32, 0.9, 1.05)
    drawn = jnp.clip(signs * level * rough, -7.0, 7.0)
    order = jax.random.permutation(jax.random.fold_in(key, 6), REL)
    aligned = (order < max(1, REL // 4))[:, None]
    row_sign = jnp.where(jax.random.uniform(jax.random.fold_in(key, 7), (REL, 1), jnp.float32) < 0.5, -1.0, 1.0)
    strength = jax.random.uniform(jax.random.fold_in(key, 8), (REL, 1), jnp.float32, 6.6, 7.0)
    wobble = jax.random.uniform(jax.random.fold_in(key, 9), (REL, D), jnp.float32, 0.97, 1.0)
    lined = jnp.clip(row_sign * strength * wobble * sign_pattern(key)[None, :], -7.0, 7.0)
    return jnp.where(aligned, lined, drawn)


def draw_live_blocks(key, part):
    counts = jax.random.randint(key, (N_GRP * N_CAND,), ADJ_BLK // 4, ADJ_BLK + 1)
    busiest = jax.random.randint(jax.random.fold_in(key, 3), (), 0, N_GRP * N_CAND)
    counts = jnp.where(jnp.arange(N_GRP * N_CAND) == busiest, ADJ_BLK, counts)
    return counts.reshape(N_GRP, N_CAND).astype(jnp.int32)


def draw_query_head(key, part):
    base_key = jax.random.fold_in(key, 21)
    share = NODE_DEV // N_GRP
    share_count = N_GRP * N_CAND
    cover = jax.random.permutation(jax.random.fold_in(base_key, 1), share_count)
    extra = jax.random.randint(jax.random.fold_in(base_key, 2), (QUERIES,), 0, share_count)
    picks = jnp.where(jnp.arange(QUERIES) < share_count, jnp.pad(cover, (0, QUERIES - share_count)), extra)
    picks = jax.random.permutation(jax.random.fold_in(base_key, 3), picks)
    offset = jax.random.randint(jax.random.fold_in(base_key, 4), (QUERIES,), 0, share)
    offset = jnp.where(picks == 0, 0, jnp.where(picks == share_count - 1, share - 1, offset))
    return (picks * share + offset).astype(jnp.int32)


def allowed_helper(key):
    base_key = jax.random.fold_in(key, 11)
    block_count = NODES // BLOCK
    blocks = jax.random.randint(base_key, (QUERIES, K_ALLOW), 0, block_count)
    column = jax.random.randint(jax.random.fold_in(base_key, 1), (QUERIES,), 0, K_ALLOW)
    cover = jax.random.permutation(jax.random.fold_in(base_key, 3), block_count)
    order = jax.random.permutation(jax.random.fold_in(base_key, 4), QUERIES)
    current = jnp.take_along_axis(blocks, column[:, None], axis=1)[:, 0]
    padded_cover = jnp.pad(cover, (0, QUERIES - block_count))
    chosen = jnp.where(order < block_count, jnp.take(padded_cover, order), current)
    blocks = jnp.where(jnp.arange(K_ALLOW)[None, :] == column[:, None], chosen[:, None], blocks)
    offset = jax.random.randint(jax.random.fold_in(base_key, 2), (QUERIES,), 0, BLOCK)
    offset = jnp.where(chosen == 0, 0, jnp.where(chosen == block_count - 1, BLOCK - 1, offset))
    return (blocks.astype(jnp.int32), (chosen * BLOCK + offset).astype(jnp.int32))


def draw_allowed(key, part):
    blocks, tails = allowed_helper(key)
    return blocks


def draw_true_tail(key, part):
    blocks, tails = allowed_helper(key)
    return tails


def plant(values, stream_key, low, high):
    longest = values.shape.index(max(values.shape))
    spots = []
    for shift in (0, 1):
        where = [jax.random.randint(jax.random.fold_in(stream_key, axis), (), 0, length) for axis, length in enumerate(values.shape)]
        where[longest] = (where[longest] + shift) % values.shape[longest]
        spots.append(tuple(where))
    return values.at[spots[0]].set(low).at[spots[1]].set(high)


def levels(own_key, extent, pieces, least, top_value):
    loudness, own = 1.0, jax.random.fold_in(own_key, 6)
    for axis_at, blocks in pieces:
        heights = jnp.exp(jax.random.uniform(jax.random.fold_in(own, axis_at), (blocks,), jnp.float32, least / len(pieces), top_value / len(pieces)))
        loudness = loudness * jnp.repeat(heights, extent[axis_at] // blocks).reshape([-1 if axis == axis_at else 1 for axis in range(len(extent))])
    return loudness


def rank_bounds(number_of, lean):
    portions = [(1 << 20) // math.isqrt(grade ** lean) + 1 for grade in range(1, number_of + 1)]
    deviation = 1 + sum(portions) // (1 << 30)
    return np.cumsum(np.array([max(1, weight // deviation) for weight in portions]))


def ranked(own_key, shape, count, skew):
    table = rank_bounds(count, skew)
    lot = jax.random.randint(jax.random.fold_in(own_key, 1), shape, 0, int(table[count - 1]))
    grade = jnp.searchsorted(jnp.asarray(table, jnp.int32), lot, side="right")
    return jax.random.permutation(jax.random.fold_in(own_key, 2), count)[grade].astype(jnp.int32)


def gaussian(stream_key, dims, deviation, reach, cuts=(), kind=jnp.bfloat16):
    gain = levels(stream_key, dims, cuts, -0.22, 0.18) if cuts else 1.0
    result = jax.random.normal(stream_key, dims, jnp.float32) * deviation * gain
    return jnp.minimum(jnp.maximum(result, -reach), reach).astype(kind)


def setup_inputs(seed: int = 0) -> dict:
    keys = jax.random.split(jax.random.key(seed), 16)
    node_emb = gaussian(keys[0], (N_CAND, NODE_DEV, D), 1.0, 6.0, ((0, 32),))
    rel_emb = gaussian(keys[1], (REL, D), 1.0, 6.0, ((0, 4),), jnp.float32)
    w_in = gaussian(keys[2], (D, D), D ** -0.5, 0.25)
    w_self = draw_w_self(jax.random.fold_in(keys[15], 71), 0)
    rel_score = draw_rel_score(jax.random.fold_in(keys[15], 71), 0)
    mirror_blocks = plant(jax.random.randint(keys[5], (N_GRP, N_CAND, N_CAND, SLOT), 0, NODE_DEV // BLOCK), jax.random.fold_in(keys[5], 1), 0, (NODE_DEV // BLOCK) - 1).astype(jnp.int32)
    adj_values = gaussian(keys[6], (N_GRP, N_CAND, ADJ_BLK, BLOCK, BLOCK), (ADJ_BLK * N_GRP * BLOCK * BLOCK // NODE_DEV) ** -0.5, 0.0390625, ((0, 4), (1, 32)))
    adj_source = plant(jax.random.randint(keys[7], (N_GRP, N_CAND, ADJ_BLK), 0, N_CAND * SLOT), jax.random.fold_in(keys[7], 1), 0, (N_CAND * SLOT) - 1).astype(jnp.int32)
    adj_target = plant(jax.random.randint(keys[8], (N_GRP, N_CAND, ADJ_BLK), 0, NODE_DEV // BLOCK), jax.random.fold_in(keys[8], 1), 0, (NODE_DEV // BLOCK) - 1).astype(jnp.int32)
    adj_relation = plant(ranked(keys[9], (N_GRP, N_CAND, ADJ_BLK), REL // N_GRP, 2), jax.random.fold_in(keys[9], 3), 0, (REL // N_GRP) - 1).astype(jnp.int32)
    live_blocks = draw_live_blocks(jax.random.fold_in(keys[15], 71), 0)
    query_head = draw_query_head(jax.random.fold_in(keys[15], 71), 0)
    query_rel = plant(ranked(keys[12], (QUERIES,), REL, 2), jax.random.fold_in(keys[12], 3), 0, REL - 1).astype(jnp.int32)
    allowed = draw_allowed(jax.random.fold_in(keys[15], 71), 0)
    true_tail = draw_true_tail(jax.random.fold_in(keys[15], 71), 0)
    return dict(node_emb=node_emb, rel_emb=rel_emb, w_in=w_in, w_self=w_self, rel_score=rel_score, mirror_blocks=mirror_blocks, adj_values=adj_values, adj_source=adj_source, adj_target=adj_target, adj_relation=adj_relation, live_blocks=live_blocks, query_head=query_head, query_rel=query_rel, allowed=allowed, true_tail=true_tail)


NEG_FILL = -1.0e30
HIGH = lax.Precision.HIGHEST


def reference(node_emb, rel_emb, w_in, w_self, rel_score, mirror_blocks, adj_values, adj_source, adj_target, adj_relation, live_blocks, query_head, query_rel, allowed, true_tail):
    tile_count = NODE_DEV // BLOCK
    rels_local = REL // N_GRP
    node_total = N_CAND * NODE_DEV
    nodes = node_emb.reshape(node_total, D)
    tiled_nodes = nodes.reshape(N_CAND * tile_count, BLOCK, D)
    grp_ids = jnp.arange(N_GRP, dtype=jnp.int32)[:, None, None]
    cand_ids = jnp.arange(N_CAND, dtype=jnp.int32)[None, :, None]
    owner = adj_source // SLOT
    mirror_flat = mirror_blocks.reshape(N_GRP, N_CAND, N_CAND * SLOT)
    local_source = jnp.take_along_axis(mirror_flat, adj_source, axis=2)
    block_total = N_GRP * N_CAND * ADJ_BLK
    stride = math.gcd(block_total, 64)
    turns = block_total // stride
    source_tile = (owner * tile_count + local_source).reshape(turns, stride).astype(jnp.int32)
    target_tile = (cand_ids * tile_count + adj_target).reshape(turns, stride).astype(jnp.int32)
    relation_ids = (grp_ids * rels_local + adj_relation).reshape(turns, stride).astype(jnp.int32)
    live_mask = (jnp.arange(ADJ_BLK, dtype=jnp.int32)[None, None, :] < live_blocks[:, :, None]).astype(jnp.float32).reshape(turns, stride)
    tile_values = adj_values.reshape(turns, stride, BLOCK, BLOCK)
    packed = (tile_values, source_tile, target_tile, relation_ids, live_mask)

    def forward_turn(partial_value, inputs_now):
        values_now, source_now, target_now, relation_now, live_now = inputs_now
        composed = (tiled_nodes[source_now].astype(jnp.float32) - rel_emb[relation_now][:, None, :]).astype(jnp.bfloat16)
        messages = jnp.einsum("bij,bjd->bid", values_now.astype(jnp.float32), composed.astype(jnp.float32), precision=HIGH)
        messages = messages * live_now[:, None, None]
        return partial_value.at[target_now].add(messages), None

    partial_value, ignored = lax.scan(forward_turn, jnp.zeros((N_CAND * tile_count, BLOCK, D), jnp.float32), packed)
    aggregate = partial_value.reshape(node_total, D).astype(jnp.bfloat16)
    pre_act = jnp.dot(aggregate, w_in, preferred_element_type=jnp.float32) + jnp.dot(nodes, w_self, preferred_element_type=jnp.float32)
    activated = jnp.tanh(pre_act)
    h_out = activated.astype(jnp.bfloat16)

    cand_rows = h_out.astype(jnp.float32)
    queries = cand_rows[query_head] + rel_score[query_rel]
    scale = D ** -0.5
    cross = jnp.dot(queries, cand_rows.T, precision=HIGH)
    scores = -scale * (jnp.sum(queries * queries, axis=1)[:, None] + jnp.sum(cand_rows * cand_rows, axis=1)[None, :] - 2.0 * cross)
    block_total_c = node_total // BLOCK
    block_ok = jnp.any(allowed[:, :, None] == jnp.arange(block_total_c, dtype=jnp.int32)[None, None, :], axis=1)
    allowed_mask = jnp.repeat(block_ok, BLOCK, axis=1)
    tail_pick = true_tail[:, None] == jnp.arange(node_total, dtype=jnp.int32)[None, :]
    row_max = jnp.max(jnp.where(allowed_mask, scores, NEG_FILL), axis=1)
    row_total = jnp.sum(jnp.exp(jnp.where(allowed_mask, scores - row_max[:, None], NEG_FILL)), axis=1)
    truth = jnp.sum(jnp.where(tail_pick, scores, 0.0), axis=1)
    log_norm = row_max + jnp.log(row_total)
    loss = log_norm - truth

    prob = jnp.exp(jnp.where(allowed_mask, scores - log_norm[:, None], NEG_FILL))
    grad_score = (prob - tail_pick.astype(jnp.float32)) / QUERIES
    query_grad = 2.0 * scale * (jnp.dot(grad_score, cand_rows, precision=HIGH) - queries * jnp.sum(grad_score, axis=1)[:, None])
    cand_grad = 2.0 * scale * (jnp.dot(grad_score.T, queries, precision=HIGH) - cand_rows * jnp.sum(grad_score, axis=0)[:, None])
    row_grad = cand_grad + jnp.zeros((node_total, D), jnp.float32).at[query_head].add(query_grad)
    pre_grad = (row_grad * (1.0 - activated * activated)).astype(jnp.bfloat16)
    grad_w_in = jnp.dot(aggregate.T, pre_grad, preferred_element_type=jnp.float32)
    grad_w_self = jnp.dot(nodes.T, pre_grad, preferred_element_type=jnp.float32)
    agg_grad = jnp.dot(pre_grad, w_in.T, preferred_element_type=jnp.float32).astype(jnp.bfloat16)
    agg_tiles = agg_grad.reshape(N_CAND * tile_count, BLOCK, D)

    def backward_turn(carry, inputs_now):
        node_acc, relation_acc = carry
        values_now, source_now, target_now, relation_now, live_now = inputs_now
        composed_grad = jnp.einsum("bij,bid->bjd", values_now.astype(jnp.float32), agg_tiles[target_now].astype(jnp.float32), precision=HIGH)
        composed_grad = composed_grad * live_now[:, None, None]
        node_acc = node_acc.at[source_now].add(composed_grad)
        relation_acc = relation_acc.at[relation_now].add(-jnp.sum(composed_grad, axis=1))
        return (node_acc, relation_acc), None

    start = (jnp.zeros((N_CAND * tile_count, BLOCK, D), jnp.float32), jnp.zeros((REL, D), jnp.float32))
    (node_acc, grad_rel), ignored = lax.scan(backward_turn, start, packed)
    grad_h = node_acc.reshape(node_total, D) + jnp.dot(pre_grad, w_self.T, preferred_element_type=jnp.float32)
    return (h_out.reshape(N_CAND, NODE_DEV, D), loss, grad_h.reshape(N_CAND, NODE_DEV, D), grad_rel, grad_w_in, grad_w_self)
```

```python
import functools

import jax
import jax.numpy as jnp
from jax import lax
from jax.experimental import pallas as pl
from jax.experimental.pallas import tpu as pltpu
from jax.sharding import PartitionSpec as P

NEG_FILL = -1e30
MESH = pl.DeviceIdType.MESH
BF = jnp.bfloat16
F32 = jnp.float32
NN = (((1,), (0,)), ((), ()))
NT = (((1,), (1,)), ((), ()))
TN = (((0,), (0,)), ((), ()))
VMEM_SPEC = pl.BlockSpec(memory_space=pltpu.VMEM)
SMEM_SPEC = pl.BlockSpec(memory_space=pltpu.SMEM)
ANY_SPEC = pl.BlockSpec(memory_space=pl.ANY)
LIMIT = 60 * 1024 * 1024
STAGES = (("z", "x", "y"), ("x", "z", "y"))
STAGES_CAND = (("z", "x"), ("x", "z"))


def dot(a, b, dims=NN):
    return lax.dot_general(a, b, dims, preferred_element_type=F32)


class Place:
    def __init__(self):
        self.g = lax.axis_index("grp")
        self.c = lax.axis_index("cand")
        self.x = self.c // 8
        self.zk = self.c % 8
        self.z = self.zk // 2
        self.k = self.c % 2
        self.xk = self.x * 2 + self.k

    def dev(self, g, c):
        return {"grp": g, "cand": c}

    def at(self, axis):
        return {"x": self.x, "z": self.z, "y": self.g}[axis]

    def peer(self, axis, other):
        if axis == "y":
            return self.dev(other, self.c)
        if axis == "x":
            return self.dev(self.g, other * 8 + self.zk)
        return self.dev(self.g, self.x * 8 + other * 2 + self.k)

    def sibling(self):
        return self.dev(self.g, self.c + 1 - 2 * self.k)


def enter(devices):
    barrier = pltpu.get_barrier_semaphore()
    for device in devices:
        pl.semaphore_signal(barrier, inc=1, device_id=device, device_id_type=MESH)
    pl.semaphore_wait(barrier, len(devices))


def ring_devices(me):
    found = [me.sibling()]
    for axis in ("y", "x", "z"):
        for d in (1, 2, 3):
            found.append(me.peer(axis, (me.at(axis) + d) % 4))
    return found


class Wire:
    def __init__(self, send_sem, recv_sem):
        self.send_sem, self.recv_sem, self.count, self.sent = send_sem, recv_sem, 0, []

    def put(self, src, dst, device):
        at = self.count
        self.count += 1
        copy = pltpu.make_async_remote_copy(
            src_ref=src,
            dst_ref=dst,
            send_sem=self.send_sem.at[at],
            recv_sem=self.recv_sem.at[at],
            device_id=device,
            device_id_type=MESH,
        )
        copy.start()
        self.sent.append(copy)
        return copy

    def drain(self):
        for copy in self.sent:
            copy.wait_send()


def add_up(read_terms, write, count):
    chunk = min(count, 8)

    def one(i, carry):
        at = pl.ds(i * chunk, chunk)
        terms = read_terms(at)
        total = terms[0].astype(F32)
        for term in terms[1:]:
            total = total + term.astype(F32)
        write(at, total)
        return carry

    if count == chunk:
        one(0, 0)
    else:
        lax.fori_loop(0, count // chunk, one, 0)


class AllReduce:
    @staticmethod
    def scratch(shards, stages):
        depth = len(stages[0])
        shapes = [
            pltpu.VMEM((4, shards, 16, 128), BF),
            pltpu.VMEM((2, shards, 16, 128), BF),
            pltpu.VMEM((4, shards, 16, 128), BF),
        ]
        for level in range(depth):
            shapes.append(pltpu.VMEM((2, shards // 4**level, 16, 128), BF))
            shapes.append(pltpu.VMEM((2, 3, shards // 4 ** (level + 1), 16, 128), BF))
        return shapes

    def __init__(self, me, wire, shards, stages, refs):
        self.me, self.wire, self.shards, self.stages = me, wire, shards, stages
        self.part, self.rcore, self.out = refs[:3]
        depth = len(stages[0])
        self.acc = refs[3 : 3 + 2 * depth : 2]
        self.recv = refs[4 : 4 + 2 * depth : 2]
        self.sizes = [shards // 4 ** (i + 1) for i in range(depth)]

    def steps(self):
        me, wire = self.me, self.wire
        mine = 2 * me.k
        copy = wire.put(self.part.at[pl.ds(2 - mine, 2)], self.rcore, me.sibling())
        yield
        copy.wait_recv()
        for col in range(2):

            def write(at, value, col=col):
                self.acc[0][col, at] = value.astype(BF)

            add_up(
                lambda at, col=col: (self.part[mine + col, at], self.rcore[col, at]),
                write,
                self.shards,
            )
        offsets = [0, 0]
        history = []
        depth = len(self.sizes)
        for level in range(depth):
            size = self.sizes[level]
            copies = []
            for d in (1, 3, 2):
                for col in range(2):
                    axis = self.stages[col][level]
                    other = (me.at(axis) + d) % 4
                    copies.append(
                        wire.put(
                            self.acc[level].at[col, pl.ds(other * size, size)],
                            self.recv[level].at[col, d - 1],
                            me.peer(axis, other),
                        )
                    )
            yield
            for copy in copies:
                copy.wait_recv()
            for col in range(2):
                own = me.at(self.stages[col][level]) * size
                offsets[col] = offsets[col] + own

                def terms(at, col=col, own=own, level=level):
                    base = pl.ds(own + at.start, at.size)
                    return [self.acc[level][col, base]] + [
                        self.recv[level][col, d, at] for d in range(3)
                    ]

                def write(at, value, col=col, level=level):
                    if level + 1 < depth:
                        self.acc[level + 1][col, at] = value.astype(BF)
                    else:
                        self.out[mine + col, pl.ds(offsets[col] + at.start, at.size)] = (
                            value.astype(BF)
                        )

                add_up(terms, write, size)
            history.append(tuple(offsets))
        for level in reversed(range(depth)):
            size = self.sizes[level]
            copies = []
            for d in (1, 3, 2):
                for col in range(2):
                    axis = self.stages[col][level]
                    other = (me.at(axis) + d) % 4
                    place = self.out.at[mine + col, pl.ds(history[level][col], size)]
                    copies.append(wire.put(place, place, me.peer(axis, other)))
            yield
            for copy in copies:
                copy.wait_recv()
        place = self.out.at[pl.ds(mine, 2)]
        copy = wire.put(place, place, me.sibling())
        yield
        copy.wait_recv()

    def run(self):
        for ignored in self.steps():
            pass


def run_together(*reduces):
    live = [r.steps() for r in reduces]
    while live:
        still = []
        for steps in live:
            try:
                next(steps)
                still.append(steps)
            except StopIteration:
                pass
        live = still


def fetch_kernel(
    node, wanted_v, w_self,
    mirrors, requests, self_part,
    wanted_row, request_s, staged, send_sem, recv_sem, local_sem, *gathered,
):
    me = Place()
    devices = []
    for e in range(1, 8):
        devices.append(me.dev(me.g, me.x * 8 + (me.zk + e) % 8))
    for e in range(1, 8):
        other = (me.xk + e) % 8
        if e == 7:
            pass
        devices.append(me.dev(me.g, (other // 2) * 8 + me.z * 2 + other % 2))
    enter(devices)
    wire = Wire(send_sem, recv_sem)
    wanted_row[...] = jnp.zeros_like(wanted_row)
    wanted_row[:, 0:32] = wanted_v[...]
    halves = (pl.ds(0, 256), pl.ds(256, 256))
    first = {}
    for d in (1, 3, 2):
        for col, axis in ((0, "x"), (1, "z")):
            other = (me.at(axis) + d) % 4
            first[col, d] = wire.put(
                node.at[:, :, halves[col]], gathered[3 * col + d - 1], me.peer(axis, other)
            )
    asks = []
    for e in range(1, 8):
        for col in range(2):
            asks.append(
                wire.put(
                    wanted_row,
                    requests.at[8 * col + (me.zk if col == 0 else me.xk)],
                    devices[7 * col + e - 1],
                )
            )
    requests[me.zk] = wanted_row[...]
    requests[8 + me.xk] = wanted_row[...]
    for copy in asks:
        copy.wait_recv()
    local = pltpu.make_async_copy(requests, request_s, local_sem)
    local.start()
    local.wait()
    moved = []
    for d in (0, 1, 3, 2):
        for col, axis in ((0, "x"), (1, "z")):
            if d:
                first[col, d].wait_recv()
            origin = (me.at(axis) + 4 - d) % 4
            own_slot = me.zk if col == 0 else me.xk
            owner = origin * 8 + me.zk if col == 0 else me.x * 8 + origin * 2 + me.k
            for e in range(8):
                slot = (own_slot + e) % 8
                index = request_s[8 * col + slot, 0, owner]
                if d:
                    tile = gathered[3 * col + d - 1][index]
                else:
                    tile = node[index, :, 256 * col : 256 * col + 256]
                if e == 0:
                    mirrors[col, own_slot, origin] = tile
                else:
                    staged[col, e - 1, d] = tile
                    moved.append(
                        wire.put(
                            staged.at[col, e - 1, d],
                            mirrors.at[col, own_slot, origin],
                            devices[7 * col + e - 1],
                        )
                    )

    self_part[...] = dot(node[me.g], w_self[...])
    for copy in moved:
        copy.wait_recv()
    wire.drain()


def fetch(node_tiles, wanted, w_self):
    depth = node_tiles.shape[2]
    copies = 6 + 14 + 56
    return pl.pallas_call(
        fetch_kernel,
        name="fetch",
        out_shape=(
            jax.ShapeDtypeStruct((2, 8, 4, 128, 256), BF),
            jax.ShapeDtypeStruct((16, 1, 128), jnp.int32),
            jax.ShapeDtypeStruct((128, depth), F32),
        ),
        in_specs=[VMEM_SPEC] * 3,
        out_specs=(VMEM_SPEC,) * 3,
        scratch_shapes=[
            pltpu.VMEM((1, 128), jnp.int32),
            pltpu.SMEM((16, 1, 128), jnp.int32),
            pltpu.VMEM((2, 7, 4, 128, 256), BF),
            pltpu.SemaphoreType.DMA((copies,)),
            pltpu.SemaphoreType.DMA((copies,)),
            pltpu.SemaphoreType.DMA,
            *[pltpu.VMEM((4, 128, 256), BF)] * 6,
        ],
        compiler_params=pltpu.CompilerParams(
            collective_id=0, has_side_effects=True, vmem_limit_bytes=LIMIT
        ),
    )(node_tiles, wanted, w_self)


GROUP = 8


def slots_of(source):
    x, zk = source // 8, source % 8
    z, k = zk // 2, zk % 2
    return zk * 4 + x, (x * 2 + k) * 4 + z


def forward_kernel(
    source, target, relation, live, values, mirrors, rel_emb, query_rel, rel_score, out, query_part
):
    step = pl.program_id(0)

    @pl.when(step < query_part.shape[0] // 64)
    def _():
        def pick(i, carry):
            for j in range(8):
                row = step * 64 + i * 8 + j
                query_part[pl.ds(row, 1), :] = rel_score[pl.ds(query_rel[row], 1), :]
            return carry

        lax.fori_loop(0, 8, pick, 0)

    @pl.when(step == 0)
    def _():
        out[...] = jnp.zeros_like(out)

    count = live[0, 0]

    @pl.when(step * GROUP < count)
    def _():
        for j in range(GROUP):
            b = step * GROUP + j
            slots = slots_of(source[0, 0, b])
            t = target[0, 0, b]
            block = values[0, 0, j]
            block = jnp.where(b < count, block, jnp.zeros_like(block))
            row = rel_emb[pl.ds(relation[0, 0, b], 1), :]
            for col in range(2):
                part = slice(256 * col, 256 * col + 256)
                composed = (mirrors[col, slots[col]].astype(F32) - row[:, part]).astype(BF)
                out[t, :, part] += dot(block, composed)


def adjacency_specs(blocks):
    return [SMEM_SPEC] * 4 + [
        pl.BlockSpec((1, 1, GROUP, 128, 128), lambda i: (0, 0, i, 0, 0)),
    ]


def forward(
    adj_source, adj_target, adj_relation, live_blocks, adj_values, mirrors, rel_emb, query_rel, rel_score
):
    blocks = adj_values.shape[2]
    queries, depth = query_rel.shape[0], rel_score.shape[1]
    return pl.pallas_call(
        forward_kernel,
        name="forward_blocks",
        grid=(blocks // GROUP,),
        out_shape=(
            jax.ShapeDtypeStruct((4, 128, depth), F32),
            jax.ShapeDtypeStruct((queries, depth), F32),
        ),
        in_specs=adjacency_specs(blocks) + [VMEM_SPEC] * 2 + [SMEM_SPEC, VMEM_SPEC],
        out_specs=(VMEM_SPEC, VMEM_SPEC),
        compiler_params=pltpu.CompilerParams(vmem_limit_bytes=LIMIT),
    )(
        adj_source, adj_target, adj_relation, live_blocks, adj_values,
        mirrors.reshape(2, 32, 128, 256), rel_emb, query_rel, rel_score,
    )


def backward_kernel(source, target, relation, live, values, agg, tiles_out, rel_out, tiles):
    step = pl.program_id(0)

    @pl.when(step == 0)
    def _():
        def clear(i, carry):
            for col in range(2):
                tiles[col, i] = jnp.zeros((128, 256), F32)
            return carry

        lax.fori_loop(0, 32, clear, 0)
        rel_out[...] = jnp.zeros_like(rel_out)

    count = live[0, 0]

    @pl.when(step * GROUP < count)
    def _():
        for j in range(GROUP):
            b = step * GROUP + j
            slots = slots_of(source[0, 0, b])
            r = pl.ds(relation[0, 0, b], 1)
            block = values[0, 0, j]
            block = jnp.where(b < count, block, jnp.zeros_like(block))
            grad = dot(block, agg[target[0, 0, b]], TN)
            rel_out[r, :] -= jnp.sum(grad, axis=0, keepdims=True)
            for col in range(2):
                tiles[col, slots[col]] += grad[:, 256 * col : 256 * col + 256]

    @pl.when(step == pl.num_programs(0) - 1)
    def _():
        def store(i, carry):
            for col in range(2):
                tiles_out[col, i] = tiles[col, i].astype(BF)
            return carry

        lax.fori_loop(0, 32, store, 0)


def backward(adj_source, adj_target, adj_relation, live_blocks, adj_values, agg_tiles):
    blocks = adj_values.shape[2]
    return pl.pallas_call(
        backward_kernel,
        name="backward_blocks",
        grid=(blocks // GROUP,),
        out_shape=(
            jax.ShapeDtypeStruct((2, 32, 128, 256), BF),
            jax.ShapeDtypeStruct((256, 512), F32),
        ),
        in_specs=adjacency_specs(blocks) + [VMEM_SPEC],
        out_specs=(VMEM_SPEC, VMEM_SPEC),
        scratch_shapes=[pltpu.VMEM((2, 32, 128, 256), F32)],
        compiler_params=pltpu.CompilerParams(vmem_limit_bytes=LIMIT),
    )(adj_source, adj_target, adj_relation, live_blocks, adj_values, agg_tiles)


def middle_kernel(
    n_ar,
    partial, self_part, w_in, query_part, query_head, true_tail, allowed,
    h_out, loss, aggregate, pre_out, agg_tiles,
    share, recv_share, act, queries, q_hi, q_lo, ok, scores, stats, cand_grad, col_sum, head_grad, *rest,
):
    ar_refs, (send_sem, recv_sem) = rest[: 2 * n_ar], rest[2 * n_ar :]
    me = Place()
    enter(ring_devices(me))
    wire = Wire(send_sem, recv_sem)
    head_sum = AllReduce(me, wire, 64, STAGES, ar_refs[:n_ar])
    grad_sum = AllReduce(me, wire, 64, STAGES, ar_refs[n_ar:])
    count = queries.shape[0]
    chunks = count // 128
    scale = 512 ** (-0.5)
    copies = []
    for d in (1, 3, 2):
        other = (me.g + d) % 4
        copies.append(wire.put(partial.at[other], recv_share.at[d - 1], me.peer("y", other)))
    for copy in copies:
        copy.wait_recv()
    total = partial[me.g] + recv_share[0] + recv_share[1] + recv_share[2]
    agg = total.astype(BF)
    aggregate[...] = agg
    activated = jnp.tanh(dot(agg, w_in[...]) + self_part[...])
    act[...] = activated
    h = activated.astype(BF)
    h_out[0] = h
    share[...] = h
    first_row = me.c * 512 + me.g * 128
    block_id = me.c * 4 + me.g

    def rows_match(ids, lanes):
        row_ids = first_row + lax.broadcasted_iota(jnp.int32, (128, 128), 0)
        return row_ids == jnp.broadcast_to(ids[:, lanes], (128, 128))

    def lanes_of(i):
        return pl.ds(pl.multiple_of(i * 128, 128), 128)

    def head_chunk(i, carry):
        pick = rows_match(query_head, lanes_of(i)).astype(F32).T.astype(BF)
        part = dot(pick, share[...]).astype(BF).astype(F32)
        for j in range(4):
            head_sum.part[j, pl.ds(i * 8, 8)] = (
                part[:, 128 * j : 128 * j + 128].reshape(8, 16, 128).astype(BF)
            )
        return carry

    lax.fori_loop(0, chunks, head_chunk, 0)
    head_sum.run()

    h32 = share[...].astype(F32)
    h_sq = jnp.sum(h32 * h32, axis=1, keepdims=True)

    def score_chunk(i, carry):
        lanes = lanes_of(i)
        rows = lanes
        square = jnp.zeros((128, 128), F32)
        for j in range(4):
            cols = slice(128 * j, 128 * j + 128)
            head = head_sum.out[j, pl.ds(i * 8, 8)].astype(F32).reshape(128, 128)
            q = head + query_part[rows, cols]
            queries[rows, cols] = q
            high = q.astype(BF)
            q_hi[rows, cols] = high
            q_lo[rows, cols] = (q - high.astype(F32)).astype(BF)
            square = square + q * q
        q_sq = jnp.sum(square.T, axis=0, keepdims=True)
        cross = dot(share[...], q_hi[rows, :], NT) + dot(share[...], q_lo[rows, :], NT)
        score = -scale * (q_sq + h_sq - 2.0 * cross)
        found = jnp.max(
            jnp.where(allowed[rows, :] == block_id, 1.0, 0.0), axis=1, keepdims=True
        )
        mask = jnp.broadcast_to(found, (128, 128)).T
        ok[:, lanes] = mask
        scores[:, lanes] = score
        seen = jnp.where(mask > 0.5, score, NEG_FILL)
        top = jnp.max(seen, axis=0, keepdims=True)
        weight = jnp.sum(
            jnp.exp(jnp.where(mask > 0.5, score - top, NEG_FILL)), axis=0, keepdims=True
        )
        truth = jnp.sum(
            jnp.where(rows_match(true_tail, lanes), score, 0.0), axis=0, keepdims=True
        )
        stats[0, 0, 0, :, lanes] = top
        stats[0, 0, 1, :, lanes] = weight
        stats[0, 0, 2, :, lanes] = truth
        return carry

    lax.fori_loop(0, chunks, score_chunk, 0)

    for level, axis in enumerate(("core", "y", "x", "z")):
        copies = []
        if axis == "core":
            copies.append(wire.put(stats.at[level, 0], stats.at[level, 1], me.sibling()))
        else:
            for d in (1, 3, 2):
                other = (me.at(axis) + d) % 4
                copies.append(
                    wire.put(stats.at[level, 0], stats.at[level, d], me.peer(axis, other))
                )
        for copy in copies:
            copy.wait_recv()
        members = range(len(copies) + 1)
        tops = [stats[level, m, 0] for m in members]
        top = functools.reduce(jnp.maximum, tops)
        stats[level + 1, 0, 0] = top
        stats[level + 1, 0, 1] = functools.reduce(
            lambda a, b: a + b, [stats[level, m, 1] * jnp.exp(tops[m] - top) for m in members]
        )
        stats[level + 1, 0, 2] = functools.reduce(
            lambda a, b: a + b, [stats[level, m, 2] for m in members]
        )
    row_max = stats[4, 0, 0]
    log_norm = row_max + jnp.log(stats[4, 0, 1])
    loss[...] = log_norm - stats[4, 0, 2]
    stats[4, 1, 0] = log_norm
    stats[4, 1, 1] = (stats[4, 0, 1] * jnp.exp(row_max - log_norm) - 1.0) / count

    cand_grad[...] = jnp.zeros_like(cand_grad)
    col_sum[...] = jnp.zeros_like(col_sum)

    def grad_chunk(i, carry):
        lanes = lanes_of(i)
        norm = jnp.broadcast_to(stats[4, 1, 0, :, lanes], (128, 128))
        prob = jnp.exp(jnp.where(ok[:, lanes] > 0.5, scores[:, lanes] - norm, NEG_FILL))
        tail = jnp.where(rows_match(true_tail, lanes), 1.0, 0.0)
        grad = (prob - tail) / count
        flipped = grad.T
        high = flipped.astype(BF)
        low = (flipped - high.astype(F32)).astype(BF)
        part = dot(high, share[...]) + dot(low, share[...])
        for j in range(4):
            grad_sum.part[j, pl.ds(i * 8, 8)] = (
                part[:, 128 * j : 128 * j + 128].reshape(8, 16, 128).astype(BF)
            )
        high = grad.astype(BF)
        low = (grad - high.astype(F32)).astype(BF)
        cand_grad[...] += (
            dot(high, q_hi[lanes, :]) + dot(high, q_lo[lanes, :]) + dot(low, q_hi[lanes, :])
        )
        col_sum[...] += grad
        return carry

    lax.fori_loop(0, chunks, grad_chunk, 0)
    grad_sum.run()

    head_grad[...] = jnp.zeros_like(head_grad)

    def head_grad_chunk(i, carry):
        lanes = lanes_of(i)
        rest_sum = jnp.broadcast_to(stats[4, 1, 1, :, lanes], (128, 128)).T
        pick = rows_match(query_head, lanes).astype(F32).astype(BF)
        for j in range(4):
            cols = slice(128 * j, 128 * j + 128)
            summed = grad_sum.out[j, pl.ds(i * 8, 8)].astype(F32).reshape(128, 128)
            query_grad = (summed - queries[lanes, cols] * rest_sum).astype(BF)
            head_grad[:, cols] += dot(pick, query_grad)
        return carry

    lax.fori_loop(0, chunks, head_grad_chunk, 0)
    sums = jnp.sum(col_sum[...], axis=1, keepdims=True)
    row_grad = (2.0 * scale) * (
        cand_grad[...] - share[...].astype(F32) * sums + head_grad[...]
    )
    activated = act[...]
    pre_grad = (row_grad * (1.0 - activated * activated)).astype(BF)
    pre_out[...] = pre_grad
    agg_tiles[me.g] = dot(pre_grad, w_in[...], NT).astype(BF)
    copies = []
    for d in (1, 3, 2):
        other = (me.g + d) % 4
        copies.append(wire.put(agg_tiles.at[me.g], agg_tiles.at[me.g], me.peer("y", other)))
    for copy in copies:
        copy.wait_recv()
    wire.drain()


def middle(partial, self_part, w_in, query_part, query_head, true_tail, allowed):
    count = query_head.shape[1]
    depth = w_in.shape[0]
    ar = AllReduce.scratch(64, STAGES)
    copies = 3 + 2 * (1 + 18 + 18 + 1) + 1 + 9 + 3
    return pl.pallas_call(
        functools.partial(middle_kernel, len(ar)),
        name="middle",
        out_shape=(
            jax.ShapeDtypeStruct((1, 128, depth), BF),
            jax.ShapeDtypeStruct((1, count), F32),
            jax.ShapeDtypeStruct((128, depth), BF),
            jax.ShapeDtypeStruct((128, depth), BF),
            jax.ShapeDtypeStruct((4, 128, depth), BF),
        ),
        in_specs=[VMEM_SPEC] * 7,
        out_specs=(VMEM_SPEC,) * 5,
        scratch_shapes=[
            pltpu.VMEM((128, depth), BF),
            pltpu.VMEM((3, 128, depth), F32),
            pltpu.VMEM((128, depth), F32),
            pltpu.VMEM((count, depth), F32),
            pltpu.VMEM((count, depth), BF),
            pltpu.VMEM((count, depth), BF),
            pltpu.VMEM((128, count), F32),
            pltpu.VMEM((128, count), F32),
            pltpu.VMEM((5, 4, 3, 1, count), F32),
            pltpu.VMEM((128, depth), F32),
            pltpu.VMEM((128, 128), F32),
            pltpu.VMEM((128, depth), F32),
            *ar,
            *ar,
            pltpu.SemaphoreType.DMA((copies,)),
            pltpu.SemaphoreType.DMA((copies,)),
        ],
        compiler_params=pltpu.CompilerParams(
            collective_id=1, has_side_effects=True, vmem_limit_bytes=LIMIT
        ),
    )(partial, self_part, w_in, query_part, query_head, true_tail, allowed)


def return_kernel(
    n_w, n_r,
    tiles, rel_part, aggregate, pre_grad, node, w_self, requests,
    node_grad, rel_grad, w_in_grad, w_self_grad,
    arrived, shipped, joined, own_sum, y_send, y_recv, self_grad, *rest,
):
    w_refs, r_refs = rest[:n_w], rest[n_w : n_w + n_r]
    send_sem, recv_sem, local_sem = rest[n_w + n_r :]
    me = Place()
    devices = []
    for e in range(1, 8):
        devices.append(me.dev(me.g, me.x * 8 + (me.zk + e) % 8))
    for e in range(1, 8):
        other = (me.xk + e) % 8
        devices.append(me.dev(me.g, (other // 2) * 8 + me.z * 2 + other % 2))
    for d in (1, 2, 3):
        devices.append(me.peer("y", (me.g + d) % 4))
    enter(devices)
    wire = Wire(send_sem, recv_sem)
    w_sum = AllReduce(me, wire, 64, STAGES, w_refs)
    r_sum = AllReduce(me, wire, 16, STAGES_CAND, r_refs)
    axes = ((0, "x"), (1, "z"))
    order = (1, 3, 2, 0)
    own_slots = (me.zk, me.xk)
    moved = {}
    for d in order:
        for col, axis in axes:
            place = (me.at(axis) + d) % 4
            for e in range(1, 8):
                slot = (own_slots[col] + e) % 8
                moved[d, col, e] = wire.put(
                    tiles.at[col, slot, place],
                    arrived.at[col, own_slots[col], place],
                    devices[7 * col + e - 1],
                )
    local = []
    for col in range(2):
        copy = pltpu.make_async_copy(
            tiles.at[col, own_slots[col]], arrived.at[col, own_slots[col]], local_sem.at[col]
        )
        copy.start()
        local.append(copy)
    own = node[0, pl.ds(pl.multiple_of(me.g * 128, 128), 128), :]
    self_grad[...] = dot(pre_grad[...], w_self[...], NT)
    for at, left in ((0, aggregate[...]), (32, own)):
        for q in range(4):
            turned = left[:, 128 * q : 128 * q + 128].astype(F32).T.astype(BF)
            part = dot(turned, pre_grad[...])
            for j in range(4):
                w_sum.part[j, at + 8 * q : at + 8 * q + 8] = (
                    part[:, 128 * j : 128 * j + 128].reshape(8, 16, 128).astype(BF)
                )
    for q in range(2):
        for j in range(4):
            r_sum.part[j, 8 * q : 8 * q + 8] = (
                rel_part[128 * q : 128 * q + 128, 128 * j : 128 * j + 128]
                .reshape(8, 16, 128)
                .astype(BF)
            )
    for copy in local:
        copy.wait()
    second = []
    for d in order:
        for col, axis in axes:
            place = (me.at(axis) + d) % 4
            owner = place * 8 + me.zk if col == 0 else me.x * 8 + place * 2 + me.k
            for e in range(1, 8):
                moved[d, col, e].wait_recv()
            index = [requests[8 * col + m, 0, owner] for m in range(8)]
            for part in range(4):
                rows = pl.ds(part * 32, 32)
                values = [arrived[col, m, place, rows, :].astype(F32) for m in range(8)]
                for s in range(4):
                    total = jnp.zeros((32, 256), F32)
                    for m in range(8):
                        total = total + jnp.where(index[m] == s, values[m], 0.0)
                    if d == 0:
                        own_sum[col, s, rows, :] = total
                    else:
                        shipped[col, d - 1, s, rows, :] = total.astype(BF)
            if d:
                second.append(
                    wire.put(
                        shipped.at[col, d - 1], joined.at[col, d - 1], me.peer(axis, place)
                    )
                )
    for copy in second:
        copy.wait_recv()
    third = []
    for d in (1, 3, 2, 0):
        s = (me.g + d) % 4
        for col in range(2):
            total = own_sum[col, s]
            for m in range(3):
                total = total + joined[col, m, s].astype(F32)
            if d == 0:
                own_sum[col, s] = total
            else:
                y_send[col, d - 1] = total.astype(BF)
                third.append(
                    wire.put(y_send.at[col, d - 1], y_recv.at[col, d - 1], me.peer("y", s))
                )
    for copy in third:
        copy.wait_recv()
    for col in range(2):
        total = own_sum[col, me.g]
        for m in range(3):
            total = total + y_recv[col, m].astype(F32)
        node_grad[0, :, 256 * col : 256 * col + 256] = (
            total + self_grad[:, 256 * col : 256 * col + 256]
        )
    run_together(w_sum, r_sum)
    for j in range(4):
        cols = slice(128 * j, 128 * j + 128)
        for q in range(4):
            rows = slice(128 * q, 128 * q + 128)
            w_in_grad[rows, cols] = w_sum.out[j, 8 * q : 8 * q + 8].astype(F32).reshape(128, 128)
            w_self_grad[rows, cols] = (
                w_sum.out[j, 32 + 8 * q : 40 + 8 * q].astype(F32).reshape(128, 128)
            )
        both = r_sum.out[j].astype(F32).reshape(256, 128)
        rel_grad[:, cols] = both[: rel_grad.shape[0]]
    wire.drain()


def give_back(tiles, rel_part, aggregate, pre_grad, node_emb, w_self, requests, relations):
    depth = w_self.shape[0]
    w_ar = AllReduce.scratch(64, STAGES)
    r_ar = AllReduce.scratch(16, STAGES_CAND)
    copies = 56 + 6 + 6 + (1 + 18 + 18 + 1) + (1 + 12 + 12 + 1)
    return pl.pallas_call(
        functools.partial(return_kernel, len(w_ar), len(r_ar)),
        name="give_back",
        out_shape=(
            jax.ShapeDtypeStruct((1, 128, depth), F32),
            jax.ShapeDtypeStruct((relations, depth), F32),
            jax.ShapeDtypeStruct((depth, depth), F32),
            jax.ShapeDtypeStruct((depth, depth), F32),
        ),
        in_specs=[ANY_SPEC] + [VMEM_SPEC] * 5 + [SMEM_SPEC],
        out_specs=(VMEM_SPEC,) * 4,
        scratch_shapes=[
            pltpu.VMEM((2, 8, 4, 128, 256), BF),
            pltpu.VMEM((2, 3, 4, 128, 256), BF),
            pltpu.VMEM((2, 3, 4, 128, 256), BF),
            pltpu.VMEM((2, 4, 128, 256), F32),
            pltpu.VMEM((2, 3, 128, 256), BF),
            pltpu.VMEM((2, 3, 128, 256), BF),
            pltpu.VMEM((128, depth), F32),
            *w_ar,
            *r_ar,
            pltpu.SemaphoreType.DMA((copies,)),
            pltpu.SemaphoreType.DMA((copies,)),
            pltpu.SemaphoreType.DMA((2,)),
        ],
        compiler_params=pltpu.CompilerParams(
            collective_id=2, has_side_effects=True, vmem_limit_bytes=LIMIT
        ),
    )(tiles, rel_part, aggregate, pre_grad, node_emb, w_self, requests)


def body(
    node_emb,
    rel_emb,
    w_in,
    w_self,
    rel_score,
    mirror_blocks,
    adj_values,
    adj_source,
    adj_target,
    adj_relation,
    live_blocks,
    query_head,
    query_rel,
    allowed,
    true_tail,
):
    wanted = mirror_blocks.reshape(1, 32)
    mirrors, requests, self_part = fetch(node_emb.reshape(4, 128, -1), wanted, w_self)
    partial, query_part = forward(
        adj_source, adj_target, adj_relation, live_blocks, adj_values, mirrors, rel_emb,
        query_rel, rel_score,
    )
    h_out, loss, aggregate, pre_grad, agg_tiles = middle(
        partial,
        self_part,
        w_in,
        query_part,
        query_head.reshape(1, -1),
        true_tail.reshape(1, -1),
        allowed,
    )
    tiles, rel_part = backward(
        adj_source, adj_target, adj_relation, live_blocks, adj_values, agg_tiles
    )
    node_grad, rel_grad, w_in_grad, w_self_grad = give_back(
        tiles.reshape(2, 8, 4, 128, 256),
        rel_part,
        aggregate,
        pre_grad,
        node_emb,
        w_self,
        requests,
        rel_emb.shape[0],
    )
    return (h_out, loss.reshape(-1), node_grad, rel_grad, w_in_grad, w_self_grad)


def solution(mesh):
    return jax.shard_map(
        body,
        mesh=mesh,
        in_specs=(
            P("cand", None, None),
            P("grp", None),
            P(),
            P(),
            P(),
            P("grp", "cand", None, None),
            P("grp", "cand", None, None, None),
            P("grp", "cand", None),
            P("grp", "cand", None),
            P("grp", "cand", None),
            P("grp", "cand"),
            P(),
            P(),
            P(),
            P(),
        ),
        out_specs=(P("cand", "grp", None), P(), P("cand", "grp", None), P("grp", None), P(), P()),
        check_vma=False,
    )
```

```python
import functools

import jax
import jax.numpy as jnp
from jax import lax
from jax.experimental import pallas as pl
from jax.experimental.pallas import tpu as pltpu
from jax.sharding import PartitionSpec as P

NEG_FILL = -1e30
MESH = pl.DeviceIdType.MESH
BF = jnp.bfloat16
F32 = jnp.float32
NN = (((1,), (0,)), ((), ()))
NT = (((1,), (1,)), ((), ()))
TN = (((0,), (0,)), ((), ()))
VMEM_SPEC = pl.BlockSpec(memory_space=pltpu.VMEM)
SMEM_SPEC = pl.BlockSpec(memory_space=pltpu.SMEM)
ANY_SPEC = pl.BlockSpec(memory_space=pl.ANY)
LIMIT = 60 * 1024 * 1024
STAGES_CAND = (("z", "x"), ("x", "z"))


def dot(a, b, dims=NN):
    return lax.dot_general(a, b, dims, preferred_element_type=F32)


class Place:
    def __init__(self):
        self.g = lax.axis_index("grp")
        self.c = lax.axis_index("cand")
        self.x = self.c // 8
        self.zk = self.c % 8
        self.z = self.zk // 2
        self.k = self.c % 2
        self.xk = self.x * 2 + self.k

    def dev(self, g, c):
        return {"grp": g, "cand": c}

    def at(self, axis):
        return {"x": self.x, "z": self.z, "y": self.g}[axis]

    def peer(self, axis, other):
        if axis == "y":
            return self.dev(other, self.c)
        if axis == "x":
            return self.dev(self.g, other * 8 + self.zk)
        return self.dev(self.g, self.x * 8 + other * 2 + self.k)

    def sibling(self):
        return self.dev(self.g, self.c + 1 - 2 * self.k)


def enter(devices):
    barrier = pltpu.get_barrier_semaphore()
    for device in devices:
        pl.semaphore_signal(barrier, inc=1, device_id=device, device_id_type=MESH)
    pl.semaphore_wait(barrier, len(devices))


def ring_devices(me):
    found = [me.sibling()]
    for axis in ("y", "x", "z"):
        for d in (1, 2, 3):
            found.append(me.peer(axis, (me.at(axis) + d) % 4))
    return found


class Wire:
    def __init__(self, send_sem, recv_sem):
        self.send_sem, self.recv_sem, self.count, self.sent = send_sem, recv_sem, 0, []

    def put(self, src, dst, device):
        at = self.count
        self.count += 1
        copy = pltpu.make_async_remote_copy(
            src_ref=src,
            dst_ref=dst,
            send_sem=self.send_sem.at[at],
            recv_sem=self.recv_sem.at[at],
            device_id=device,
            device_id_type=MESH,
        )
        copy.start()
        self.sent.append(copy)
        return copy

    def drain(self):
        for copy in self.sent:
            copy.wait_send()


def add_up(read_terms, write, count):
    chunk = min(count, 8)

    def one(i, carry):
        at = pl.ds(i * chunk, chunk)
        terms = read_terms(at)
        total = terms[0].astype(F32)
        for term in terms[1:]:
            total = total + term.astype(F32)
        write(at, total)
        return carry

    if count == chunk:
        one(0, 0)
    else:
        lax.fori_loop(0, count // chunk, one, 0)


class AllReduce:
    @staticmethod
    def scratch(shards, stages, height):
        depth = len(stages[0])
        shapes = [
            pltpu.VMEM((4, shards, height, 128), BF),
            pltpu.VMEM((2, shards, height, 128), BF),
            pltpu.VMEM((4, shards, height, 128), BF),
        ]
        for level in range(depth):
            shapes.append(pltpu.VMEM((2, shards // 4**level, height, 128), BF))
            shapes.append(pltpu.VMEM((2, 3, shards // 4 ** (level + 1), height, 128), BF))
        return shapes

    def __init__(self, me, wire, shards, stages, refs):
        self.me, self.wire, self.shards, self.stages = me, wire, shards, stages
        self.part, self.rcore, self.out = refs[:3]
        depth = len(stages[0])
        self.acc = refs[3 : 3 + 2 * depth : 2]
        self.recv = refs[4 : 4 + 2 * depth : 2]
        self.sizes = [shards // 4 ** (i + 1) for i in range(depth)]

    def steps(self):
        me, wire = self.me, self.wire
        mine = 2 * me.k
        copy = wire.put(self.part.at[pl.ds(2 - mine, 2)], self.rcore, me.sibling())
        yield
        copy.wait_recv()
        for col in range(2):

            def write(at, value, col=col):
                self.acc[0][col, at] = value.astype(BF)

            add_up(
                lambda at, col=col: (self.part[mine + col, at], self.rcore[col, at]),
                write,
                self.shards,
            )
        offsets = [0, 0]
        history = []
        depth = len(self.sizes)
        for level in range(depth):
            size = self.sizes[level]
            copies = []
            for d in (1, 3, 2):
                for col in range(2):
                    axis = self.stages[col][level]
                    other = (me.at(axis) + d) % 4
                    copies.append(
                        wire.put(
                            self.acc[level].at[col, pl.ds(other * size, size)],
                            self.recv[level].at[col, d - 1],
                            me.peer(axis, other),
                        )
                    )
            yield
            for copy in copies:
                copy.wait_recv()
            for col in range(2):
                own = me.at(self.stages[col][level]) * size
                offsets[col] = offsets[col] + own

                def terms(at, col=col, own=own, level=level):
                    base = pl.ds(own + at.start, at.size)
                    return [self.acc[level][col, base]] + [
                        self.recv[level][col, d, at] for d in range(3)
                    ]

                def write(at, value, col=col, level=level):
                    if level + 1 < depth:
                        self.acc[level + 1][col, at] = value.astype(BF)
                    else:
                        self.out[mine + col, pl.ds(offsets[col] + at.start, at.size)] = (
                            value.astype(BF)
                        )

                add_up(terms, write, size)
            history.append(tuple(offsets))
        for level in reversed(range(depth)):
            size = self.sizes[level]
            copies = []
            for d in (1, 3, 2):
                for col in range(2):
                    axis = self.stages[col][level]
                    other = (me.at(axis) + d) % 4
                    place = self.out.at[mine + col, pl.ds(history[level][col], size)]
                    copies.append(wire.put(place, place, me.peer(axis, other)))
            yield
            for copy in copies:
                copy.wait_recv()


def fetch_kernel(
    node, wanted_v, w_self,
    mirrors, requests, self_part,
    wanted_row, request_s, staged, send_sem, recv_sem, local_sem, *gathered,
):
    me = Place()
    devices = []
    for e in range(1, 8):
        devices.append(me.dev(me.g, me.x * 8 + (me.zk + e) % 8))
    for e in range(1, 8):
        other = (me.xk + e) % 8
        if e == 7:
            pass
        devices.append(me.dev(me.g, (other // 2) * 8 + me.z * 2 + other % 2))
    enter(devices)
    wire = Wire(send_sem, recv_sem)
    wanted_row[...] = jnp.zeros_like(wanted_row)
    wanted_row[:, 0:32] = wanted_v[...]
    halves = (pl.ds(0, 256), pl.ds(256, 256))
    first = {}
    for d in (1, 3, 2):
        for col, axis in ((0, "x"), (1, "z")):
            other = (me.at(axis) + d) % 4
            first[col, d] = wire.put(
                node.at[:, :, halves[col]], gathered[3 * col + d - 1], me.peer(axis, other)
            )
    asks = []
    for e in range(1, 8):
        for col in range(2):
            asks.append(
                wire.put(
                    wanted_row,
                    requests.at[8 * col + (me.zk if col == 0 else me.xk)],
                    devices[7 * col + e - 1],
                )
            )
    requests[me.zk] = wanted_row[...]
    requests[8 + me.xk] = wanted_row[...]
    for copy in asks:
        copy.wait_recv()
    local = pltpu.make_async_copy(requests, request_s, local_sem)
    local.start()
    local.wait()
    moved = []
    for d in (0, 1, 3, 2):
        for col, axis in ((0, "x"), (1, "z")):
            if d:
                first[col, d].wait_recv()
            origin = (me.at(axis) + 4 - d) % 4
            own_slot = me.zk if col == 0 else me.xk
            owner = origin * 8 + me.zk if col == 0 else me.x * 8 + origin * 2 + me.k
            for e in range(8):
                slot = (own_slot + e) % 8
                index = request_s[8 * col + slot, 0, owner]
                if d:
                    tile = gathered[3 * col + d - 1][index]
                else:
                    tile = node[index, :, 256 * col : 256 * col + 256]
                if e == 0:
                    mirrors[col, own_slot, origin] = tile
                else:
                    staged[col, e - 1, d] = tile
                    moved.append(
                        wire.put(
                            staged.at[col, e - 1, d],
                            mirrors.at[col, own_slot, origin],
                            devices[7 * col + e - 1],
                        )
                    )

    self_part[...] = dot(node[me.g], w_self[...])
    for copy in moved:
        copy.wait_recv()
    wire.drain()


def fetch(node_tiles, wanted, w_self):
    depth = node_tiles.shape[2]
    copies = 6 + 14 + 56
    return pl.pallas_call(
        fetch_kernel,
        name="fetch",
        out_shape=(
            jax.ShapeDtypeStruct((2, 8, 4, 128, 256), BF),
            jax.ShapeDtypeStruct((16, 1, 128), jnp.int32),
            jax.ShapeDtypeStruct((128, depth), F32),
        ),
        in_specs=[VMEM_SPEC] * 3,
        out_specs=(VMEM_SPEC,) * 3,
        scratch_shapes=[
            pltpu.VMEM((1, 128), jnp.int32),
            pltpu.SMEM((16, 1, 128), jnp.int32),
            pltpu.VMEM((2, 7, 4, 128, 256), BF),
            pltpu.SemaphoreType.DMA((copies,)),
            pltpu.SemaphoreType.DMA((copies,)),
            pltpu.SemaphoreType.DMA,
            *[pltpu.VMEM((4, 128, 256), BF)] * 6,
        ],
        compiler_params=pltpu.CompilerParams(
            collective_id=0, has_side_effects=True, vmem_limit_bytes=LIMIT
        ),
    )(node_tiles, wanted, w_self)


GROUP = 8


def slots_of(source):
    x, zk = source // 8, source % 8
    z, k = zk // 2, zk % 2
    return zk * 4 + x, (x * 2 + k) * 4 + z


def forward_kernel(
    source, target, relation, live, values, mirrors, rel_emb, query_rel, rel_score,
    out, out_low, query_part,
):
    step = pl.program_id(0)
    first = (lax.axis_index("grp") * 2 + lax.axis_index("cand") % 2) * 128

    @pl.when(step < 16)
    def _():
        for j in range(8):
            row = step * 8 + j
            query_part[pl.ds(row, 1), :] = rel_score[pl.ds(query_rel[first + row], 1), :]

    @pl.when(step == 0)
    def _():
        out[...] = jnp.zeros_like(out)

    count = live[0, 0]

    @pl.when(step * GROUP < count)
    def _():
        for j in range(GROUP):
            b = step * GROUP + j
            slots = slots_of(source[0, 0, b])
            t = target[0, 0, b]
            block = values[0, 0, j]
            block = jnp.where(b < count, block, jnp.zeros_like(block))
            row = rel_emb[pl.ds(relation[0, 0, b], 1), :]
            for col in range(2):
                part = slice(256 * col, 256 * col + 256)
                composed = (mirrors[col, slots[col]].astype(F32) - row[:, part]).astype(BF)
                out[t, :, part] += dot(block, composed)

    @pl.when(step == pl.num_programs(0) - 1)
    def _():
        for t in range(4):
            out_low[t] = out[t].astype(BF)


def adjacency_specs(blocks):
    return [SMEM_SPEC] * 4 + [
        pl.BlockSpec((1, 1, GROUP, 128, 128), lambda i: (0, 0, i, 0, 0)),
    ]


def forward(
    adj_source, adj_target, adj_relation, live_blocks, adj_values, mirrors, rel_emb, query_rel, rel_score
):
    blocks = adj_values.shape[2]
    depth = rel_score.shape[1]
    return pl.pallas_call(
        forward_kernel,
        name="forward_blocks",
        grid=(blocks // GROUP,),
        out_shape=(
            jax.ShapeDtypeStruct((4, 128, depth), F32),
            jax.ShapeDtypeStruct((4, 128, depth), BF),
            jax.ShapeDtypeStruct((128, depth), F32),
        ),
        in_specs=adjacency_specs(blocks) + [VMEM_SPEC] * 2 + [SMEM_SPEC, VMEM_SPEC],
        out_specs=(VMEM_SPEC,) * 3,
        compiler_params=pltpu.CompilerParams(vmem_limit_bytes=LIMIT),
    )(
        adj_source, adj_target, adj_relation, live_blocks, adj_values,
        mirrors.reshape(2, 32, 128, 256), rel_emb, query_rel, rel_score,
    )


def backward_kernel(source, target, relation, live, values, agg, tiles_out, rel_out, tiles):
    step = pl.program_id(0)

    @pl.when(step == 0)
    def _():
        def clear(i, carry):
            for col in range(2):
                tiles[col, i] = jnp.zeros((128, 256), F32)
            return carry

        lax.fori_loop(0, 32, clear, 0)
        rel_out[...] = jnp.zeros_like(rel_out)

    count = live[0, 0]

    @pl.when(step * GROUP < count)
    def _():
        for j in range(GROUP):
            b = step * GROUP + j
            slots = slots_of(source[0, 0, b])
            r = pl.ds(relation[0, 0, b], 1)
            block = values[0, 0, j]
            block = jnp.where(b < count, block, jnp.zeros_like(block))
            grad = dot(block, agg[target[0, 0, b]], TN)
            rel_out[r, :] -= jnp.sum(grad, axis=0, keepdims=True)
            for col in range(2):
                tiles[col, slots[col]] += grad[:, 256 * col : 256 * col + 256]

    @pl.when(step == pl.num_programs(0) - 1)
    def _():
        def store(i, carry):
            for col in range(2):
                tiles_out[col, i] = tiles[col, i].astype(BF)
            return carry

        lax.fori_loop(0, 32, store, 0)


def backward(adj_source, adj_target, adj_relation, live_blocks, adj_values, agg_tiles):
    blocks = adj_values.shape[2]
    return pl.pallas_call(
        backward_kernel,
        name="backward_blocks",
        grid=(blocks // GROUP,),
        out_shape=(
            jax.ShapeDtypeStruct((2, 32, 128, 256), BF),
            jax.ShapeDtypeStruct((256, 512), F32),
        ),
        in_specs=adjacency_specs(blocks) + [VMEM_SPEC],
        out_specs=(VMEM_SPEC, VMEM_SPEC),
        scratch_shapes=[pltpu.VMEM((2, 32, 128, 256), F32)],
        compiler_params=pltpu.CompilerParams(vmem_limit_bytes=LIMIT),
    )(adj_source, adj_target, adj_relation, live_blocks, adj_values, agg_tiles)


def exchange_sum(me, wire, send, recv, out, during=None):
    for level in range(2):
        copies = []
        for d in (1, 3, 2):
            for col in range(2):
                axis = STAGES_CAND[col][level]
                other = (me.at(axis) + d) % 4
                copies.append(
                    wire.put(
                        send.at[level, col], recv.at[level, col, d - 1], me.peer(axis, other)
                    )
                )
        if level == 0 and during is not None:
            during()
        for copy in copies:
            copy.wait_recv()
        for col in range(2):
            total = send[level, col].astype(F32)
            for d in range(3):
                total = total + recv[level, col, d].astype(F32)
            if level == 0:
                send[1, col] = total.astype(BF)
            else:
                out[:, 256 * col : 256 * col + 256] = total


def middle_kernel(
    partial_low, partial, self_part, w_in, query_part, query_head, true_tail, allowed,
    h_out, loss, agg_all, pre_all, agg_tiles,
    share_recv, act, column, head_send, head_recv, queries, q_hi, q_lo, scores, stats,
    grad_send, grad_recv, summed, g_hi, g_lo, rows, core_send, core_recv, y_send, y_recv,
    send_sem, recv_sem,
):
    me = Place()
    enter(ring_devices(me))
    wire = Wire(send_sem, recv_sem)
    count = true_tail.shape[1]
    scale = 512 ** (-0.5)
    group = me.g * 2 + me.k
    lanes = pl.ds(pl.multiple_of(group * 128, 128), 128)
    first_chip = me.x * 8 + me.z * 2
    base = first_chip * 512

    def to_y(ref, at, order=(1, 3, 2)):
        copies = {}
        for d in order:
            copies[d] = wire.put(ref.at[at], ref.at[at], me.peer("y", (me.g + d) % 4))
        return copies

    copies = []
    for d in (1, 3, 2):
        other = (me.g + d) % 4
        copies.append(wire.put(partial_low.at[other], share_recv.at[d - 1], me.peer("y", other)))
    for copy in copies:
        copy.wait_recv()
    total = partial[me.g]
    for d in range(3):
        total = total + share_recv[d].astype(F32)
    agg = total.astype(BF)
    activated = jnp.tanh(dot(agg, w_in[...]) + self_part[...])
    h = activated.astype(BF)
    own_chunk = me.k * 4 + me.g
    column[own_chunk] = h
    from_y = to_y(column, own_chunk)
    from_sibling = [wire.put(column.at[own_chunk], column.at[own_chunk], me.sibling())]
    h_out[0] = h
    act[...] = activated
    agg_all[me.g] = agg
    agg_copies = to_y(agg_all, me.g)
    for d in (1, 3, 2):
        from_y[d].wait_recv()
        chunk = me.k * 4 + (me.g + 4 - d) % 4
        from_sibling.append(wire.put(column.at[chunk], column.at[chunk], me.sibling()))

    head_row = jnp.broadcast_to(query_head[:, lanes] - base, (128, 128))
    head_col = head_row.astype(F32).T
    lane_ids = lax.broadcasted_iota(jnp.int32, (128, 128), 1).astype(F32)
    row_ids = lax.broadcasted_iota(jnp.int32, (128, 128), 0)
    for copy in from_sibling:
        copy.wait_recv()
    part = jnp.zeros((128, 512), F32)
    for j in range(8):
        pick = jnp.where(head_col == lane_ids + 128.0 * j, 1.0, 0.0).astype(BF)
        part = part + dot(pick, column[j])
    for col in range(2):
        head_send[0, col] = part[:, 256 * col : 256 * col + 256].astype(BF)
    exchange_sum(me, wire, head_send, head_recv, summed)

    q = summed[...] + query_part[...]
    queries[...] = q
    high = q.astype(BF)
    q_hi[...] = high
    q_lo[...] = (q - high.astype(F32)).astype(BF)
    square = jnp.zeros((128, 128), F32)
    for j in range(4):
        piece = q[:, 128 * j : 128 * j + 128]
        square = square + piece * piece
    q_sq = jnp.sum(square.T, axis=0, keepdims=True)
    tail_row = jnp.broadcast_to(true_tail[:, lanes] - base, (128, 128))
    kinds = allowed[:, lanes]

    def allowed_row(j):
        hit = jnp.where(kinds == first_chip * 4 + j, 1.0, 0.0)
        return jnp.max(hit, axis=0, keepdims=True)

    masks = [jnp.broadcast_to(allowed_row(j), (128, 128)) > 0.5 for j in range(8)]
    tops, truths = [], []
    for j in range(8):
        h32 = column[j].astype(F32)
        h_sq = jnp.sum(h32 * h32, axis=1, keepdims=True)
        cross = dot(column[j], q_hi[...], NT) + dot(column[j], q_lo[...], NT)
        score = -scale * (q_sq + h_sq - 2.0 * cross)
        scores[j] = score
        tops.append(jnp.max(jnp.where(masks[j], score, NEG_FILL), axis=0, keepdims=True))
        truths.append(
            jnp.sum(
                jnp.where(row_ids + 128 * j == tail_row, score, 0.0), axis=0, keepdims=True
            )
        )
    top = functools.reduce(jnp.maximum, tops)
    weight = jnp.zeros((1, 128), F32)
    for j in range(8):
        weight = weight + jnp.sum(
            jnp.exp(jnp.where(masks[j], scores[j] - top, NEG_FILL)), axis=0, keepdims=True
        )
    stats[0, 0, 0:1, :] = top
    stats[0, 0, 1:2, :] = weight
    stats[0, 0, 2:3, :] = functools.reduce(lambda a, b: a + b, truths)

    for level, axis in enumerate(("z", "x")):
        copies = []
        for d in (1, 3, 2):
            other = (me.at(axis) + d) % 4
            copies.append(wire.put(stats.at[level, 0], stats.at[level, d], me.peer(axis, other)))
        for copy in copies:
            copy.wait_recv()
        members = [stats[level, m] for m in range(4)]
        tops = [m[0:1, :] for m in members]
        top = functools.reduce(jnp.maximum, tops)
        weight = members[0][1:2, :] * jnp.exp(tops[0] - top)
        truth = members[0][2:3, :]
        for m in range(1, 4):
            weight = weight + members[m][1:2, :] * jnp.exp(tops[m] - top)
            truth = truth + members[m][2:3, :]
        if level == 0:
            stats[1, 0, 0:1, :] = top
            stats[1, 0, 1:2, :] = weight
            stats[1, 0, 2:3, :] = truth
    log_norm = top + jnp.log(weight)
    loss[group] = log_norm - truth
    loss_copies = to_y(loss, group)
    rest_sum = (weight * jnp.exp(top - log_norm) - 1.0) / count
    rest_col = jnp.broadcast_to(rest_sum, (128, 128)).T

    part = jnp.zeros((128, 512), F32)
    for j in range(8):
        prob = jnp.exp(jnp.where(masks[j], scores[j] - log_norm, NEG_FILL))
        tail = jnp.where(row_ids + 128 * j == tail_row, 1.0, 0.0)
        grad = (prob - tail) / count
        scores[j] = grad
        high = grad.astype(BF)
        g_hi[j] = high
        g_lo[j] = (grad - high.astype(F32)).astype(BF)
        flipped = grad.T
        high = flipped.astype(BF)
        low = (flipped - high.astype(F32)).astype(BF)
        part = part + (dot(high, column[j]) + dot(low, column[j]))
    for col in range(2):
        grad_send[0, col] = part[:, 256 * col : 256 * col + 256].astype(BF)

    def candidates():
        for j in range(8):
            sums = jnp.sum(scores[j], axis=1, keepdims=True)
            rows[j] = (
                dot(g_hi[j], q_hi[...]) + dot(g_hi[j], q_lo[...]) + dot(g_lo[j], q_hi[...])
            ) - column[j].astype(F32) * sums

    exchange_sum(me, wire, grad_send, grad_recv, summed, candidates)

    query_grad = jnp.concatenate(
        [
            summed[:, 128 * j : 128 * j + 128] - queries[:, 128 * j : 128 * j + 128] * rest_col
            for j in range(4)
        ],
        axis=1,
    ).astype(BF)

    def row_part(chunk):
        pick = jnp.where(row_ids + 128 * chunk == head_row, 1.0, 0.0).astype(BF)
        return rows[chunk] + dot(pick, query_grad)

    order = (1, 3, 2, 0)
    core_copies = {}
    for at, d in enumerate(order):
        chunk = (1 - me.k) * 4 + (me.g + d) % 4
        core_send[d] = row_part(chunk).astype(BF)
        core_copies[d] = wire.put(core_send.at[d], core_recv.at[d], me.sibling())
    y_copies = []
    for d in order:
        own = row_part(me.k * 4 + (me.g + d) % 4)
        core_copies[d].wait_recv()
        total = own + core_recv[d].astype(F32)
        if d:
            y_send[d - 1] = total.astype(BF)
            y_copies.append(
                wire.put(y_send.at[d - 1], y_recv.at[d - 1], me.peer("y", (me.g + d) % 4))
            )
    for d in (1, 3, 2):
        loss_copies[d].wait_recv()
    loss_rows = []
    for d in range(4):
        row = ((me.g + d) % 4) * 2 + me.k
        loss_rows.append(wire.put(loss.at[row], loss.at[row], me.sibling()))
    for copy in y_copies:
        copy.wait_recv()
    for d in range(3):
        total = total + y_recv[d].astype(F32)
    activated = act[...]
    pre_grad = (((2.0 * scale) * total) * (1.0 - activated * activated)).astype(BF)
    pre_all[me.g] = pre_grad
    pre_copies = to_y(pre_all, me.g)
    agg_tiles[me.g] = dot(pre_grad, w_in[...], NT).astype(BF)
    for d in (1, 3, 2):
        pre_copies[d].wait_recv()
        other = (me.g + 4 - d) % 4
        agg_tiles[other] = dot(pre_all[other], w_in[...], NT).astype(BF)
    for d in (1, 3, 2):
        agg_copies[d].wait_recv()
    for copy in loss_rows:
        copy.wait_recv()
    wire.drain()


def middle(partial_low, partial, self_part, w_in, query_part, query_head, true_tail, allowed):
    depth = w_in.shape[0]
    copies = 64
    tile_bf = jax.ShapeDtypeStruct((4, 128, depth), BF)
    return pl.pallas_call(
        middle_kernel,
        name="middle",
        out_shape=(
            jax.ShapeDtypeStruct((1, 128, depth), BF),
            jax.ShapeDtypeStruct((8, 1, 128), F32),
            tile_bf,
            tile_bf,
            tile_bf,
        ),
        in_specs=[VMEM_SPEC] * 8,
        out_specs=(VMEM_SPEC,) * 5,
        scratch_shapes=[
            pltpu.VMEM((3, 128, depth), BF),
            pltpu.VMEM((128, depth), F32),
            pltpu.VMEM((8, 128, depth), BF),
            pltpu.VMEM((2, 2, 128, 256), BF),
            pltpu.VMEM((2, 2, 3, 128, 256), BF),
            pltpu.VMEM((128, depth), F32),
            pltpu.VMEM((128, depth), BF),
            pltpu.VMEM((128, depth), BF),
            pltpu.VMEM((8, 128, 128), F32),
            pltpu.VMEM((2, 4, 8, 128), F32),
            pltpu.VMEM((2, 2, 128, 256), BF),
            pltpu.VMEM((2, 2, 3, 128, 256), BF),
            pltpu.VMEM((128, depth), F32),
            pltpu.VMEM((8, 128, 128), BF),
            pltpu.VMEM((8, 128, 128), BF),
            pltpu.VMEM((8, 128, depth), F32),
            pltpu.VMEM((4, 128, depth), BF),
            pltpu.VMEM((4, 128, depth), BF),
            pltpu.VMEM((3, 128, depth), BF),
            pltpu.VMEM((3, 128, depth), BF),
            pltpu.SemaphoreType.DMA((copies,)),
            pltpu.SemaphoreType.DMA((copies,)),
        ],
        compiler_params=pltpu.CompilerParams(
            collective_id=1, has_side_effects=True, vmem_limit_bytes=LIMIT
        ),
    )(partial_low, partial, self_part, w_in, query_part, query_head, true_tail, allowed)


def return_kernel(
    n_ar,
    tiles, rel_part, agg_all, pre_all, node, w_self, requests,
    node_grad, rel_grad, w_in_grad, w_self_grad,
    arrived, shipped, joined, own_sum, y_send, y_recv, self_grad, w_all, *rest,
):
    ar_refs = rest[:n_ar]
    send_sem, recv_sem, local_sem = rest[n_ar:]
    me = Place()
    devices = []
    for e in range(1, 8):
        devices.append(me.dev(me.g, me.x * 8 + (me.zk + e) % 8))
    for e in range(1, 8):
        other = (me.xk + e) % 8
        devices.append(me.dev(me.g, (other // 2) * 8 + me.z * 2 + other % 2))
    for d in (1, 2, 3):
        devices.append(me.peer("y", (me.g + d) % 4))
    enter(devices)
    wire = Wire(send_sem, recv_sem)
    reduce = AllReduce(me, wire, 16, STAGES_CAND, ar_refs)
    steps = reduce.steps()

    def advance():
        next(steps, None)

    axes = ((0, "x"), (1, "z"))
    order = (1, 3, 2, 0)
    own_slots = (me.zk, me.xk)
    moved = {}

    def send_round(d):
        for col, axis in axes:
            place = (me.at(axis) + d) % 4
            for e in range(1, 8):
                slot = (own_slots[col] + e) % 8
                moved[d, col, e] = wire.put(
                    tiles.at[col, slot, place],
                    arrived.at[col, own_slots[col], place],
                    devices[7 * col + e - 1],
                )

    send_round(order[0])
    send_round(order[1])
    local = []
    for col in range(2):
        copy = pltpu.make_async_copy(
            tiles.at[col, own_slots[col]], arrived.at[col, own_slots[col]], local_sem.at[col]
        )
        copy.start()
        local.append(copy)
    cols = pl.ds(pl.multiple_of(me.g * 128, 128), 128)
    right = pre_all[:, :, cols].reshape(512, 128)
    for which, left in ((0, agg_all), (1, node)):
        for q in range(4):
            turned = left[:, :, 128 * q : 128 * q + 128].astype(F32).reshape(512, 128).T.astype(BF)
            reduce.part[2 * which + q // 2, 8 * (q % 2) : 8 * (q % 2) + 8, 0:16] = (
                dot(turned, right).reshape(8, 16, 128).astype(BF)
            )
    for q in range(2):
        for j in range(4):
            reduce.part[j, 8 * q : 8 * q + 8, 16:32] = (
                rel_part[128 * q : 128 * q + 128, 128 * j : 128 * j + 128]
                .reshape(8, 16, 128)
                .astype(BF)
            )
    advance()
    self_grad[...] = dot(pre_all[me.g], w_self[...], NT)
    advance()
    for copy in local:
        copy.wait()
    second = []
    for at, d in enumerate(order):
        if at + 2 < 4:
            send_round(order[at + 2])
        for col, axis in axes:
            place = (me.at(axis) + d) % 4
            owner = place * 8 + me.zk if col == 0 else me.x * 8 + place * 2 + me.k
            for e in range(1, 8):
                moved[d, col, e].wait_recv()
            index = [requests[8 * col + m, 0, owner] for m in range(8)]
            for part in range(4):
                rows = pl.ds(part * 32, 32)
                values = [arrived[col, m, place, rows, :].astype(F32) for m in range(8)]
                for s in range(4):
                    total = jnp.zeros((32, 256), F32)
                    for m in range(8):
                        total = total + jnp.where(index[m] == s, values[m], 0.0)
                    if d == 0:
                        own_sum[col, s, rows, :] = total
                    else:
                        shipped[col, d - 1, s, rows, :] = total.astype(BF)
            if d:
                second.append(
                    wire.put(
                        shipped.at[col, d - 1], joined.at[col, d - 1], me.peer(axis, place)
                    )
                )
        advance()
    for copy in second:
        copy.wait_recv()
    third = []
    for d in (1, 3, 2, 0):
        s = (me.g + d) % 4
        for col in range(2):
            total = own_sum[col, s]
            for m in range(3):
                total = total + joined[col, m, s].astype(F32)
            if d == 0:
                own_sum[col, s] = total
            else:
                y_send[col, d - 1] = total.astype(BF)
                third.append(
                    wire.put(y_send.at[col, d - 1], y_recv.at[col, d - 1], me.peer("y", s))
                )
    advance()
    advance()
    mine = 2 * me.k
    pair = pl.ds(mine, 2)
    both = wire.put(reduce.out.at[pair], reduce.out.at[pair], me.sibling())
    for col in range(2):
        w_all[me.g, mine + col] = reduce.out[mine + col, :, 0:16]
    w_copies = {}
    for d in (1, 3, 2):
        w_copies[d] = wire.put(
            w_all.at[me.g, pair], w_all.at[me.g, pair], me.peer("y", (me.g + d) % 4)
        )
    w_rows = [wire.put(w_all.at[me.g, pair], w_all.at[me.g, pair], me.sibling())]
    for copy in third:
        copy.wait_recv()
    for col in range(2):
        total = own_sum[col, me.g]
        for m in range(3):
            total = total + y_recv[col, m].astype(F32)
        node_grad[0, :, 256 * col : 256 * col + 256] = (
            total + self_grad[:, 256 * col : 256 * col + 256]
        )
    for d in (1, 3, 2):
        w_copies[d].wait_recv()
        other = (me.g + 4 - d) % 4
        w_rows.append(wire.put(w_all.at[other, pair], w_all.at[other, pair], me.sibling()))
    both.wait_recv()
    for j in range(4):
        whole = reduce.out[j, :, 16:32].astype(F32).reshape(256, 128)
        rel_grad[:, 128 * j : 128 * j + 128] = whole[: rel_grad.shape[0]]
    for copy in w_rows:
        copy.wait_recv()
    for j in range(4):
        for q in range(2):
            rows = slice(256 * q, 256 * q + 256)
            for at, target in ((q, w_in_grad), (2 + q, w_self_grad)):
                target[rows, 128 * j : 128 * j + 128] = (
                    w_all[j, at].astype(F32).reshape(256, 128)
                )
    wire.drain()


def give_back(tiles, rel_part, agg_all, pre_all, node_tiles, w_self, requests, relations):
    depth = w_self.shape[0]
    ar = AllReduce.scratch(16, STAGES_CAND, 32)
    copies = 56 + 6 + 6 + (1 + 12 + 12) + 1 + 3 + 4
    return pl.pallas_call(
        functools.partial(return_kernel, len(ar)),
        name="give_back",
        out_shape=(
            jax.ShapeDtypeStruct((1, 128, depth), F32),
            jax.ShapeDtypeStruct((relations, depth), F32),
            jax.ShapeDtypeStruct((depth, depth), F32),
            jax.ShapeDtypeStruct((depth, depth), F32),
        ),
        in_specs=[ANY_SPEC] + [VMEM_SPEC] * 5 + [SMEM_SPEC],
        out_specs=(VMEM_SPEC,) * 4,
        scratch_shapes=[
            pltpu.VMEM((2, 8, 4, 128, 256), BF),
            pltpu.VMEM((2, 3, 4, 128, 256), BF),
            pltpu.VMEM((2, 3, 4, 128, 256), BF),
            pltpu.VMEM((2, 4, 128, 256), F32),
            pltpu.VMEM((2, 3, 128, 256), BF),
            pltpu.VMEM((2, 3, 128, 256), BF),
            pltpu.VMEM((128, depth), F32),
            pltpu.VMEM((4, 4, 16, 16, 128), BF),
            *ar,
            pltpu.SemaphoreType.DMA((copies,)),
            pltpu.SemaphoreType.DMA((copies,)),
            pltpu.SemaphoreType.DMA((2,)),
        ],
        compiler_params=pltpu.CompilerParams(
            collective_id=2, has_side_effects=True, vmem_limit_bytes=LIMIT
        ),
    )(tiles, rel_part, agg_all, pre_all, node_tiles, w_self, requests)


def body(
    node_emb,
    rel_emb,
    w_in,
    w_self,
    rel_score,
    mirror_blocks,
    adj_values,
    adj_source,
    adj_target,
    adj_relation,
    live_blocks,
    query_head,
    query_rel,
    allowed,
    true_tail,
):
    wanted = mirror_blocks.reshape(1, 32)
    node_tiles = node_emb.reshape(4, 128, -1)
    mirrors, requests, self_part = fetch(node_tiles, wanted, w_self)
    partial, partial_low, query_part = forward(
        adj_source, adj_target, adj_relation, live_blocks, adj_values, mirrors, rel_emb,
        query_rel, rel_score,
    )
    h_out, loss, agg_all, pre_all, agg_tiles = middle(
        partial_low,
        partial,
        self_part,
        w_in,
        query_part,
        query_head.reshape(1, -1),
        true_tail.reshape(1, -1),
        allowed.T,
    )
    tiles, rel_part = backward(
        adj_source, adj_target, adj_relation, live_blocks, adj_values, agg_tiles
    )
    node_grad, rel_grad, w_in_grad, w_self_grad = give_back(
        tiles.reshape(2, 8, 4, 128, 256),
        rel_part,
        agg_all,
        pre_all,
        node_tiles,
        w_self,
        requests,
        rel_emb.shape[0],
    )
    return (h_out, loss.reshape(-1), node_grad, rel_grad, w_in_grad, w_self_grad)


def solution(mesh):
    return jax.shard_map(
        body,
        mesh=mesh,
        in_specs=(
            P("cand", None, None),
            P("grp", None),
            P(),
            P(),
            P(),
            P("grp", "cand", None, None),
            P("grp", "cand", None, None, None),
            P("grp", "cand", None),
            P("grp", "cand", None),
            P("grp", "cand", None),
            P("grp", "cand"),
            P(),
            P(),
            P(),
            P(),
        ),
        out_specs=(P("cand", "grp", None), P(), P("cand", "grp", None), P("grp", None), P(), P()),
        check_vma=False,
    )
```

```python
import functools

import jax
import jax.numpy as jnp
from jax import lax
from jax.experimental import pallas as pl
from jax.experimental.pallas import tpu as pltpu
from jax.sharding import PartitionSpec as P

NEG_FILL = -1e30
MESH = pl.DeviceIdType.MESH
BF = jnp.bfloat16
F32 = jnp.float32
NN = (((1,), (0,)), ((), ()))
NT = (((1,), (1,)), ((), ()))
TN = (((0,), (0,)), ((), ()))
VMEM_SPEC = pl.BlockSpec(memory_space=pltpu.VMEM)
SMEM_SPEC = pl.BlockSpec(memory_space=pltpu.SMEM)
ANY_SPEC = pl.BlockSpec(memory_space=pl.ANY)
LIMIT = 60 * 1024 * 1024
STAGES_CAND = (("z", "x"), ("x", "z"))


def dot(a, b, dims=NN):
    return lax.dot_general(a, b, dims, preferred_element_type=F32)


class Place:
    def __init__(self):
        self.g = lax.axis_index("grp")
        self.c = lax.axis_index("cand")
        self.x = self.c // 8
        self.zk = self.c % 8
        self.z = self.zk // 2
        self.k = self.c % 2
        self.xk = self.x * 2 + self.k

    def dev(self, g, c):
        return {"grp": g, "cand": c}

    def at(self, axis):
        return {"x": self.x, "z": self.z, "y": self.g}[axis]

    def peer(self, axis, other):
        if axis == "y":
            return self.dev(other, self.c)
        if axis == "x":
            return self.dev(self.g, other * 8 + self.zk)
        return self.dev(self.g, self.x * 8 + other * 2 + self.k)

    def sibling(self):
        return self.dev(self.g, self.c + 1 - 2 * self.k)


def enter(devices):
    barrier = pltpu.get_barrier_semaphore()
    for device in devices:
        pl.semaphore_signal(barrier, inc=1, device_id=device, device_id_type=MESH)
    pl.semaphore_wait(barrier, len(devices))


def ring_devices(me):
    found = [me.sibling()]
    for axis in ("y", "x", "z"):
        for d in (1, 2, 3):
            found.append(me.peer(axis, (me.at(axis) + d) % 4))
    return found


class Wire:
    def __init__(self, send_sem, recv_sem):
        self.send_sem, self.recv_sem, self.count, self.sent = send_sem, recv_sem, 0, []

    def put(self, src, dst, device):
        at = self.count
        self.count += 1
        copy = pltpu.make_async_remote_copy(
            src_ref=src,
            dst_ref=dst,
            send_sem=self.send_sem.at[at],
            recv_sem=self.recv_sem.at[at],
            device_id=device,
            device_id_type=MESH,
        )
        copy.start()
        self.sent.append(copy)
        return copy

    def drain(self):
        for copy in self.sent:
            copy.wait_send()


def add_up(read_terms, write, count):
    chunk = min(count, 8)

    def one(i, carry):
        at = pl.ds(i * chunk, chunk)
        terms = read_terms(at)
        total = terms[0].astype(F32)
        for term in terms[1:]:
            total = total + term.astype(F32)
        write(at, total)
        return carry

    if count == chunk:
        one(0, 0)
    else:
        lax.fori_loop(0, count // chunk, one, 0)


class AllReduce:
    @staticmethod
    def scratch(shards, stages, height):
        depth = len(stages[0])
        shapes = [
            pltpu.VMEM((4, shards, height, 128), BF),
            pltpu.VMEM((2, shards, height, 128), BF),
        ]
        for level in range(depth):
            shapes.append(pltpu.VMEM((2, shards // 4**level, height, 128), BF))
            shapes.append(pltpu.VMEM((2, 3, shards // 4 ** (level + 1), height, 128), BF))
        return shapes

    def __init__(self, me, wire, shards, stages, refs):
        self.me, self.wire, self.shards, self.stages = me, wire, shards, stages
        self.part, self.rcore, self.out = refs[:3]
        depth = len(stages[0])
        self.acc = refs[3 : 3 + 2 * depth : 2]
        self.recv = refs[4 : 4 + 2 * depth : 2]
        self.sizes = [shards // 4 ** (i + 1) for i in range(depth)]

    def steps(self):
        me, wire = self.me, self.wire
        mine = 2 * me.k
        copy = wire.put(self.part.at[pl.ds(2 - mine, 2)], self.rcore, me.sibling())
        yield
        copy.wait_recv()
        for col in range(2):

            def write(at, value, col=col):
                self.acc[0][col, at] = value.astype(BF)

            add_up(
                lambda at, col=col: (self.part[mine + col, at], self.rcore[col, at]),
                write,
                self.shards,
            )
        offsets = [0, 0]
        history = []
        depth = len(self.sizes)
        for level in range(depth):
            size = self.sizes[level]
            copies = []
            for d in (1, 3, 2):
                for col in range(2):
                    axis = self.stages[col][level]
                    other = (me.at(axis) + d) % 4
                    copies.append(
                        wire.put(
                            self.acc[level].at[col, pl.ds(other * size, size)],
                            self.recv[level].at[col, d - 1],
                            me.peer(axis, other),
                        )
                    )
            yield
            for copy in copies:
                copy.wait_recv()
            for col in range(2):
                own = me.at(self.stages[col][level]) * size
                offsets[col] = offsets[col] + own

                def terms(at, col=col, own=own, level=level):
                    base = pl.ds(own + at.start, at.size)
                    return [self.acc[level][col, base]] + [
                        self.recv[level][col, d, at] for d in range(3)
                    ]

                def write(at, value, col=col, level=level):
                    if level + 1 < depth:
                        self.acc[level + 1][col, at] = value.astype(BF)
                    else:
                        self.out[mine + col, pl.ds(offsets[col] + at.start, at.size)] = (
                            value.astype(BF)
                        )

                add_up(terms, write, size)
            history.append(tuple(offsets))
        for level in reversed(range(depth)):
            size = self.sizes[level]
            copies = []
            for d in (1, 3, 2):
                for col in range(2):
                    axis = self.stages[col][level]
                    other = (me.at(axis) + d) % 4
                    place = self.out.at[mine + col, pl.ds(history[level][col], size)]
                    copies.append(wire.put(place, place, me.peer(axis, other)))
            yield
            for copy in copies:
                copy.wait_recv()


def fetch_kernel(
    node, wanted_v, w_self,
    mirrors, requests, self_part,
    wanted_row, request_s, staged, send_sem, recv_sem, local_sem, *gathered,
):
    me = Place()
    devices = []
    for e in range(1, 8):
        devices.append(me.dev(me.g, me.x * 8 + (me.zk + e) % 8))
    for e in range(1, 8):
        other = (me.xk + e) % 8
        if e == 7:
            pass
        devices.append(me.dev(me.g, (other // 2) * 8 + me.z * 2 + other % 2))
    enter(devices)
    wire = Wire(send_sem, recv_sem)
    wanted_row[...] = jnp.zeros_like(wanted_row)
    wanted_row[:, 0:32] = wanted_v[...]
    halves = (pl.ds(0, 256), pl.ds(256, 256))
    first = {}
    for d in (1, 3, 2):
        for col, axis in ((0, "x"), (1, "z")):
            other = (me.at(axis) + d) % 4
            first[col, d] = wire.put(
                node.at[:, :, halves[col]], gathered[3 * col + d - 1], me.peer(axis, other)
            )
    asks = []
    for e in range(1, 8):
        for col in range(2):
            asks.append(
                wire.put(
                    wanted_row,
                    requests.at[8 * col + (me.zk if col == 0 else me.xk)],
                    devices[7 * col + e - 1],
                )
            )
    requests[me.zk] = wanted_row[...]
    requests[8 + me.xk] = wanted_row[...]
    for copy in asks:
        copy.wait_recv()
    local = pltpu.make_async_copy(requests, request_s, local_sem)
    local.start()
    local.wait()
    moved = []
    for d in (0, 1, 3, 2):
        for col, axis in ((0, "x"), (1, "z")):
            if d:
                first[col, d].wait_recv()
            origin = (me.at(axis) + 4 - d) % 4
            own_slot = me.zk if col == 0 else me.xk
            owner = origin * 8 + me.zk if col == 0 else me.x * 8 + origin * 2 + me.k
            for e in range(8):
                slot = (own_slot + e) % 8
                index = request_s[8 * col + slot, 0, owner]
                if d:
                    tile = gathered[3 * col + d - 1][index]
                else:
                    tile = node[index, :, 256 * col : 256 * col + 256]
                if e == 0:
                    mirrors[col, own_slot, origin] = tile
                else:
                    staged[col, e - 1, d] = tile
                    moved.append(
                        wire.put(
                            staged.at[col, e - 1, d],
                            mirrors.at[col, own_slot, origin],
                            devices[7 * col + e - 1],
                        )
                    )

    self_part[...] = dot(node[me.g], w_self[...])
    for copy in moved:
        copy.wait_recv()
    wire.drain()


def fetch(node_tiles, wanted, w_self):
    depth = node_tiles.shape[2]
    copies = 6 + 14 + 56
    return pl.pallas_call(
        fetch_kernel,
        name="fetch",
        out_shape=(
            jax.ShapeDtypeStruct((2, 8, 4, 128, 256), BF),
            jax.ShapeDtypeStruct((16, 1, 128), jnp.int32),
            jax.ShapeDtypeStruct((128, depth), F32),
        ),
        in_specs=[VMEM_SPEC] * 3,
        out_specs=(VMEM_SPEC,) * 3,
        scratch_shapes=[
            pltpu.VMEM((1, 128), jnp.int32),
            pltpu.SMEM((16, 1, 128), jnp.int32),
            pltpu.VMEM((2, 7, 4, 128, 256), BF),
            pltpu.SemaphoreType.DMA((copies,)),
            pltpu.SemaphoreType.DMA((copies,)),
            pltpu.SemaphoreType.DMA,
            *[pltpu.VMEM((4, 128, 256), BF)] * 6,
        ],
        compiler_params=pltpu.CompilerParams(
            collective_id=0, has_side_effects=True, vmem_limit_bytes=LIMIT
        ),
    )(node_tiles, wanted, w_self)


GROUP = 24


def slots_of(source):
    x, zk = source // 8, source % 8
    z, k = zk // 2, zk % 2
    return zk * 4 + x, (x * 2 + k) * 4 + z


def forward_kernel(
    source, target, relation, live, values, mirrors, rel_emb, query_rel, rel_score,
    out, out_low, query_part,
):
    step = pl.program_id(0)
    first = (lax.axis_index("grp") * 2 + lax.axis_index("cand") % 2) * 128

    for j in range(16):
        row = step * 16 + j
        query_part[pl.ds(row, 1), :] = rel_score[pl.ds(query_rel[first + row], 1), :]

    @pl.when(step == 0)
    def _():
        out[...] = jnp.zeros_like(out)

    count = live[0, 0]

    @pl.when(step * GROUP < count)
    def _():
        for j in range(GROUP):
            b = step * GROUP + j
            slots = slots_of(source[0, 0, b])
            t = target[0, 0, b]
            block = values[0, 0, j]
            block = jnp.where(b < count, block, jnp.zeros_like(block))
            row = rel_emb[pl.ds(relation[0, 0, b], 1), :]
            for col in range(2):
                part = slice(256 * col, 256 * col + 256)
                composed = (mirrors[col, slots[col]].astype(F32) - row[:, part]).astype(BF)
                out[t, :, part] += dot(block, composed)

    @pl.when(step == pl.num_programs(0) - 1)
    def _():
        for t in range(4):
            out_low[t] = out[t].astype(BF)


def adjacency_specs(blocks):
    return [SMEM_SPEC] * 4 + [
        pl.BlockSpec((1, 1, GROUP, 128, 128), lambda i: (0, 0, i, 0, 0)),
    ]


def forward(
    adj_source, adj_target, adj_relation, live_blocks, adj_values, mirrors, rel_emb, query_rel, rel_score
):
    blocks = adj_values.shape[2]
    depth = rel_score.shape[1]
    return pl.pallas_call(
        forward_kernel,
        name="forward_blocks",
        grid=(blocks // GROUP,),
        out_shape=(
            jax.ShapeDtypeStruct((4, 128, depth), F32),
            jax.ShapeDtypeStruct((4, 128, depth), BF),
            jax.ShapeDtypeStruct((128, depth), F32),
        ),
        in_specs=adjacency_specs(blocks) + [VMEM_SPEC] * 2 + [SMEM_SPEC, VMEM_SPEC],
        out_specs=(VMEM_SPEC,) * 3,
        compiler_params=pltpu.CompilerParams(vmem_limit_bytes=LIMIT),
    )(
        adj_source, adj_target, adj_relation, live_blocks, adj_values,
        mirrors.reshape(2, 32, 128, 256), rel_emb, query_rel, rel_score,
    )


def backward_kernel(
    source, target, relation, live, values, agg, h_in, loss_in,
    tiles_out, rel_out, h_out, loss_out, tiles,
):
    step = pl.program_id(0)

    @pl.when(step == 0)
    def _():
        def clear(i, carry):
            for col in range(2):
                tiles[col, i] = jnp.zeros((128, 256), F32)
            return carry

        lax.fori_loop(0, 32, clear, 0)
        rel_out[...] = jnp.zeros_like(rel_out)
        h_out[...] = h_in[...]
        for j in range(8):
            loss_out[j : j + 1, :] = loss_in[j]

    count = live[0, 0]

    @pl.when(step * GROUP < count)
    def _():
        for j in range(GROUP):
            b = step * GROUP + j
            slots = slots_of(source[0, 0, b])
            r = pl.ds(relation[0, 0, b], 1)
            block = values[0, 0, j]
            block = jnp.where(b < count, block, jnp.zeros_like(block))
            grad = dot(block, agg[target[0, 0, b]], TN)
            rel_out[r, :] -= jnp.sum(grad, axis=0, keepdims=True)
            for col in range(2):
                tiles[col, slots[col]] += grad[:, 256 * col : 256 * col + 256]

    @pl.when(step == pl.num_programs(0) - 1)
    def _():
        def store(i, carry):
            for col in range(2):
                tiles_out[col, i] = tiles[col, i].astype(BF)
            return carry

        lax.fori_loop(0, 32, store, 0)


def backward(adj_source, adj_target, adj_relation, live_blocks, adj_values, agg_tiles, h, loss):
    blocks = adj_values.shape[2]
    return pl.pallas_call(
        backward_kernel,
        name="backward_blocks",
        grid=(blocks // GROUP,),
        out_shape=(
            jax.ShapeDtypeStruct((2, 32, 128, 256), BF),
            jax.ShapeDtypeStruct((256, 512), F32),
            jax.ShapeDtypeStruct(h.shape, h.dtype),
            jax.ShapeDtypeStruct((8, 128), F32),
        ),
        in_specs=adjacency_specs(blocks) + [VMEM_SPEC] * 3,
        out_specs=(VMEM_SPEC,) * 4,
        scratch_shapes=[pltpu.VMEM((2, 32, 128, 256), F32)],
        compiler_params=pltpu.CompilerParams(vmem_limit_bytes=LIMIT),
    )(adj_source, adj_target, adj_relation, live_blocks, adj_values, agg_tiles, h, loss)


def exchange_sum(me, wire, send, recv, out, during=None):
    for level in range(2):
        copies = []
        for d in (1, 3, 2):
            for col in range(2):
                axis = STAGES_CAND[col][level]
                other = (me.at(axis) + d) % 4
                copies.append(
                    wire.put(
                        send.at[level, col], recv.at[level, col, d - 1], me.peer(axis, other)
                    )
                )
        if level == 0 and during is not None:
            during()
        for copy in copies:
            copy.wait_recv()
        for col in range(2):
            total = send[level, col].astype(F32)
            for d in range(3):
                total = total + recv[level, col, d].astype(F32)
            if level == 0:
                send[1, col] = total.astype(BF)
            else:
                out[:, 256 * col : 256 * col + 256] = total


def middle_kernel(
    partial_low, partial, self_part, w_in, query_part, query_head, true_tail, allowed,
    h_out, loss, agg_all, pre_all, agg_tiles,
    share_recv, act, column, head_send, head_recv, queries, q_hi, q_lo, scores, stats,
    grad_send, grad_recv, summed, g_hi, g_lo, rows, core_send, core_recv, y_send, y_recv,
    send_sem, recv_sem,
):
    me = Place()
    enter(ring_devices(me))
    wire = Wire(send_sem, recv_sem)
    count = true_tail.shape[1]
    scale = 512 ** (-0.5)
    group = me.g * 2 + me.k
    lanes = pl.ds(pl.multiple_of(group * 128, 128), 128)
    first_chip = me.x * 8 + me.z * 2
    base = first_chip * 512

    def to_y(ref, at, order=(1, 3, 2)):
        copies = {}
        for d in order:
            copies[d] = wire.put(ref.at[at], ref.at[at], me.peer("y", (me.g + d) % 4))
        return copies

    copies = []
    for d in (1, 3, 2):
        other = (me.g + d) % 4
        copies.append(wire.put(partial_low.at[other], share_recv.at[d - 1], me.peer("y", other)))
    for copy in copies:
        copy.wait_recv()
    total = partial[me.g]
    for d in range(3):
        total = total + share_recv[d].astype(F32)
    agg = total.astype(BF)
    activated = jnp.tanh(dot(agg, w_in[...]) + self_part[...])
    h = activated.astype(BF)
    own_chunk = me.k * 4 + me.g
    column[own_chunk] = h
    from_y = to_y(column, own_chunk)
    from_sibling = [wire.put(column.at[own_chunk], column.at[own_chunk], me.sibling())]
    h_out[0] = h
    act[...] = activated
    agg_all[me.g] = agg
    agg_copies = to_y(agg_all, me.g)
    for d in (1, 3, 2):
        from_y[d].wait_recv()
        chunk = me.k * 4 + (me.g + 4 - d) % 4
        from_sibling.append(wire.put(column.at[chunk], column.at[chunk], me.sibling()))

    head_row = jnp.broadcast_to(query_head[:, lanes] - base, (128, 128))
    head_col = head_row.astype(F32).T
    lane_ids = lax.broadcasted_iota(jnp.int32, (128, 128), 1).astype(F32)
    row_ids = lax.broadcasted_iota(jnp.int32, (128, 128), 0)
    for copy in from_sibling:
        copy.wait_recv()
    part = jnp.zeros((128, 512), F32)
    for j in range(8):
        pick = jnp.where(head_col == lane_ids + 128.0 * j, 1.0, 0.0).astype(BF)
        part = part + dot(pick, column[j])
    for col in range(2):
        head_send[0, col] = part[:, 256 * col : 256 * col + 256].astype(BF)
    exchange_sum(me, wire, head_send, head_recv, summed)

    q = summed[...] + query_part[...]
    queries[...] = q
    high = q.astype(BF)
    q_hi[...] = high
    q_lo[...] = (q - high.astype(F32)).astype(BF)
    square = jnp.zeros((128, 128), F32)
    for j in range(4):
        piece = q[:, 128 * j : 128 * j + 128]
        square = square + piece * piece
    q_sq = jnp.sum(square.T, axis=0, keepdims=True)
    tail_row = jnp.broadcast_to(true_tail[:, lanes] - base, (128, 128))
    kinds = allowed[:, lanes]

    def allowed_row(j):
        hit = jnp.where(kinds == first_chip * 4 + j, 1.0, 0.0)
        return jnp.max(hit, axis=0, keepdims=True)

    masks = [jnp.broadcast_to(allowed_row(j), (128, 128)) > 0.5 for j in range(8)]
    tops, truths = [], []
    for j in range(8):
        h32 = column[j].astype(F32)
        h_sq = jnp.sum(h32 * h32, axis=1, keepdims=True)
        cross = dot(column[j], q_hi[...], NT) + dot(column[j], q_lo[...], NT)
        score = -scale * (q_sq + h_sq - 2.0 * cross)
        scores[j] = score
        tops.append(jnp.max(jnp.where(masks[j], score, NEG_FILL), axis=0, keepdims=True))
        truths.append(
            jnp.sum(
                jnp.where(row_ids + 128 * j == tail_row, score, 0.0), axis=0, keepdims=True
            )
        )
    top = functools.reduce(jnp.maximum, tops)
    weight = jnp.zeros((1, 128), F32)
    for j in range(8):
        weight = weight + jnp.sum(
            jnp.exp(jnp.where(masks[j], scores[j] - top, NEG_FILL)), axis=0, keepdims=True
        )
    stats[0, 0, 0:1, :] = top
    stats[0, 0, 1:2, :] = weight
    stats[0, 0, 2:3, :] = functools.reduce(lambda a, b: a + b, truths)

    for level, axis in enumerate(("z", "x")):
        copies = []
        for d in (1, 3, 2):
            other = (me.at(axis) + d) % 4
            copies.append(wire.put(stats.at[level, 0], stats.at[level, d], me.peer(axis, other)))
        for copy in copies:
            copy.wait_recv()
        members = [stats[level, m] for m in range(4)]
        tops = [m[0:1, :] for m in members]
        top = functools.reduce(jnp.maximum, tops)
        weight = members[0][1:2, :] * jnp.exp(tops[0] - top)
        truth = members[0][2:3, :]
        for m in range(1, 4):
            weight = weight + members[m][1:2, :] * jnp.exp(tops[m] - top)
            truth = truth + members[m][2:3, :]
        if level == 0:
            stats[1, 0, 0:1, :] = top
            stats[1, 0, 1:2, :] = weight
            stats[1, 0, 2:3, :] = truth
    log_norm = top + jnp.log(weight)
    loss[group] = log_norm - truth
    loss_copies = to_y(loss, group)
    rest_sum = (weight * jnp.exp(top - log_norm) - 1.0) / count
    rest_col = jnp.broadcast_to(rest_sum, (128, 128)).T

    part = jnp.zeros((128, 512), F32)
    for j in range(8):
        prob = jnp.exp(jnp.where(masks[j], scores[j] - log_norm, NEG_FILL))
        tail = jnp.where(row_ids + 128 * j == tail_row, 1.0, 0.0)
        grad = (prob - tail) / count
        scores[j] = grad
        high = grad.astype(BF)
        g_hi[j] = high
        g_lo[j] = (grad - high.astype(F32)).astype(BF)
        flipped = grad.T
        high = flipped.astype(BF)
        low = (flipped - high.astype(F32)).astype(BF)
        part = part + (dot(high, column[j]) + dot(low, column[j]))
    for col in range(2):
        grad_send[0, col] = part[:, 256 * col : 256 * col + 256].astype(BF)

    def candidates():
        for j in range(8):
            sums = jnp.sum(scores[j], axis=1, keepdims=True)
            rows[j] = (
                dot(g_hi[j], q_hi[...]) + dot(g_hi[j], q_lo[...]) + dot(g_lo[j], q_hi[...])
            ) - column[j].astype(F32) * sums

    exchange_sum(me, wire, grad_send, grad_recv, summed, candidates)

    query_grad = jnp.concatenate(
        [
            summed[:, 128 * j : 128 * j + 128] - queries[:, 128 * j : 128 * j + 128] * rest_col
            for j in range(4)
        ],
        axis=1,
    ).astype(BF)

    def row_part(chunk):
        pick = jnp.where(row_ids + 128 * chunk == head_row, 1.0, 0.0).astype(BF)
        return rows[chunk] + dot(pick, query_grad)

    order = (1, 3, 2, 0)
    core_copies = {}
    for at, d in enumerate(order):
        chunk = (1 - me.k) * 4 + (me.g + d) % 4
        core_send[d] = row_part(chunk).astype(BF)
        core_copies[d] = wire.put(core_send.at[d], core_recv.at[d], me.sibling())
    y_copies = []
    for d in order:
        own = row_part(me.k * 4 + (me.g + d) % 4)
        core_copies[d].wait_recv()
        total = own + core_recv[d].astype(F32)
        if d:
            y_send[d - 1] = total.astype(BF)
            y_copies.append(
                wire.put(y_send.at[d - 1], y_recv.at[d - 1], me.peer("y", (me.g + d) % 4))
            )
    for d in (1, 3, 2):
        loss_copies[d].wait_recv()
    loss_rows = []
    for d in range(4):
        row = ((me.g + d) % 4) * 2 + me.k
        loss_rows.append(wire.put(loss.at[row], loss.at[row], me.sibling()))
    for copy in y_copies:
        copy.wait_recv()
    for d in range(3):
        total = total + y_recv[d].astype(F32)
    activated = act[...]
    pre_grad = (((2.0 * scale) * total) * (1.0 - activated * activated)).astype(BF)
    pre_all[me.g] = pre_grad
    pre_copies = to_y(pre_all, me.g)
    agg_tiles[me.g] = dot(pre_grad, w_in[...], NT).astype(BF)
    for d in (1, 3, 2):
        pre_copies[d].wait_recv()
        other = (me.g + 4 - d) % 4
        agg_tiles[other] = dot(pre_all[other], w_in[...], NT).astype(BF)
    for d in (1, 3, 2):
        agg_copies[d].wait_recv()
    for copy in loss_rows:
        copy.wait_recv()
    wire.drain()


def middle(partial_low, partial, self_part, w_in, query_part, query_head, true_tail, allowed):
    depth = w_in.shape[0]
    copies = 64
    tile_bf = jax.ShapeDtypeStruct((4, 128, depth), BF)
    return pl.pallas_call(
        middle_kernel,
        name="middle",
        out_shape=(
            jax.ShapeDtypeStruct((1, 128, depth), BF),
            jax.ShapeDtypeStruct((8, 1, 128), F32),
            tile_bf,
            tile_bf,
            tile_bf,
        ),
        in_specs=[VMEM_SPEC] * 8,
        out_specs=(VMEM_SPEC,) * 5,
        scratch_shapes=[
            pltpu.VMEM((3, 128, depth), BF),
            pltpu.VMEM((128, depth), F32),
            pltpu.VMEM((8, 128, depth), BF),
            pltpu.VMEM((2, 2, 128, 256), BF),
            pltpu.VMEM((2, 2, 3, 128, 256), BF),
            pltpu.VMEM((128, depth), F32),
            pltpu.VMEM((128, depth), BF),
            pltpu.VMEM((128, depth), BF),
            pltpu.VMEM((8, 128, 128), F32),
            pltpu.VMEM((2, 4, 8, 128), F32),
            pltpu.VMEM((2, 2, 128, 256), BF),
            pltpu.VMEM((2, 2, 3, 128, 256), BF),
            pltpu.VMEM((128, depth), F32),
            pltpu.VMEM((8, 128, 128), BF),
            pltpu.VMEM((8, 128, 128), BF),
            pltpu.VMEM((8, 128, depth), F32),
            pltpu.VMEM((4, 128, depth), BF),
            pltpu.VMEM((4, 128, depth), BF),
            pltpu.VMEM((3, 128, depth), BF),
            pltpu.VMEM((3, 128, depth), BF),
            pltpu.SemaphoreType.DMA((copies,)),
            pltpu.SemaphoreType.DMA((copies,)),
        ],
        compiler_params=pltpu.CompilerParams(
            collective_id=1, has_side_effects=True, vmem_limit_bytes=LIMIT
        ),
    )(partial_low, partial, self_part, w_in, query_part, query_head, true_tail, allowed)


def return_kernel(
    n_ar,
    tiles, rel_part, agg_all, pre_all, node, w_self, requests,
    node_grad, summed, w_all,
    arrived, shipped, joined, own_sum, y_send, y_recv, self_grad, *rest,
):
    ar_refs = list(rest[:n_ar])
    ar_refs.insert(2, summed)
    send_sem, recv_sem, local_sem = rest[n_ar:]
    me = Place()
    devices = []
    for e in range(1, 8):
        devices.append(me.dev(me.g, me.x * 8 + (me.zk + e) % 8))
    for e in range(1, 8):
        other = (me.xk + e) % 8
        devices.append(me.dev(me.g, (other // 2) * 8 + me.z * 2 + other % 2))
    for d in (1, 2, 3):
        devices.append(me.peer("y", (me.g + d) % 4))
    enter(devices)
    wire = Wire(send_sem, recv_sem)
    reduce = AllReduce(me, wire, 16, STAGES_CAND, ar_refs)
    steps = reduce.steps()

    def advance():
        next(steps, None)

    axes = ((0, "x"), (1, "z"))
    order = (1, 3, 2, 0)
    own_slots = (me.zk, me.xk)
    moved = {}

    def send_round(d):
        for col, axis in axes:
            place = (me.at(axis) + d) % 4
            for e in range(1, 8):
                slot = (own_slots[col] + e) % 8
                moved[d, col, e] = wire.put(
                    tiles.at[col, slot, place],
                    arrived.at[col, own_slots[col], place],
                    devices[7 * col + e - 1],
                )

    send_round(order[0])
    send_round(order[1])
    local = []
    for col in range(2):
        copy = pltpu.make_async_copy(
            tiles.at[col, own_slots[col]], arrived.at[col, own_slots[col]], local_sem.at[col]
        )
        copy.start()
        local.append(copy)
    cols = pl.ds(pl.multiple_of(me.g * 128, 128), 128)
    right = pre_all[:, :, cols].reshape(512, 128)
    for which, left in ((0, agg_all), (1, node)):
        for q in range(4):
            turned = left[:, :, 128 * q : 128 * q + 128].astype(F32).reshape(512, 128).T.astype(BF)
            reduce.part[2 * which + q // 2, 8 * (q % 2) : 8 * (q % 2) + 8, 0:16] = (
                dot(turned, right).reshape(8, 16, 128).astype(BF)
            )
    for q in range(2):
        for j in range(4):
            reduce.part[j, 8 * q : 8 * q + 8, 16:32] = (
                rel_part[128 * q : 128 * q + 128, 128 * j : 128 * j + 128]
                .reshape(8, 16, 128)
                .astype(BF)
            )
    advance()
    self_grad[...] = dot(pre_all[me.g], w_self[...], NT)
    advance()
    for copy in local:
        copy.wait()
    second = []
    for at, d in enumerate(order):
        if at + 2 < 4:
            send_round(order[at + 2])
        for col, axis in axes:
            place = (me.at(axis) + d) % 4
            owner = place * 8 + me.zk if col == 0 else me.x * 8 + place * 2 + me.k
            for e in range(1, 8):
                moved[d, col, e].wait_recv()
            index = [requests[8 * col + m, 0, owner] for m in range(8)]
            for part in range(4):
                rows = pl.ds(part * 32, 32)
                values = [arrived[col, m, place, rows, :].astype(F32) for m in range(8)]
                for s in range(4):
                    total = jnp.zeros((32, 256), F32)
                    for m in range(8):
                        total = total + jnp.where(index[m] == s, values[m], 0.0)
                    if d == 0:
                        own_sum[col, s, rows, :] = total
                    else:
                        shipped[col, d - 1, s, rows, :] = total.astype(BF)
            if d:
                second.append(
                    wire.put(
                        shipped.at[col, d - 1], joined.at[col, d - 1], me.peer(axis, place)
                    )
                )
        advance()
    for copy in second:
        copy.wait_recv()
    third = []
    for d in (1, 3, 2, 0):
        s = (me.g + d) % 4
        for col in range(2):
            total = own_sum[col, s]
            for m in range(3):
                total = total + joined[col, m, s].astype(F32)
            if d == 0:
                own_sum[col, s] = total
            else:
                y_send[col, d - 1] = total.astype(BF)
                third.append(
                    wire.put(y_send.at[col, d - 1], y_recv.at[col, d - 1], me.peer("y", s))
                )
    advance()
    advance()
    mine = 2 * me.k
    pair = pl.ds(mine, 2)
    both = wire.put(reduce.out.at[pair], reduce.out.at[pair], me.sibling())
    for col in range(2):
        w_all[me.g, mine + col] = reduce.out[mine + col, :, 0:16]
    w_copies = {}
    for d in (1, 3, 2):
        w_copies[d] = wire.put(
            w_all.at[me.g, pair], w_all.at[me.g, pair], me.peer("y", (me.g + d) % 4)
        )
    w_rows = [wire.put(w_all.at[me.g, pair], w_all.at[me.g, pair], me.sibling())]
    for copy in third:
        copy.wait_recv()
    for col in range(2):
        total = own_sum[col, me.g]
        for m in range(3):
            total = total + y_recv[col, m].astype(F32)
        node_grad[0, :, 256 * col : 256 * col + 256] = (
            total + self_grad[:, 256 * col : 256 * col + 256]
        )
    for d in (1, 3, 2):
        w_copies[d].wait_recv()
        other = (me.g + 4 - d) % 4
        w_rows.append(wire.put(w_all.at[other, pair], w_all.at[other, pair], me.sibling()))
    both.wait_recv()
    for copy in w_rows:
        copy.wait_recv()
    wire.drain()


def give_back(tiles, rel_part, agg_all, pre_all, node_tiles, w_self, requests):
    depth = w_self.shape[0]
    ar = AllReduce.scratch(16, STAGES_CAND, 32)
    copies = 56 + 6 + 6 + (1 + 12 + 12) + 1 + 3 + 4
    return pl.pallas_call(
        functools.partial(return_kernel, len(ar)),
        name="give_back",
        out_shape=(
            jax.ShapeDtypeStruct((1, 128, depth), F32),
            jax.ShapeDtypeStruct((4, 16, 32, 128), BF),
            jax.ShapeDtypeStruct((4, 4, 16, 16, 128), BF),
        ),
        in_specs=[ANY_SPEC] + [VMEM_SPEC] * 5 + [SMEM_SPEC],
        out_specs=(VMEM_SPEC,) * 3,
        scratch_shapes=[
            pltpu.VMEM((2, 8, 4, 128, 256), BF),
            pltpu.VMEM((2, 3, 4, 128, 256), BF),
            pltpu.VMEM((2, 3, 4, 128, 256), BF),
            pltpu.VMEM((2, 4, 128, 256), F32),
            pltpu.VMEM((2, 3, 128, 256), BF),
            pltpu.VMEM((2, 3, 128, 256), BF),
            pltpu.VMEM((128, depth), F32),
            *ar,
            pltpu.SemaphoreType.DMA((copies,)),
            pltpu.SemaphoreType.DMA((copies,)),
            pltpu.SemaphoreType.DMA((2,)),
        ],
        compiler_params=pltpu.CompilerParams(
            collective_id=2, has_side_effects=True, vmem_limit_bytes=LIMIT
        ),
    )(tiles, rel_part, agg_all, pre_all, node_tiles, w_self, requests)


def finish_kernel(node_in, summed, w_all, node_grad, rel_grad, w_in_grad, w_self_grad):
    node_grad[...] = node_in[...]
    for j in range(4):
        cols = slice(128 * j, 128 * j + 128)
        whole = summed[j, :, 16:32].astype(F32).reshape(256, 128)
        rel_grad[:, cols] = whole[: rel_grad.shape[0]]
        for q in range(2):
            rows = slice(256 * q, 256 * q + 256)
            for at, target in ((q, w_in_grad), (2 + q, w_self_grad)):
                target[rows, cols] = w_all[j, at].astype(F32).reshape(256, 128)


def finish(node_grad, summed, w_all, relations):
    depth = node_grad.shape[2]
    return pl.pallas_call(
        finish_kernel,
        name="finish",
        out_shape=(
            jax.ShapeDtypeStruct(node_grad.shape, F32),
            jax.ShapeDtypeStruct((relations, depth), F32),
            jax.ShapeDtypeStruct((depth, depth), F32),
            jax.ShapeDtypeStruct((depth, depth), F32),
        ),
        in_specs=[VMEM_SPEC] * 3,
        out_specs=(VMEM_SPEC,) * 4,
    )(node_grad, summed, w_all)


def body(
    node_emb,
    rel_emb,
    w_in,
    w_self,
    rel_score,
    mirror_blocks,
    adj_values,
    adj_source,
    adj_target,
    adj_relation,
    live_blocks,
    query_head,
    query_rel,
    allowed,
    true_tail,
):
    wanted = mirror_blocks.reshape(1, 32)
    node_tiles = node_emb.reshape(4, 128, -1)
    mirrors, requests, self_part = fetch(node_tiles, wanted, w_self)
    partial, partial_low, query_part = forward(
        adj_source, adj_target, adj_relation, live_blocks, adj_values, mirrors, rel_emb,
        query_rel, rel_score,
    )
    h, loss, agg_all, pre_all, agg_tiles = middle(
        partial_low,
        partial,
        self_part,
        w_in,
        query_part,
        query_head.reshape(1, -1),
        true_tail.reshape(1, -1),
        allowed.T,
    )
    tiles, rel_part, h_out, loss = backward(
        adj_source, adj_target, adj_relation, live_blocks, adj_values, agg_tiles, h, loss
    )
    node_grad, summed, w_all = give_back(
        tiles.reshape(2, 8, 4, 128, 256),
        rel_part,
        agg_all,
        pre_all,
        node_tiles,
        w_self,
        requests,
    )
    node_grad, rel_grad, w_in_grad, w_self_grad = finish(
        node_grad, summed, w_all, rel_emb.shape[0]
    )
    return (h_out, loss.reshape(-1), node_grad, rel_grad, w_in_grad, w_self_grad)


def solution(mesh):
    return jax.shard_map(
        body,
        mesh=mesh,
        in_specs=(
            P("cand", None, None),
            P("grp", None),
            P(),
            P(),
            P(),
            P("grp", "cand", None, None),
            P("grp", "cand", None, None, None),
            P("grp", "cand", None),
            P("grp", "cand", None),
            P("grp", "cand", None),
            P("grp", "cand"),
            P(),
            P(),
            P(),
            P(),
        ),
        out_specs=(P("cand", "grp", None), P(), P("cand", "grp", None), P("grp", None), P(), P()),
        check_vma=False,
    )
```

```python
import functools

import jax
import jax.numpy as jnp
from jax import lax
from jax.experimental import pallas as pl
from jax.experimental.pallas import tpu as pltpu
from jax.sharding import PartitionSpec as P

NEG_FILL = -1e30
MESH = pl.DeviceIdType.MESH
BF = jnp.bfloat16
F32 = jnp.float32
NN = (((1,), (0,)), ((), ()))
NT = (((1,), (1,)), ((), ()))
TN = (((0,), (0,)), ((), ()))
VMEM_SPEC = pl.BlockSpec(memory_space=pltpu.VMEM)
SMEM_SPEC = pl.BlockSpec(memory_space=pltpu.SMEM)
ANY_SPEC = pl.BlockSpec(memory_space=pl.ANY)
LIMIT = 60 * 1024 * 1024
STAGES_CAND = (("z", "x"), ("x", "z"))


def dot(a, b, dims=NN):
    return lax.dot_general(a, b, dims, preferred_element_type=F32)


class Place:
    def __init__(self):
        self.g = lax.axis_index("grp")
        self.c = lax.axis_index("cand")
        self.x = self.c // 8
        self.zk = self.c % 8
        self.z = self.zk // 2
        self.k = self.c % 2
        self.xk = self.x * 2 + self.k

    def dev(self, g, c):
        return {"grp": g, "cand": c}

    def at(self, axis):
        return {"x": self.x, "z": self.z, "y": self.g}[axis]

    def peer(self, axis, other):
        if axis == "y":
            return self.dev(other, self.c)
        if axis == "x":
            return self.dev(self.g, other * 8 + self.zk)
        return self.dev(self.g, self.x * 8 + other * 2 + self.k)

    def sibling(self):
        return self.dev(self.g, self.c + 1 - 2 * self.k)


def enter(devices):
    barrier = pltpu.get_barrier_semaphore()
    for device in devices:
        pl.semaphore_signal(barrier, inc=1, device_id=device, device_id_type=MESH)
    pl.semaphore_wait(barrier, len(devices))


def ring_devices(me):
    found = [me.sibling()]
    for axis in ("y", "x", "z"):
        for d in (1, 2, 3):
            found.append(me.peer(axis, (me.at(axis) + d) % 4))
    return found


class Wire:
    def __init__(self, send_sem, recv_sem):
        self.send_sem, self.recv_sem, self.count, self.sent = send_sem, recv_sem, 0, []

    def put(self, src, dst, device):
        at = self.count
        self.count += 1
        copy = pltpu.make_async_remote_copy(
            src_ref=src,
            dst_ref=dst,
            send_sem=self.send_sem.at[at],
            recv_sem=self.recv_sem.at[at],
            device_id=device,
            device_id_type=MESH,
        )
        copy.start()
        self.sent.append(copy)
        return copy

    def drain(self):
        for copy in self.sent:
            copy.wait_send()


def add_up(read_terms, write, count):
    chunk = min(count, 8)

    def one(i, carry):
        at = pl.ds(i * chunk, chunk)
        terms = read_terms(at)
        total = terms[0].astype(F32)
        for term in terms[1:]:
            total = total + term.astype(F32)
        write(at, total)
        return carry

    if count == chunk:
        one(0, 0)
    else:
        lax.fori_loop(0, count // chunk, one, 0)


class AllReduce:
    @staticmethod
    def scratch(shards, stages, height):
        depth = len(stages[0])
        shapes = [
            pltpu.VMEM((4, shards, height, 128), BF),
            pltpu.VMEM((2, shards, height, 128), BF),
        ]
        for level in range(depth):
            shapes.append(pltpu.VMEM((2, shards // 4**level, height, 128), BF))
            shapes.append(pltpu.VMEM((2, 3, shards // 4 ** (level + 1), height, 128), BF))
        return shapes

    def __init__(self, me, wire, shards, stages, refs, summed, w_all):
        self.me, self.wire, self.shards, self.stages = me, wire, shards, stages
        self.part, self.rcore = refs[:2]
        self.summed, self.w_all = summed, w_all
        depth = len(stages[0])
        self.acc = refs[2 : 2 + 2 * depth : 2]
        self.recv = refs[3 : 3 + 2 * depth : 2]
        self.sizes = [shards // 4 ** (i + 1) for i in range(depth)]

    def steps(self):
        me, wire = self.me, self.wire
        mine = 2 * me.k
        copy = wire.put(self.part.at[pl.ds(2 - mine, 2)], self.rcore, me.sibling())
        yield
        copy.wait_recv()
        for col in range(2):

            def write(at, value, col=col):
                self.acc[0][col, at] = value.astype(BF)

            add_up(
                lambda at, col=col: (self.part[mine + col, at], self.rcore[col, at]),
                write,
                self.shards,
            )
        offsets = [0, 0]
        history = []
        depth = len(self.sizes)
        for level in range(depth):
            size = self.sizes[level]
            copies = []
            for d in (1, 3, 2):
                for col in range(2):
                    axis = self.stages[col][level]
                    other = (me.at(axis) + d) % 4
                    copies.append(
                        wire.put(
                            self.acc[level].at[col, pl.ds(other * size, size)],
                            self.recv[level].at[col, d - 1],
                            me.peer(axis, other),
                        )
                    )
            yield
            for copy in copies:
                copy.wait_recv()
            for col in range(2):
                own = me.at(self.stages[col][level]) * size
                offsets[col] = offsets[col] + own

                def terms(at, col=col, own=own, level=level):
                    base = pl.ds(own + at.start, at.size)
                    return [self.acc[level][col, base]] + [
                        self.recv[level][col, d, at] for d in range(3)
                    ]

                def write(at, value, col=col, level=level):
                    if level + 1 < depth:
                        self.acc[level + 1][col, at] = value.astype(BF)
                    else:
                        final = value.astype(BF)
                        place = pl.ds(offsets[col] + at.start, at.size)
                        self.w_all[me.g, mine + col, place] = final[:, 0:16]
                        self.summed[mine + col, place] = final[:, 16:32]

                add_up(terms, write, size)
            history.append(tuple(offsets))
        copies = []
        for d in (1, 3, 2):
            for col in range(2):
                place = self.w_all.at[me.g, mine + col, pl.ds(offsets[col], self.sizes[-1])]
                copies.append(wire.put(place, place, me.peer("y", (me.g + d) % 4)))
        yield
        for copy in copies:
            copy.wait_recv()
        for level in reversed(range(depth)):
            size = self.sizes[level]
            copies = []
            for d in (1, 3, 2):
                for col in range(2):
                    axis = self.stages[col][level]
                    other = (me.at(axis) + d) % 4
                    shards = pl.ds(history[level][col], size)
                    for place in (
                        self.summed.at[mine + col, shards],
                        self.w_all.at[:, mine + col, shards],
                    ):
                        copies.append(wire.put(place, place, me.peer(axis, other)))
            yield
            for copy in copies:
                copy.wait_recv()


def fetch_kernel(
    node, wanted_v, w_self,
    mirrors, requests, self_part,
    wanted_row, request_s, staged, send_sem, recv_sem, local_sem, *gathered,
):
    me = Place()
    devices = []
    for e in range(1, 8):
        devices.append(me.dev(me.g, me.x * 8 + (me.zk + e) % 8))
    for e in range(1, 8):
        other = (me.xk + e) % 8
        devices.append(me.dev(me.g, (other // 2) * 8 + me.z * 2 + other % 2))
    for d in (1, 2, 3):
        devices.append(me.peer("y", (me.g + d) % 4))
    enter(devices)
    wire = Wire(send_sem, recv_sem)
    wanted_row[...] = jnp.zeros_like(wanted_row)
    wanted_row[:, 0:32] = wanted_v[...]
    halves = (pl.ds(0, 256), pl.ds(256, 256))
    first = {}
    for d in (1, 3, 2):
        for col, axis in ((0, "x"), (1, "z")):
            other = (me.at(axis) + d) % 4
            first[col, d] = wire.put(
                node.at[me.g, :, halves[col]],
                gathered[3 * col + d - 1].at[me.g],
                me.peer(axis, other),
            )
    asks = []
    for e in range(1, 8):
        for col in range(2):
            asks.append(
                wire.put(
                    wanted_row,
                    requests.at[8 * col + (me.zk if col == 0 else me.xk)],
                    devices[7 * col + e - 1],
                )
            )
    requests[me.zk] = wanted_row[...]
    requests[8 + me.xk] = wanted_row[...]
    spread = {}

    def pass_on(d):
        for col in range(2):
            first[col, d].wait_recv()
            place = gathered[3 * col + d - 1].at[me.g]
            spread[col, d] = [
                wire.put(place, place, me.peer("y", (me.g + e) % 4)) for e in (1, 3, 2)
            ]

    pass_on(1)
    for copy in asks:
        copy.wait_recv()
    local = pltpu.make_async_copy(requests, request_s, local_sem)
    local.start()
    local.wait()
    moved = []
    for d in (0, 1, 3, 2):
        for col, axis in ((0, "x"), (1, "z")):
            if d:
                for copy in spread[col, d]:
                    copy.wait_recv()
            origin = (me.at(axis) + 4 - d) % 4
            own_slot = me.zk if col == 0 else me.xk
            owner = origin * 8 + me.zk if col == 0 else me.x * 8 + origin * 2 + me.k
            for e in range(8):
                slot = (own_slot + e) % 8
                index = request_s[8 * col + slot, 0, owner]
                if d:
                    tile = gathered[3 * col + d - 1][index]
                else:
                    tile = node[index, :, 256 * col : 256 * col + 256]
                if e == 0:
                    mirrors[col, own_slot, origin] = tile
                else:
                    staged[col, e - 1, d] = tile
                    moved.append(
                        wire.put(
                            staged.at[col, e - 1, d],
                            mirrors.at[col, own_slot, origin],
                            devices[7 * col + e - 1],
                        )
                    )
        if d == 0:
            pass_on(3)
            pass_on(2)
    self_part[...] = dot(node[me.g], w_self[...])
    for copy in moved:
        copy.wait_recv()
    wire.drain()


def fetch(node_tiles, wanted, w_self):
    depth = node_tiles.shape[2]
    copies = 6 + 14 + 56 + 18
    return pl.pallas_call(
        fetch_kernel,
        name="fetch",
        out_shape=(
            jax.ShapeDtypeStruct((2, 8, 4, 128, 256), BF),
            jax.ShapeDtypeStruct((16, 1, 128), jnp.int32),
            jax.ShapeDtypeStruct((128, depth), F32),
        ),
        in_specs=[VMEM_SPEC] * 3,
        out_specs=(VMEM_SPEC,) * 3,
        scratch_shapes=[
            pltpu.VMEM((1, 128), jnp.int32),
            pltpu.SMEM((16, 1, 128), jnp.int32),
            pltpu.VMEM((2, 7, 4, 128, 256), BF),
            pltpu.SemaphoreType.DMA((copies,)),
            pltpu.SemaphoreType.DMA((copies,)),
            pltpu.SemaphoreType.DMA,
            *[pltpu.VMEM((4, 128, 256), BF)] * 6,
        ],
        compiler_params=pltpu.CompilerParams(
            collective_id=0, has_side_effects=True, vmem_limit_bytes=LIMIT
        ),
    )(node_tiles, wanted, w_self)


GROUP = 24


def slots_of(source):
    x, zk = source // 8, source % 8
    z, k = zk // 2, zk % 2
    return zk * 4 + x, (x * 2 + k) * 4 + z


def forward_kernel(
    source, target, relation, live, values, mirrors, rel_emb, query_rel, rel_score,
    out, out_low, query_part,
):
    step = pl.program_id(0)
    first = (lax.axis_index("grp") * 2 + lax.axis_index("cand") % 2) * 128

    for j in range(16):
        row = step * 16 + j
        query_part[pl.ds(row, 1), :] = rel_score[pl.ds(query_rel[first + row], 1), :]

    @pl.when(step == 0)
    def _():
        out[...] = jnp.zeros_like(out)

    count = live[0, 0]

    @pl.when(step * GROUP < count)
    def _():
        for j in range(GROUP):
            b = step * GROUP + j
            slots = slots_of(source[0, 0, b])
            t = target[0, 0, b]
            block = values[0, 0, j]
            block = jnp.where(b < count, block, jnp.zeros_like(block))
            row = rel_emb[pl.ds(relation[0, 0, b], 1), :]
            for col in range(2):
                part = slice(256 * col, 256 * col + 256)
                composed = (mirrors[col, slots[col]].astype(F32) - row[:, part]).astype(BF)
                out[t, :, part] += dot(block, composed)

    @pl.when(step == pl.num_programs(0) - 1)
    def _():
        for t in range(4):
            out_low[t] = out[t].astype(BF)


def adjacency_specs(blocks):
    return [SMEM_SPEC] * 4 + [
        pl.BlockSpec((1, 1, GROUP, 128, 128), lambda i: (0, 0, i, 0, 0)),
    ]


def forward(
    adj_source, adj_target, adj_relation, live_blocks, adj_values, mirrors, rel_emb, query_rel, rel_score
):
    blocks = adj_values.shape[2]
    depth = rel_score.shape[1]
    return pl.pallas_call(
        forward_kernel,
        name="forward_blocks",
        grid=(blocks // GROUP,),
        out_shape=(
            jax.ShapeDtypeStruct((4, 128, depth), F32),
            jax.ShapeDtypeStruct((4, 128, depth), BF),
            jax.ShapeDtypeStruct((128, depth), F32),
        ),
        in_specs=adjacency_specs(blocks) + [VMEM_SPEC] * 2 + [SMEM_SPEC, VMEM_SPEC],
        out_specs=(VMEM_SPEC,) * 3,
        compiler_params=pltpu.CompilerParams(vmem_limit_bytes=LIMIT),
    )(
        adj_source, adj_target, adj_relation, live_blocks, adj_values,
        mirrors.reshape(2, 32, 128, 256), rel_emb, query_rel, rel_score,
    )


def backward_kernel(
    source, target, relation, live, values, agg, h_in, loss_in,
    tiles_out, rel_out, h_out, loss_out, tiles,
):
    step = pl.program_id(0)

    @pl.when(step == 0)
    def _():
        def clear(i, carry):
            for col in range(2):
                tiles[col, i] = jnp.zeros((128, 256), F32)
            return carry

        lax.fori_loop(0, 32, clear, 0)
        rel_out[...] = jnp.zeros_like(rel_out)
        h_out[...] = h_in[...]
        for j in range(8):
            loss_out[j : j + 1, :] = loss_in[j]

    count = live[0, 0]

    @pl.when(step * GROUP < count)
    def _():
        for j in range(GROUP):
            b = step * GROUP + j
            slots = slots_of(source[0, 0, b])
            r = pl.ds(relation[0, 0, b], 1)
            block = values[0, 0, j]
            block = jnp.where(b < count, block, jnp.zeros_like(block))
            grad = dot(block, agg[target[0, 0, b]], TN)
            rel_out[r, :] -= jnp.sum(grad, axis=0, keepdims=True)
            for col in range(2):
                tiles[col, slots[col]] += grad[:, 256 * col : 256 * col + 256]

    @pl.when(step == pl.num_programs(0) - 1)
    def _():
        def store(i, carry):
            for col in range(2):
                tiles_out[col, i] = tiles[col, i].astype(BF)
            return carry

        lax.fori_loop(0, 32, store, 0)


def backward(adj_source, adj_target, adj_relation, live_blocks, adj_values, agg_tiles, h, loss):
    blocks = adj_values.shape[2]
    return pl.pallas_call(
        backward_kernel,
        name="backward_blocks",
        grid=(blocks // GROUP,),
        out_shape=(
            jax.ShapeDtypeStruct((2, 32, 128, 256), BF),
            jax.ShapeDtypeStruct((256, 512), F32),
            jax.ShapeDtypeStruct(h.shape, h.dtype),
            jax.ShapeDtypeStruct((8, 128), F32),
        ),
        in_specs=adjacency_specs(blocks) + [VMEM_SPEC] * 3,
        out_specs=(VMEM_SPEC,) * 4,
        scratch_shapes=[pltpu.VMEM((2, 32, 128, 256), F32)],
        compiler_params=pltpu.CompilerParams(vmem_limit_bytes=LIMIT),
    )(adj_source, adj_target, adj_relation, live_blocks, adj_values, agg_tiles, h, loss)


def exchange_sum(me, wire, send, recv, out, during=None):
    for level in range(2):
        copies = []
        for d in (1, 3, 2):
            for col in range(2):
                axis = STAGES_CAND[col][level]
                other = (me.at(axis) + d) % 4
                copies.append(
                    wire.put(
                        send.at[level, col], recv.at[level, col, d - 1], me.peer(axis, other)
                    )
                )
        if level == 0 and during is not None:
            during()
        for copy in copies:
            copy.wait_recv()
        for col in range(2):
            total = send[level, col].astype(F32)
            for d in range(3):
                total = total + recv[level, col, d].astype(F32)
            if level == 0:
                send[1, col] = total.astype(BF)
            else:
                out[:, 256 * col : 256 * col + 256] = total


def middle_kernel(
    partial_low, partial, self_part, w_in, query_part, query_head, true_tail, allowed,
    h_out, loss, agg_all, pre_all, agg_tiles,
    share_recv, act, column, head_send, head_recv, queries, q_hi, q_lo, scores, stats,
    grad_send, grad_recv, summed, g_hi, g_lo, rows, core_send, core_recv, y_send, y_recv,
    send_sem, recv_sem,
):
    me = Place()
    enter(ring_devices(me))
    wire = Wire(send_sem, recv_sem)
    count = true_tail.shape[1]
    scale = 512 ** (-0.5)
    group = me.g * 2 + me.k
    lanes = pl.ds(pl.multiple_of(group * 128, 128), 128)
    first_chip = me.x * 8 + me.z * 2
    base = first_chip * 512

    def to_y(ref, at, order=(1, 3, 2)):
        copies = {}
        for d in order:
            copies[d] = wire.put(ref.at[at], ref.at[at], me.peer("y", (me.g + d) % 4))
        return copies

    copies = []
    for d in (1, 3, 2):
        other = (me.g + d) % 4
        copies.append(wire.put(partial_low.at[other], share_recv.at[d - 1], me.peer("y", other)))
    for copy in copies:
        copy.wait_recv()
    total = partial[me.g]
    for d in range(3):
        total = total + share_recv[d].astype(F32)
    agg = total.astype(BF)
    activated = jnp.tanh(dot(agg, w_in[...]) + self_part[...])
    h = activated.astype(BF)
    own_chunk = me.k * 4 + me.g
    column[own_chunk] = h
    from_y = to_y(column, own_chunk)
    from_sibling = [wire.put(column.at[own_chunk], column.at[own_chunk], me.sibling())]
    h_out[0] = h
    act[...] = activated
    agg_all[me.g] = agg
    agg_copies = to_y(agg_all, me.g)
    for d in (1, 3, 2):
        from_y[d].wait_recv()
        chunk = me.k * 4 + (me.g + 4 - d) % 4
        from_sibling.append(wire.put(column.at[chunk], column.at[chunk], me.sibling()))

    head_row = jnp.broadcast_to(query_head[:, lanes] - base, (128, 128))
    head_col = head_row.astype(F32).T
    lane_ids = lax.broadcasted_iota(jnp.int32, (128, 128), 1).astype(F32)
    row_ids = lax.broadcasted_iota(jnp.int32, (128, 128), 0)
    for copy in from_sibling:
        copy.wait_recv()
    part = jnp.zeros((128, 512), F32)
    for j in range(8):
        pick = jnp.where(head_col == lane_ids + 128.0 * j, 1.0, 0.0).astype(BF)
        part = part + dot(pick, column[j])
    for col in range(2):
        head_send[0, col] = part[:, 256 * col : 256 * col + 256].astype(BF)
    exchange_sum(me, wire, head_send, head_recv, summed)

    q = summed[...] + query_part[...]
    queries[...] = q
    high = q.astype(BF)
    q_hi[...] = high
    q_lo[...] = (q - high.astype(F32)).astype(BF)
    square = jnp.zeros((128, 128), F32)
    for j in range(4):
        piece = q[:, 128 * j : 128 * j + 128]
        square = square + piece * piece
    q_sq = jnp.sum(square.T, axis=0, keepdims=True)
    tail_row = jnp.broadcast_to(true_tail[:, lanes] - base, (128, 128))
    kinds = allowed[:, lanes]

    def allowed_row(j):
        hit = jnp.where(kinds == first_chip * 4 + j, 1.0, 0.0)
        return jnp.max(hit, axis=0, keepdims=True)

    masks = [jnp.broadcast_to(allowed_row(j), (128, 128)) > 0.5 for j in range(8)]
    tops, truths = [], []
    for j in range(8):
        h32 = column[j].astype(F32)
        h_sq = jnp.sum(h32 * h32, axis=1, keepdims=True)
        cross = dot(column[j], q_hi[...], NT) + dot(column[j], q_lo[...], NT)
        score = -scale * (q_sq + h_sq - 2.0 * cross)
        scores[j] = score
        tops.append(jnp.max(jnp.where(masks[j], score, NEG_FILL), axis=0, keepdims=True))
        truths.append(
            jnp.sum(
                jnp.where(row_ids + 128 * j == tail_row, score, 0.0), axis=0, keepdims=True
            )
        )
    top = functools.reduce(jnp.maximum, tops)
    weight = jnp.zeros((1, 128), F32)
    for j in range(8):
        weight = weight + jnp.sum(
            jnp.exp(jnp.where(masks[j], scores[j] - top, NEG_FILL)), axis=0, keepdims=True
        )
    stats[0, 0, 0:1, :] = top
    stats[0, 0, 1:2, :] = weight
    stats[0, 0, 2:3, :] = functools.reduce(lambda a, b: a + b, truths)

    for level, axis in enumerate(("z", "x")):
        copies = []
        for d in (1, 3, 2):
            other = (me.at(axis) + d) % 4
            copies.append(wire.put(stats.at[level, 0], stats.at[level, d], me.peer(axis, other)))
        for copy in copies:
            copy.wait_recv()
        members = [stats[level, m] for m in range(4)]
        tops = [m[0:1, :] for m in members]
        top = functools.reduce(jnp.maximum, tops)
        weight = members[0][1:2, :] * jnp.exp(tops[0] - top)
        truth = members[0][2:3, :]
        for m in range(1, 4):
            weight = weight + members[m][1:2, :] * jnp.exp(tops[m] - top)
            truth = truth + members[m][2:3, :]
        if level == 0:
            stats[1, 0, 0:1, :] = top
            stats[1, 0, 1:2, :] = weight
            stats[1, 0, 2:3, :] = truth
    log_norm = top + jnp.log(weight)
    loss[group] = log_norm - truth
    loss_copies = to_y(loss, group)
    rest_sum = (weight * jnp.exp(top - log_norm) - 1.0) / count
    rest_col = jnp.broadcast_to(rest_sum, (128, 128)).T

    part = jnp.zeros((128, 512), F32)
    for j in range(8):
        prob = jnp.exp(jnp.where(masks[j], scores[j] - log_norm, NEG_FILL))
        tail = jnp.where(row_ids + 128 * j == tail_row, 1.0, 0.0)
        grad = (prob - tail) / count
        scores[j] = grad
        high = grad.astype(BF)
        g_hi[j] = high
        g_lo[j] = (grad - high.astype(F32)).astype(BF)
        flipped = grad.T
        high = flipped.astype(BF)
        low = (flipped - high.astype(F32)).astype(BF)
        part = part + (dot(high, column[j]) + dot(low, column[j]))
    for col in range(2):
        grad_send[0, col] = part[:, 256 * col : 256 * col + 256].astype(BF)

    def candidates():
        for j in range(8):
            sums = jnp.sum(scores[j], axis=1, keepdims=True)
            rows[j] = (
                dot(g_hi[j], q_hi[...]) + dot(g_hi[j], q_lo[...]) + dot(g_lo[j], q_hi[...])
            ) - column[j].astype(F32) * sums

    exchange_sum(me, wire, grad_send, grad_recv, summed, candidates)

    query_grad = jnp.concatenate(
        [
            summed[:, 128 * j : 128 * j + 128] - queries[:, 128 * j : 128 * j + 128] * rest_col
            for j in range(4)
        ],
        axis=1,
    ).astype(BF)

    def row_part(chunk):
        pick = jnp.where(row_ids + 128 * chunk == head_row, 1.0, 0.0).astype(BF)
        return rows[chunk] + dot(pick, query_grad)

    order = (1, 3, 2, 0)
    core_copies = {}
    for at, d in enumerate(order):
        chunk = (1 - me.k) * 4 + (me.g + d) % 4
        core_send[d] = row_part(chunk).astype(BF)
        core_copies[d] = wire.put(core_send.at[d], core_recv.at[d], me.sibling())
    y_copies = []
    for d in order:
        own = row_part(me.k * 4 + (me.g + d) % 4)
        core_copies[d].wait_recv()
        total = own + core_recv[d].astype(F32)
        if d:
            y_send[d - 1] = total.astype(BF)
            y_copies.append(
                wire.put(y_send.at[d - 1], y_recv.at[d - 1], me.peer("y", (me.g + d) % 4))
            )
    for d in (1, 3, 2):
        loss_copies[d].wait_recv()
    loss_rows = []
    for d in range(4):
        row = ((me.g + d) % 4) * 2 + me.k
        loss_rows.append(wire.put(loss.at[row], loss.at[row], me.sibling()))
    for copy in y_copies:
        copy.wait_recv()
    for d in range(3):
        total = total + y_recv[d].astype(F32)
    activated = act[...]
    pre_grad = (((2.0 * scale) * total) * (1.0 - activated * activated)).astype(BF)
    pre_all[me.g] = pre_grad
    pre_copies = to_y(pre_all, me.g)
    agg_tiles[me.g] = dot(pre_grad, w_in[...], NT).astype(BF)
    for d in (1, 3, 2):
        pre_copies[d].wait_recv()
        other = (me.g + 4 - d) % 4
        agg_tiles[other] = dot(pre_all[other], w_in[...], NT).astype(BF)
    for d in (1, 3, 2):
        agg_copies[d].wait_recv()
    for copy in loss_rows:
        copy.wait_recv()
    wire.drain()


def middle(partial_low, partial, self_part, w_in, query_part, query_head, true_tail, allowed):
    depth = w_in.shape[0]
    copies = 64
    tile_bf = jax.ShapeDtypeStruct((4, 128, depth), BF)
    return pl.pallas_call(
        middle_kernel,
        name="middle",
        out_shape=(
            jax.ShapeDtypeStruct((1, 128, depth), BF),
            jax.ShapeDtypeStruct((8, 1, 128), F32),
            tile_bf,
            tile_bf,
            tile_bf,
        ),
        in_specs=[VMEM_SPEC] * 8,
        out_specs=(VMEM_SPEC,) * 5,
        scratch_shapes=[
            pltpu.VMEM((3, 128, depth), BF),
            pltpu.VMEM((128, depth), F32),
            pltpu.VMEM((8, 128, depth), BF),
            pltpu.VMEM((2, 2, 128, 256), BF),
            pltpu.VMEM((2, 2, 3, 128, 256), BF),
            pltpu.VMEM((128, depth), F32),
            pltpu.VMEM((128, depth), BF),
            pltpu.VMEM((128, depth), BF),
            pltpu.VMEM((8, 128, 128), F32),
            pltpu.VMEM((2, 4, 8, 128), F32),
            pltpu.VMEM((2, 2, 128, 256), BF),
            pltpu.VMEM((2, 2, 3, 128, 256), BF),
            pltpu.VMEM((128, depth), F32),
            pltpu.VMEM((8, 128, 128), BF),
            pltpu.VMEM((8, 128, 128), BF),
            pltpu.VMEM((8, 128, depth), F32),
            pltpu.VMEM((4, 128, depth), BF),
            pltpu.VMEM((4, 128, depth), BF),
            pltpu.VMEM((3, 128, depth), BF),
            pltpu.VMEM((3, 128, depth), BF),
            pltpu.SemaphoreType.DMA((copies,)),
            pltpu.SemaphoreType.DMA((copies,)),
        ],
        compiler_params=pltpu.CompilerParams(
            collective_id=1, has_side_effects=True, vmem_limit_bytes=LIMIT
        ),
    )(partial_low, partial, self_part, w_in, query_part, query_head, true_tail, allowed)


def return_kernel(
    n_ar,
    tiles, rel_part, agg_all, pre_all, node, w_self, requests,
    node_grad, summed, w_all,
    arrived, shipped, y_recv, x_send, joined, self_grad, *rest,
):
    ar_refs = rest[:n_ar]
    send_sem, recv_sem, local_sem = rest[n_ar:]
    me = Place()
    devices = []
    for e in range(1, 8):
        devices.append(me.dev(me.g, me.x * 8 + (me.zk + e) % 8))
    for e in range(1, 8):
        other = (me.xk + e) % 8
        devices.append(me.dev(me.g, (other // 2) * 8 + me.z * 2 + other % 2))
    for d in (1, 2, 3):
        devices.append(me.peer("y", (me.g + d) % 4))
    enter(devices)
    wire = Wire(send_sem, recv_sem)
    reduce = AllReduce(me, wire, 16, STAGES_CAND, ar_refs, summed, w_all)
    steps = reduce.steps()

    def advance():
        next(steps, None)

    axes = ((0, "x"), (1, "z"))
    order = (1, 3, 2, 0)
    own_slots = (me.zk, me.xk)
    moved = {}

    def send_round(d):
        for col, axis in axes:
            place = (me.at(axis) + d) % 4
            for e in range(1, 8):
                slot = (own_slots[col] + e) % 8
                moved[d, col, e] = wire.put(
                    tiles.at[col, slot, place],
                    arrived.at[col, own_slots[col], place],
                    devices[7 * col + e - 1],
                )

    send_round(order[0])
    local = []
    for col in range(2):
        copy = pltpu.make_async_copy(
            tiles.at[col, own_slots[col]], arrived.at[col, own_slots[col]], local_sem.at[col]
        )
        copy.start()
        local.append(copy)
    cols = pl.ds(pl.multiple_of(me.g * 128, 128), 128)
    right = pre_all[:, :, cols].reshape(512, 128)
    for which, left in ((0, agg_all), (1, node)):
        for q in range(4):
            turned = left[:, :, 128 * q : 128 * q + 128].astype(F32).reshape(512, 128).T.astype(BF)
            reduce.part[2 * which + q // 2, 8 * (q % 2) : 8 * (q % 2) + 8, 0:16] = (
                dot(turned, right).reshape(8, 16, 128).astype(BF)
            )
    for q in range(2):
        for j in range(4):
            reduce.part[j, 8 * q : 8 * q + 8, 16:32] = (
                rel_part[128 * q : 128 * q + 128, 128 * j : 128 * j + 128]
                .reshape(8, 16, 128)
                .astype(BF)
            )
    advance()
    send_round(order[1])
    self_grad[...] = dot(pre_all[me.g], w_self[...], NT)
    advance()
    for copy in local:
        copy.wait()
    over_y = {}
    second = []

    def combine(d, col):
        for copy in over_y[d, col]:
            copy.wait_recv()
        total = shipped[col, d, me.g].astype(F32)
        for m in range(3):
            total = total + y_recv[col, d, m].astype(F32)
        return total

    def send_combined(d):
        for col, axis in axes:
            x_send[col, d - 1] = combine(d, col).astype(BF)
            second.append(
                wire.put(
                    x_send.at[col, d - 1],
                    joined.at[col, d - 1],
                    me.peer(axis, (me.at(axis) + d) % 4),
                )
            )

    for at, d in enumerate(order):
        for col, axis in axes:
            place = (me.at(axis) + d) % 4
            owner = place * 8 + me.zk if col == 0 else me.x * 8 + place * 2 + me.k
            for e in range(1, 8):
                moved[d, col, e].wait_recv()
            index = [requests[8 * col + m, 0, owner] for m in range(8)]
            for part in range(4):
                rows = pl.ds(part * 32, 32)
                values = [arrived[col, m, place, rows, :].astype(F32) for m in range(8)]
                for s in range(4):
                    total = jnp.zeros((32, 256), F32)
                    for m in range(8):
                        total = total + jnp.where(index[m] == s, values[m], 0.0)
                    shipped[col, d, s, rows, :] = total.astype(BF)
            over_y[d, col] = []
            for e in (1, 3, 2):
                s = (me.g + e) % 4
                over_y[d, col].append(
                    wire.put(
                        shipped.at[col, d, s], y_recv.at[col, d, e - 1], me.peer("y", s)
                    )
                )
        advance()
        if at + 2 < 4:
            send_round(order[at + 2])
        if at:
            send_combined(order[at - 1])
    advance()
    pair = pl.ds(2 * me.k, 2)
    last = [
        wire.put(summed.at[pair], summed.at[pair], me.sibling()),
        wire.put(w_all.at[:, pair], w_all.at[:, pair], me.sibling()),
    ]
    for copy in second:
        copy.wait_recv()
    for col in range(2):
        total = combine(0, col)
        for m in range(3):
            total = total + joined[col, m].astype(F32)
        node_grad[0, :, 256 * col : 256 * col + 256] = (
            total + self_grad[:, 256 * col : 256 * col + 256]
        )
    for copy in last:
        copy.wait_recv()
    wire.drain()


def give_back(tiles, rel_part, agg_all, pre_all, node_tiles, w_self, requests):
    depth = w_self.shape[0]
    ar = AllReduce.scratch(16, STAGES_CAND, 32)
    copies = 56 + 24 + 6 + (1 + 12 + 6 + 24) + 2
    return pl.pallas_call(
        functools.partial(return_kernel, len(ar)),
        name="give_back",
        out_shape=(
            jax.ShapeDtypeStruct((1, 128, depth), F32),
            jax.ShapeDtypeStruct((4, 16, 16, 128), BF),
            jax.ShapeDtypeStruct((4, 4, 16, 16, 128), BF),
        ),
        in_specs=[ANY_SPEC] + [VMEM_SPEC] * 5 + [SMEM_SPEC],
        out_specs=(VMEM_SPEC,) * 3,
        scratch_shapes=[
            pltpu.VMEM((2, 8, 4, 128, 256), BF),
            pltpu.VMEM((2, 4, 4, 128, 256), BF),
            pltpu.VMEM((2, 4, 3, 128, 256), BF),
            pltpu.VMEM((2, 3, 128, 256), BF),
            pltpu.VMEM((2, 3, 128, 256), BF),
            pltpu.VMEM((128, depth), F32),
            *ar,
            pltpu.SemaphoreType.DMA((copies,)),
            pltpu.SemaphoreType.DMA((copies,)),
            pltpu.SemaphoreType.DMA((2,)),
        ],
        compiler_params=pltpu.CompilerParams(
            collective_id=2, has_side_effects=True, vmem_limit_bytes=LIMIT
        ),
    )(tiles, rel_part, agg_all, pre_all, node_tiles, w_self, requests)


def finish_kernel(node_in, summed, w_all, node_grad, rel_grad, w_in_grad, w_self_grad):
    node_grad[...] = node_in[...]
    for j in range(4):
        cols = slice(128 * j, 128 * j + 128)
        whole = summed[j].astype(F32).reshape(256, 128)
        rel_grad[:, cols] = whole[: rel_grad.shape[0]]
        for q in range(2):
            rows = slice(256 * q, 256 * q + 256)
            for at, target in ((q, w_in_grad), (2 + q, w_self_grad)):
                target[rows, cols] = w_all[j, at].astype(F32).reshape(256, 128)


def finish(node_grad, summed, w_all, relations):
    depth = node_grad.shape[2]
    return pl.pallas_call(
        finish_kernel,
        name="finish",
        out_shape=(
            jax.ShapeDtypeStruct(node_grad.shape, F32),
            jax.ShapeDtypeStruct((relations, depth), F32),
            jax.ShapeDtypeStruct((depth, depth), F32),
            jax.ShapeDtypeStruct((depth, depth), F32),
        ),
        in_specs=[VMEM_SPEC] * 3,
        out_specs=(VMEM_SPEC,) * 4,
    )(node_grad, summed, w_all)


def body(
    node_emb,
    rel_emb,
    w_in,
    w_self,
    rel_score,
    mirror_blocks,
    adj_values,
    adj_source,
    adj_target,
    adj_relation,
    live_blocks,
    query_head,
    query_rel,
    allowed,
    true_tail,
):
    wanted = mirror_blocks.reshape(1, 32)
    node_tiles = node_emb.reshape(4, 128, -1)
    mirrors, requests, self_part = fetch(node_tiles, wanted, w_self)
    partial, partial_low, query_part = forward(
        adj_source, adj_target, adj_relation, live_blocks, adj_values, mirrors, rel_emb,
        query_rel, rel_score,
    )
    h, loss, agg_all, pre_all, agg_tiles = middle(
        partial_low,
        partial,
        self_part,
        w_in,
        query_part,
        query_head.reshape(1, -1),
        true_tail.reshape(1, -1),
        allowed.T,
    )
    tiles, rel_part, h_out, loss = backward(
        adj_source, adj_target, adj_relation, live_blocks, adj_values, agg_tiles, h, loss
    )
    node_grad, summed, w_all = give_back(
        tiles.reshape(2, 8, 4, 128, 256),
        rel_part,
        agg_all,
        pre_all,
        node_tiles,
        w_self,
        requests,
    )
    node_grad, rel_grad, w_in_grad, w_self_grad = finish(
        node_grad, summed, w_all, rel_emb.shape[0]
    )
    return (h_out, loss.reshape(-1), node_grad, rel_grad, w_in_grad, w_self_grad)


def solution(mesh):
    return jax.shard_map(
        body,
        mesh=mesh,
        in_specs=(
            P("cand", None, None),
            P("grp", None),
            P(),
            P(),
            P(),
            P("grp", "cand", None, None),
            P("grp", "cand", None, None, None),
            P("grp", "cand", None),
            P("grp", "cand", None),
            P("grp", "cand", None),
            P("grp", "cand"),
            P(),
            P(),
            P(),
            P(),
        ),
        out_specs=(P("cand", "grp", None), P(), P("cand", "grp", None), P("grp", None), P(), P()),
        check_vma=False,
    )
```

```python
import functools

import jax
import jax.numpy as jnp
from jax import lax
from jax.experimental import pallas as pl
from jax.experimental.pallas import tpu as pltpu
from jax.sharding import PartitionSpec as P

NEG_FILL = -1e30
MESH = pl.DeviceIdType.MESH
BF = jnp.bfloat16
F32 = jnp.float32
NN = (((1,), (0,)), ((), ()))
NT = (((1,), (1,)), ((), ()))
TN = (((0,), (0,)), ((), ()))
VMEM_SPEC = pl.BlockSpec(memory_space=pltpu.VMEM)
SMEM_SPEC = pl.BlockSpec(memory_space=pltpu.SMEM)
ANY_SPEC = pl.BlockSpec(memory_space=pl.ANY)
LIMIT = 60 * 1024 * 1024
STAGES_CAND = (("z", "x"), ("x", "z"))


def dot(a, b, dims=NN):
    return lax.dot_general(a, b, dims, preferred_element_type=F32)


class Place:
    def __init__(self):
        self.g = lax.axis_index("grp")
        self.c = lax.axis_index("cand")
        self.x = self.c // 8
        self.zk = self.c % 8
        self.z = self.zk // 2
        self.k = self.c % 2
        self.xk = self.x * 2 + self.k

    def dev(self, g, c):
        return {"grp": g, "cand": c}

    def at(self, axis):
        return {"x": self.x, "z": self.z, "y": self.g}[axis]

    def peer(self, axis, other):
        if axis == "y":
            return self.dev(other, self.c)
        if axis == "x":
            return self.dev(self.g, other * 8 + self.zk)
        return self.dev(self.g, self.x * 8 + other * 2 + self.k)

    def sibling(self):
        return self.dev(self.g, self.c + 1 - 2 * self.k)


def enter(devices):
    barrier = pltpu.get_barrier_semaphore()
    for device in devices:
        pl.semaphore_signal(barrier, inc=1, device_id=device, device_id_type=MESH)
    pl.semaphore_wait(barrier, len(devices))


class Wire:
    def __init__(self, send_sem, recv_sem):
        self.send_sem, self.recv_sem, self.count, self.sent = send_sem, recv_sem, 0, []

    def put(self, src, dst, device):
        at = self.count
        self.count += 1
        copy = pltpu.make_async_remote_copy(
            src_ref=src,
            dst_ref=dst,
            send_sem=self.send_sem.at[at],
            recv_sem=self.recv_sem.at[at],
            device_id=device,
            device_id_type=MESH,
        )
        copy.start()
        self.sent.append(copy)
        return copy

    def drain(self):
        for copy in self.sent:
            copy.wait_send()


def add_up(read_terms, write, count):
    chunk = min(count, 8)

    def one(i, carry):
        at = pl.ds(i * chunk, chunk)
        terms = read_terms(at)
        total = terms[0].astype(F32)
        for term in terms[1:]:
            total = total + term.astype(F32)
        write(at, total)
        return carry

    if count == chunk:
        one(0, 0)
    else:
        lax.fori_loop(0, count // chunk, one, 0)


class AllReduce:
    @staticmethod
    def scratch(shards, stages, height):
        depth = len(stages[0])
        shapes = [
            pltpu.VMEM((4, shards, height, 128), BF),
            pltpu.VMEM((2, shards, height, 128), BF),
        ]
        for level in range(depth):
            shapes.append(pltpu.VMEM((2, shards // 4**level, height, 128), BF))
            shapes.append(pltpu.VMEM((2, 3, shards // 4 ** (level + 1), height, 128), BF))
        return shapes

    def __init__(self, me, wire, shards, stages, refs, summed, w_all):
        self.me, self.wire, self.shards, self.stages = me, wire, shards, stages
        self.part, self.rcore = refs[:2]
        self.summed, self.w_all = summed, w_all
        depth = len(stages[0])
        self.acc = refs[2 : 2 + 2 * depth : 2]
        self.recv = refs[3 : 3 + 2 * depth : 2]
        self.sizes = [shards // 4 ** (i + 1) for i in range(depth)]

    def steps(self):
        me, wire = self.me, self.wire
        mine = 2 * me.k
        copy = wire.put(self.part.at[pl.ds(2 - mine, 2)], self.rcore, me.sibling())
        yield
        copy.wait_recv()
        for col in range(2):

            def write(at, value, col=col):
                self.acc[0][col, at] = value.astype(BF)

            add_up(
                lambda at, col=col: (self.part[mine + col, at], self.rcore[col, at]),
                write,
                self.shards,
            )
        offsets = [0, 0]
        history = []
        depth = len(self.sizes)
        for level in range(depth):
            size = self.sizes[level]
            copies = []
            for d in (1, 3, 2):
                for col in range(2):
                    axis = self.stages[col][level]
                    other = (me.at(axis) + d) % 4
                    copies.append(
                        wire.put(
                            self.acc[level].at[col, pl.ds(other * size, size)],
                            self.recv[level].at[col, d - 1],
                            me.peer(axis, other),
                        )
                    )
            yield
            for copy in copies:
                copy.wait_recv()
            for col in range(2):
                own = me.at(self.stages[col][level]) * size
                offsets[col] = offsets[col] + own

                def terms(at, col=col, own=own, level=level):
                    base = pl.ds(own + at.start, at.size)
                    return [self.acc[level][col, base]] + [
                        self.recv[level][col, d, at] for d in range(3)
                    ]

                def write(at, value, col=col, level=level):
                    if level + 1 < depth:
                        self.acc[level + 1][col, at] = value.astype(BF)
                    else:
                        final = value.astype(BF)
                        place = pl.ds(offsets[col] + at.start, at.size)
                        self.w_all[me.g, mine + col, place] = final[:, 0:16]
                        self.summed[mine + col, place] = final[:, 16:32]

                add_up(terms, write, size)
            history.append(tuple(offsets))
        copies = []
        for d in (1, 3, 2):
            for col in range(2):
                place = self.w_all.at[me.g, mine + col, pl.ds(offsets[col], self.sizes[-1])]
                copies.append(wire.put(place, place, me.peer("y", (me.g + d) % 4)))
        yield
        for copy in copies:
            copy.wait_recv()
        for level in reversed(range(depth)):
            size = self.sizes[level]
            copies = []
            for d in (1, 3, 2):
                for col in range(2):
                    axis = self.stages[col][level]
                    other = (me.at(axis) + d) % 4
                    shards = pl.ds(history[level][col], size)
                    for place in (
                        self.summed.at[mine + col, shards],
                        self.w_all.at[:, mine + col, shards],
                    ):
                        copies.append(wire.put(place, place, me.peer(axis, other)))
            yield
            for copy in copies:
                copy.wait_recv()


def fetch_kernel(
    node, wanted_v, w_self,
    mirrors, requests, self_part,
    wanted_row, request_s, staged, send_sem, recv_sem, local_sem, *gathered,
):
    me = Place()
    devices = []
    for e in range(1, 8):
        devices.append(me.dev(me.g, me.x * 8 + (me.zk + e) % 8))
    for e in range(1, 8):
        other = (me.xk + e) % 8
        devices.append(me.dev(me.g, (other // 2) * 8 + me.z * 2 + other % 2))
    for d in (1, 2, 3):
        devices.append(me.peer("y", (me.g + d) % 4))
    enter(devices)
    wire = Wire(send_sem, recv_sem)
    wanted_row[...] = jnp.zeros_like(wanted_row)
    wanted_row[:, 0:32] = wanted_v[...]
    halves = (pl.ds(0, 256), pl.ds(256, 256))
    first = {}
    for d in (1, 3, 2):
        for col, axis in ((0, "x"), (1, "z")):
            other = (me.at(axis) + d) % 4
            first[col, d] = wire.put(
                node.at[me.g, :, halves[col]],
                gathered[3 * col + d - 1].at[me.g],
                me.peer(axis, other),
            )
    asks = []
    for e in range(1, 8):
        for col in range(2):
            asks.append(
                wire.put(
                    wanted_row,
                    requests.at[8 * col + (me.zk if col == 0 else me.xk)],
                    devices[7 * col + e - 1],
                )
            )
    requests[me.zk] = wanted_row[...]
    requests[8 + me.xk] = wanted_row[...]
    spread = {}

    def pass_on(d):
        for col in range(2):
            first[col, d].wait_recv()
            place = gathered[3 * col + d - 1].at[me.g]
            spread[col, d] = [
                wire.put(place, place, me.peer("y", (me.g + e) % 4)) for e in (1, 3, 2)
            ]

    pass_on(1)
    for copy in asks:
        copy.wait_recv()
    local = pltpu.make_async_copy(requests, request_s, local_sem)
    local.start()
    local.wait()
    moved = []
    for d in (0, 1, 3, 2):
        for col, axis in ((0, "x"), (1, "z")):
            if d:
                for copy in spread[col, d]:
                    copy.wait_recv()
            origin = (me.at(axis) + 4 - d) % 4
            own_slot = me.zk if col == 0 else me.xk
            owner = origin * 8 + me.zk if col == 0 else me.x * 8 + origin * 2 + me.k
            for e in range(8):
                slot = (own_slot + e) % 8
                index = request_s[8 * col + slot, 0, owner]
                if d:
                    tile = gathered[3 * col + d - 1][index]
                else:
                    tile = node[index, :, 256 * col : 256 * col + 256]
                if e == 0:
                    mirrors[col, own_slot, origin] = tile
                else:
                    staged[col, e - 1, d] = tile
                    moved.append(
                        wire.put(
                            staged.at[col, e - 1, d],
                            mirrors.at[col, own_slot, origin],
                            devices[7 * col + e - 1],
                        )
                    )
        if d == 0:
            pass_on(3)
            pass_on(2)
    self_part[...] = dot(node[me.g], w_self[...])
    for copy in moved:
        copy.wait_recv()
    wire.drain()


def fetch(node_tiles, wanted, w_self):
    depth = node_tiles.shape[2]
    copies = 6 + 14 + 56 + 18
    return pl.pallas_call(
        fetch_kernel,
        name="fetch",
        out_shape=(
            jax.ShapeDtypeStruct((2, 8, 4, 128, 256), BF),
            jax.ShapeDtypeStruct((16, 1, 128), jnp.int32),
            jax.ShapeDtypeStruct((128, depth), F32),
        ),
        in_specs=[VMEM_SPEC] * 3,
        out_specs=(VMEM_SPEC,) * 3,
        scratch_shapes=[
            pltpu.VMEM((1, 128), jnp.int32),
            pltpu.SMEM((16, 1, 128), jnp.int32),
            pltpu.VMEM((2, 7, 4, 128, 256), BF),
            pltpu.SemaphoreType.DMA((copies,)),
            pltpu.SemaphoreType.DMA((copies,)),
            pltpu.SemaphoreType.DMA,
            *[pltpu.VMEM((4, 128, 256), BF)] * 6,
        ],
        compiler_params=pltpu.CompilerParams(
            collective_id=0, has_side_effects=True, vmem_limit_bytes=LIMIT
        ),
    )(node_tiles, wanted, w_self)


GROUP = 24


def slots_of(source):
    x, zk = source // 8, source % 8
    z, k = zk // 2, zk % 2
    return zk * 4 + x, (x * 2 + k) * 4 + z


def forward_kernel(
    source, target, relation, live, values, mirrors, rel_emb, query_rel, rel_score,
    out, out_low, query_part,
):
    step = pl.program_id(0)
    first = (lax.axis_index("grp") * 2 + lax.axis_index("cand") % 2) * 128

    for j in range(16):
        row = step * 16 + j
        query_part[pl.ds(row, 1), :] = rel_score[pl.ds(query_rel[first + row], 1), :]

    @pl.when(step == 0)
    def _():
        out[...] = jnp.zeros_like(out)

    count = live[0, 0]

    @pl.when(step * GROUP < count)
    def _():
        for j in range(GROUP):
            b = step * GROUP + j
            slots = slots_of(source[0, 0, b])
            t = target[0, 0, b]
            block = values[0, 0, j]
            block = jnp.where(b < count, block, jnp.zeros_like(block))
            row = rel_emb[pl.ds(relation[0, 0, b], 1), :]
            for col in range(2):
                part = slice(256 * col, 256 * col + 256)
                composed = (mirrors[col, slots[col]].astype(F32) - row[:, part]).astype(BF)
                out[t, :, part] += dot(block, composed)

    @pl.when(step == pl.num_programs(0) - 1)
    def _():
        for t in range(4):
            out_low[t] = out[t].astype(BF)


def adjacency_specs(blocks):
    return [SMEM_SPEC] * 4 + [
        pl.BlockSpec((1, 1, GROUP, 128, 128), lambda i: (0, 0, i, 0, 0)),
    ]


def forward(
    adj_source, adj_target, adj_relation, live_blocks, adj_values, mirrors, rel_emb, query_rel, rel_score
):
    blocks = adj_values.shape[2]
    depth = rel_score.shape[1]
    return pl.pallas_call(
        forward_kernel,
        name="forward_blocks",
        grid=(blocks // GROUP,),
        out_shape=(
            jax.ShapeDtypeStruct((4, 128, depth), F32),
            jax.ShapeDtypeStruct((4, 128, depth), BF),
            jax.ShapeDtypeStruct((128, depth), F32),
        ),
        in_specs=adjacency_specs(blocks) + [VMEM_SPEC] * 2 + [SMEM_SPEC, VMEM_SPEC],
        out_specs=(VMEM_SPEC,) * 3,
        compiler_params=pltpu.CompilerParams(vmem_limit_bytes=LIMIT),
    )(
        adj_source, adj_target, adj_relation, live_blocks, adj_values,
        mirrors.reshape(2, 32, 128, 256), rel_emb, query_rel, rel_score,
    )


def backward_kernel(
    source, target, relation, live, values, agg, h_in, loss_in,
    tiles_out, rel_out, h_out, loss_out, tiles,
):
    step = pl.program_id(0)

    @pl.when(step == 0)
    def _():
        def clear(i, carry):
            for col in range(2):
                tiles[col, i] = jnp.zeros((128, 256), F32)
            return carry

        lax.fori_loop(0, 32, clear, 0)
        rel_out[...] = jnp.zeros_like(rel_out)
        h_out[...] = h_in[...]
        for j in range(8):
            loss_out[j : j + 1, :] = loss_in[j]

    count = live[0, 0]

    @pl.when(step * GROUP < count)
    def _():
        for j in range(GROUP):
            b = step * GROUP + j
            slots = slots_of(source[0, 0, b])
            r = pl.ds(relation[0, 0, b], 1)
            block = values[0, 0, j]
            block = jnp.where(b < count, block, jnp.zeros_like(block))
            grad = dot(block, agg[target[0, 0, b]], TN)
            rel_out[r, :] -= jnp.sum(grad, axis=0, keepdims=True)
            for col in range(2):
                tiles[col, slots[col]] += grad[:, 256 * col : 256 * col + 256]

    @pl.when(step == pl.num_programs(0) - 1)
    def _():
        def store(i, carry):
            for col in range(2):
                tiles_out[col, i] = tiles[col, i].astype(BF)
            return carry

        lax.fori_loop(0, 32, store, 0)


def backward(adj_source, adj_target, adj_relation, live_blocks, adj_values, agg_tiles, h, loss):
    blocks = adj_values.shape[2]
    return pl.pallas_call(
        backward_kernel,
        name="backward_blocks",
        grid=(blocks // GROUP,),
        out_shape=(
            jax.ShapeDtypeStruct((2, 32, 128, 256), BF),
            jax.ShapeDtypeStruct((256, 512), F32),
            jax.ShapeDtypeStruct(h.shape, h.dtype),
            jax.ShapeDtypeStruct((8, 128), F32),
        ),
        in_specs=adjacency_specs(blocks) + [VMEM_SPEC] * 3,
        out_specs=(VMEM_SPEC,) * 4,
        scratch_shapes=[pltpu.VMEM((2, 32, 128, 256), F32)],
        compiler_params=pltpu.CompilerParams(vmem_limit_bytes=LIMIT),
    )(adj_source, adj_target, adj_relation, live_blocks, adj_values, agg_tiles, h, loss)


def exchange_sum(me, wire, send, recv, out, during=None):
    for level in range(2):
        copies = []
        for d in (1, 3, 2):
            for col in range(2):
                axis = STAGES_CAND[col][level]
                other = (me.at(axis) + d) % 4
                copies.append(
                    wire.put(
                        send.at[level, col], recv.at[level, col, d - 1], me.peer(axis, other)
                    )
                )
        if level == 0 and during is not None:
            during()
        for copy in copies:
            copy.wait_recv()
        for col in range(2):
            total = send[level, col].astype(F32)
            for d in range(3):
                total = total + recv[level, col, d].astype(F32)
            if level == 0:
                send[1, col] = total.astype(BF)
            else:
                out[:, 256 * col : 256 * col + 256] = total


class GatherY:
    def __init__(self, me, wire, ref, slot):
        self.me, self.wire, self.ref, self.slot = me, wire, ref, slot
        self.near = (me.peer("y", (me.g + 1) % 4), me.peer("y", (me.g + 3) % 4))
        self.first = [self.put(0, 0, 0), self.put(0, 1, 1)]
        self.second = [self.put(0, 1, 0), self.put(0, 0, 1)]

    def put(self, d, half, way):
        place = self.ref.at[self.slot(d), pl.ds(64 * half, 64)]
        return self.wire.put(place, place, self.near[way])

    def neighbours(self):
        self.first[0].wait_recv()
        far = [self.put(1, 0, 0)]
        self.first[1].wait_recv()
        far.append(self.put(3, 1, 1))
        for copy in self.second:
            copy.wait_recv()
        self.far = far

    def opposite(self):
        for copy in self.far:
            copy.wait_recv()


def middle_kernel(
    partial_low, partial, self_part, w_in, query_part, query_head, true_tail, allowed,
    h_out, loss, agg_all, pre_all, agg_tiles,
    share_recv, act, column, head_send, head_recv, queries, q_hi, q_lo, scores, stats,
    h_sq, grad_send, grad_recv, summed, g_hi, g_lo, rows, core_send, core_recv, y_send, y_recv,
    send_sem, recv_sem,
):
    me = Place()
    plane = []
    for dx, dz in sorted(
        [(i, j) for i in range(4) for j in range(4) if i or j],
        key=lambda p: -(min(p[0], 4 - p[0]) + min(p[1], 4 - p[1])),
    ):
        plane.append(
            me.dev(me.g, ((me.x + dx) % 4) * 8 + ((me.z + dz) % 4) * 2 + me.k)
        )
    enter(
        [me.sibling()] + [me.peer("y", (me.g + d) % 4) for d in (1, 2, 3)] + plane
    )
    wire = Wire(send_sem, recv_sem)
    count = true_tail.shape[1]
    scale = 512 ** (-0.5)
    group = me.g * 2 + me.k
    lanes = pl.ds(pl.multiple_of(group * 128, 128), 128)
    first_chip = me.x * 8 + me.z * 2
    base = first_chip * 512

    def to_y(ref, at, order=(1, 3, 2)):
        copies = {}
        for d in order:
            copies[d] = wire.put(ref.at[at], ref.at[at], me.peer("y", (me.g + d) % 4))
        return copies

    copies = []
    for d in (1, 3, 2):
        other = (me.g + d) % 4
        copies.append(wire.put(partial_low.at[other], share_recv.at[d - 1], me.peer("y", other)))
    for copy in copies:
        copy.wait_recv()
    total = partial[me.g]
    for d in range(3):
        total = total + share_recv[d].astype(F32)
    agg = total.astype(BF)
    activated = jnp.tanh(dot(agg, w_in[...]) + self_part[...])
    h = activated.astype(BF)
    own_chunk = me.k * 4 + me.g
    column[own_chunk] = h
    gather_h = GatherY(me, wire, column, lambda d: me.k * 4 + (me.g + 4 - d) % 4)
    from_sibling = [wire.put(column.at[own_chunk], column.at[own_chunk], me.sibling())]
    h_out[0] = h
    act[...] = activated
    agg_all[me.g] = agg
    gather_h.neighbours()
    for d in (1, 3, 2):
        if d == 2:
            gather_h.opposite()
        chunk = me.k * 4 + (me.g + 4 - d) % 4
        from_sibling.append(wire.put(column.at[chunk], column.at[chunk], me.sibling()))

    agg_copies = to_y(agg_all, me.g)

    head_row = jnp.broadcast_to(query_head[:, lanes] - base, (128, 128))
    head_col = head_row.astype(F32).T
    lane_ids = lax.broadcasted_iota(jnp.int32, (128, 128), 1).astype(F32)
    row_ids = lax.broadcasted_iota(jnp.int32, (128, 128), 0)
    for copy in from_sibling:
        copy.wait_recv()
    part = jnp.zeros((128, 512), F32)
    for j in range(8):
        pick = jnp.where(head_col == lane_ids + 128.0 * j, 1.0, 0.0).astype(BF)
        part = part + dot(pick, column[j])
    for col in range(2):
        head_send[0, col] = part[:, 256 * col : 256 * col + 256].astype(BF)

    def squares():
        for j in range(8):
            h32 = column[j].astype(F32)
            h_sq[j] = jnp.broadcast_to(jnp.sum(h32 * h32, axis=1, keepdims=True), (128, 128))

    exchange_sum(me, wire, head_send, head_recv, summed, squares)

    q = summed[...] + query_part[...]
    queries[...] = q
    high = q.astype(BF)
    q_hi[...] = high
    q_lo[...] = (q - high.astype(F32)).astype(BF)
    square = jnp.zeros((128, 128), F32)
    for j in range(4):
        piece = q[:, 128 * j : 128 * j + 128]
        square = square + piece * piece
    q_sq = jnp.sum(square.T, axis=0, keepdims=True)
    tail_row = jnp.broadcast_to(true_tail[:, lanes] - base, (128, 128))
    kinds = allowed[:, lanes]

    def allowed_row(j):
        hit = jnp.where(kinds == first_chip * 4 + j, 1.0, 0.0)
        return jnp.max(hit, axis=0, keepdims=True)

    masks = [jnp.broadcast_to(allowed_row(j), (128, 128)) > 0.5 for j in range(8)]
    tops, truths = [], []
    for j in range(8):
        cross = dot(column[j], q_hi[...], NT) + dot(column[j], q_lo[...], NT)
        score = -scale * (q_sq + h_sq[j] - 2.0 * cross)
        scores[j] = score
        tops.append(jnp.max(jnp.where(masks[j], score, NEG_FILL), axis=0, keepdims=True))
        truths.append(
            jnp.sum(
                jnp.where(row_ids + 128 * j == tail_row, score, 0.0), axis=0, keepdims=True
            )
        )
    top = functools.reduce(jnp.maximum, tops)
    weight = jnp.zeros((1, 128), F32)
    for j in range(8):
        weight = weight + jnp.sum(
            jnp.exp(jnp.where(masks[j], scores[j] - top, NEG_FILL)), axis=0, keepdims=True
        )
    stats[0, 0:1, :] = top
    stats[0, 1:2, :] = weight
    stats[0, 2:3, :] = functools.reduce(lambda a, b: a + b, truths)

    copies = [wire.put(stats.at[0], stats.at[e + 1], plane[e]) for e in range(15)]
    for copy in copies:
        copy.wait_recv()
    members = [stats[m] for m in range(16)]
    tops = [m[0:1, :] for m in members]
    top = functools.reduce(jnp.maximum, tops)
    weight = jnp.zeros((1, 128), F32)
    truth = jnp.zeros((1, 128), F32)
    for m in range(16):
        weight = weight + members[m][1:2, :] * jnp.exp(tops[m] - top)
        truth = truth + members[m][2:3, :]
    log_norm = top + jnp.log(weight)
    loss[group] = log_norm - truth
    loss_copies = to_y(loss, group)
    rest_sum = (weight * jnp.exp(top - log_norm) - 1.0) / count
    rest_col = jnp.broadcast_to(rest_sum, (128, 128)).T

    part = jnp.zeros((128, 512), F32)
    for j in range(8):
        prob = jnp.exp(jnp.where(masks[j], scores[j] - log_norm, NEG_FILL))
        tail = jnp.where(row_ids + 128 * j == tail_row, 1.0, 0.0)
        grad = (prob - tail) / count
        scores[j] = grad
        high = grad.astype(BF)
        g_hi[j] = high
        g_lo[j] = (grad - high.astype(F32)).astype(BF)
        flipped = grad.T
        high = flipped.astype(BF)
        low = (flipped - high.astype(F32)).astype(BF)
        part = part + (dot(high, column[j]) + dot(low, column[j]))
    for col in range(2):
        grad_send[0, col] = part[:, 256 * col : 256 * col + 256].astype(BF)

    def candidates():
        for j in range(8):
            sums = jnp.sum(scores[j], axis=1, keepdims=True)
            rows[j] = (
                dot(g_hi[j], q_hi[...]) + dot(g_hi[j], q_lo[...]) + dot(g_lo[j], q_hi[...])
            ) - column[j].astype(F32) * sums

    exchange_sum(me, wire, grad_send, grad_recv, summed, candidates)

    query_grad = jnp.concatenate(
        [
            summed[:, 128 * j : 128 * j + 128] - queries[:, 128 * j : 128 * j + 128] * rest_col
            for j in range(4)
        ],
        axis=1,
    ).astype(BF)

    def row_part(chunk):
        pick = jnp.where(row_ids + 128 * chunk == head_row, 1.0, 0.0).astype(BF)
        return rows[chunk] + dot(pick, query_grad)

    order = (1, 3, 2, 0)
    core_copies = {}
    for at, d in enumerate(order):
        chunk = (1 - me.k) * 4 + (me.g + d) % 4
        core_send[d] = row_part(chunk).astype(BF)
        core_copies[d] = wire.put(core_send.at[d], core_recv.at[d], me.sibling())
    y_copies = []
    for d in order:
        own = row_part(me.k * 4 + (me.g + d) % 4)
        core_copies[d].wait_recv()
        total = own + core_recv[d].astype(F32)
        if d:
            y_send[d - 1] = total.astype(BF)
            y_copies.append(
                wire.put(y_send.at[d - 1], y_recv.at[d - 1], me.peer("y", (me.g + d) % 4))
            )
    for d in (1, 3, 2):
        loss_copies[d].wait_recv()
    loss_rows = []
    for d in range(4):
        row = ((me.g + d) % 4) * 2 + me.k
        loss_rows.append(wire.put(loss.at[row], loss.at[row], me.sibling()))
    for copy in y_copies:
        copy.wait_recv()
    for d in range(3):
        total = total + y_recv[d].astype(F32)
    activated = act[...]
    pre_grad = (((2.0 * scale) * total) * (1.0 - activated * activated)).astype(BF)
    pre_all[me.g] = pre_grad
    gather_pre = GatherY(me, wire, pre_all, lambda d: (me.g + 4 - d) % 4)
    agg_tiles[me.g] = dot(pre_grad, w_in[...], NT).astype(BF)
    gather_pre.neighbours()
    for d in (1, 3, 2):
        if d == 2:
            gather_pre.opposite()
        other = (me.g + 4 - d) % 4
        agg_tiles[other] = dot(pre_all[other], w_in[...], NT).astype(BF)
    for d in (1, 3, 2):
        agg_copies[d].wait_recv()
    for copy in loss_rows:
        copy.wait_recv()
    wire.drain()


def middle(partial_low, partial, self_part, w_in, query_part, query_head, true_tail, allowed):
    depth = w_in.shape[0]
    copies = 3 + 6 + 4 + 3 + 12 + 15 + 3 + 12 + 4 + 3 + 4 + 6
    tile_bf = jax.ShapeDtypeStruct((4, 128, depth), BF)
    return pl.pallas_call(
        middle_kernel,
        name="middle",
        out_shape=(
            jax.ShapeDtypeStruct((1, 128, depth), BF),
            jax.ShapeDtypeStruct((8, 1, 128), F32),
            tile_bf,
            tile_bf,
            tile_bf,
        ),
        in_specs=[VMEM_SPEC] * 8,
        out_specs=(VMEM_SPEC,) * 5,
        scratch_shapes=[
            pltpu.VMEM((3, 128, depth), BF),
            pltpu.VMEM((128, depth), F32),
            pltpu.VMEM((8, 128, depth), BF),
            pltpu.VMEM((2, 2, 128, 256), BF),
            pltpu.VMEM((2, 2, 3, 128, 256), BF),
            pltpu.VMEM((128, depth), F32),
            pltpu.VMEM((128, depth), BF),
            pltpu.VMEM((128, depth), BF),
            pltpu.VMEM((8, 128, 128), F32),
            pltpu.VMEM((16, 8, 128), F32),
            pltpu.VMEM((8, 128, 128), F32),
            pltpu.VMEM((2, 2, 128, 256), BF),
            pltpu.VMEM((2, 2, 3, 128, 256), BF),
            pltpu.VMEM((128, depth), F32),
            pltpu.VMEM((8, 128, 128), BF),
            pltpu.VMEM((8, 128, 128), BF),
            pltpu.VMEM((8, 128, depth), F32),
            pltpu.VMEM((4, 128, depth), BF),
            pltpu.VMEM((4, 128, depth), BF),
            pltpu.VMEM((3, 128, depth), BF),
            pltpu.VMEM((3, 128, depth), BF),
            pltpu.SemaphoreType.DMA((copies,)),
            pltpu.SemaphoreType.DMA((copies,)),
        ],
        compiler_params=pltpu.CompilerParams(
            collective_id=1, has_side_effects=True, vmem_limit_bytes=LIMIT
        ),
    )(partial_low, partial, self_part, w_in, query_part, query_head, true_tail, allowed)


def return_kernel(
    n_ar,
    tiles, rel_part, agg_all, pre_all, node, w_self, requests,
    node_grad, summed, w_all,
    arrived, shipped, y_recv, x_send, joined, self_grad, *rest,
):
    ar_refs = rest[:n_ar]
    send_sem, recv_sem, local_sem = rest[n_ar:]
    me = Place()
    devices = []
    for e in range(1, 8):
        devices.append(me.dev(me.g, me.x * 8 + (me.zk + e) % 8))
    for e in range(1, 8):
        other = (me.xk + e) % 8
        devices.append(me.dev(me.g, (other // 2) * 8 + me.z * 2 + other % 2))
    for d in (1, 2, 3):
        devices.append(me.peer("y", (me.g + d) % 4))
    enter(devices)
    wire = Wire(send_sem, recv_sem)
    reduce = AllReduce(me, wire, 16, STAGES_CAND, ar_refs, summed, w_all)
    steps = reduce.steps()

    def advance():
        next(steps, None)

    axes = ((0, "x"), (1, "z"))
    own_slots = (me.zk, me.xk)
    moved = {}

    rounds = ((1, 0, 128), (3, 0, 128), (2, 0, 128), (0, 0, 64), (0, 64, 64))

    def send_round(at):
        d, start, size = rounds[at]
        part = pl.ds(start, size)
        for col, axis in axes:
            place = (me.at(axis) + d) % 4
            for e in range(1, 8):
                slot = (own_slots[col] + e) % 8
                moved[at, col, e] = wire.put(
                    tiles.at[col, slot, place, part],
                    arrived.at[col, own_slots[col], place, part],
                    devices[7 * col + e - 1],
                )

    send_round(0)
    local = []
    for col in range(2):
        copy = pltpu.make_async_copy(
            tiles.at[col, own_slots[col]], arrived.at[col, own_slots[col]], local_sem.at[col]
        )
        copy.start()
        local.append(copy)
    cols = pl.ds(pl.multiple_of(me.g * 128, 128), 128)
    right = pre_all[:, :, cols].reshape(512, 128)
    for which, left in ((0, agg_all), (1, node)):
        for q in range(4):
            turned = left[:, :, 128 * q : 128 * q + 128].astype(F32).reshape(512, 128).T.astype(BF)
            reduce.part[2 * which + q // 2, 8 * (q % 2) : 8 * (q % 2) + 8, 0:16] = (
                dot(turned, right).reshape(8, 16, 128).astype(BF)
            )
    for q in range(2):
        for j in range(4):
            reduce.part[j, 8 * q : 8 * q + 8, 16:32] = (
                rel_part[128 * q : 128 * q + 128, 128 * j : 128 * j + 128]
                .reshape(8, 16, 128)
                .astype(BF)
            )
    advance()
    send_round(1)
    self_grad[...] = dot(pre_all[me.g], w_self[...], NT)
    advance()
    for copy in local:
        copy.wait()
    over_y = {}
    second = []

    def combine(d, col):
        for at in range(len(rounds)):
            if rounds[at][0] == d:
                for copy in over_y[at, col]:
                    copy.wait_recv()
        total = shipped[col, d, me.g].astype(F32)
        for m in range(3):
            total = total + y_recv[col, d, m].astype(F32)
        return total

    def send_combined(d):
        for col, axis in axes:
            x_send[col, d - 1] = combine(d, col).astype(BF)
            second.append(
                wire.put(
                    x_send.at[col, d - 1],
                    joined.at[col, d - 1],
                    me.peer(axis, (me.at(axis) + d) % 4),
                )
            )

    for at, (d, start, size) in enumerate(rounds):
        for col, axis in axes:
            place = (me.at(axis) + d) % 4
            owner = place * 8 + me.zk if col == 0 else me.x * 8 + place * 2 + me.k
            for e in range(1, 8):
                moved[at, col, e].wait_recv()
            index = [requests[8 * col + m, 0, owner] for m in range(8)]
            for part in range(size // 32):
                rows = pl.ds(start + part * 32, 32)
                values = [arrived[col, m, place, rows, :].astype(F32) for m in range(8)]
                for s in range(4):
                    total = jnp.zeros((32, 256), F32)
                    for m in range(8):
                        total = total + jnp.where(index[m] == s, values[m], 0.0)
                    shipped[col, d, s, rows, :] = total.astype(BF)
            over_y[at, col] = []
            rows = pl.ds(start, size)
            for e in (1, 3, 2):
                s = (me.g + e) % 4
                over_y[at, col].append(
                    wire.put(
                        shipped.at[col, d, s, rows],
                        y_recv.at[col, d, e - 1, rows],
                        me.peer("y", s),
                    )
                )
        advance()
        if at + 2 < len(rounds):
            send_round(at + 2)
        if at and rounds[at - 1][0]:
            send_combined(rounds[at - 1][0])
    advance()
    pair = pl.ds(2 * me.k, 2)
    last = [
        wire.put(summed.at[pair], summed.at[pair], me.sibling()),
        wire.put(w_all.at[:, pair], w_all.at[:, pair], me.sibling()),
    ]
    for copy in second:
        copy.wait_recv()
    for col in range(2):
        total = combine(0, col)
        for m in range(3):
            total = total + joined[col, m].astype(F32)
        node_grad[0, :, 256 * col : 256 * col + 256] = (
            total + self_grad[:, 256 * col : 256 * col + 256]
        )
    for copy in last:
        copy.wait_recv()
    wire.drain()


def give_back(tiles, rel_part, agg_all, pre_all, node_tiles, w_self, requests):
    depth = w_self.shape[0]
    ar = AllReduce.scratch(16, STAGES_CAND, 32)
    copies = 70 + 30 + 6 + (1 + 12 + 6 + 24) + 2
    return pl.pallas_call(
        functools.partial(return_kernel, len(ar)),
        name="give_back",
        out_shape=(
            jax.ShapeDtypeStruct((1, 128, depth), F32),
            jax.ShapeDtypeStruct((4, 16, 16, 128), BF),
            jax.ShapeDtypeStruct((4, 4, 16, 16, 128), BF),
        ),
        in_specs=[ANY_SPEC] + [VMEM_SPEC] * 5 + [SMEM_SPEC],
        out_specs=(VMEM_SPEC,) * 3,
        scratch_shapes=[
            pltpu.VMEM((2, 8, 4, 128, 256), BF),
            pltpu.VMEM((2, 4, 4, 128, 256), BF),
            pltpu.VMEM((2, 4, 3, 128, 256), BF),
            pltpu.VMEM((2, 3, 128, 256), BF),
            pltpu.VMEM((2, 3, 128, 256), BF),
            pltpu.VMEM((128, depth), F32),
            *ar,
            pltpu.SemaphoreType.DMA((copies,)),
            pltpu.SemaphoreType.DMA((copies,)),
            pltpu.SemaphoreType.DMA((2,)),
        ],
        compiler_params=pltpu.CompilerParams(
            collective_id=2, has_side_effects=True, vmem_limit_bytes=LIMIT
        ),
    )(tiles, rel_part, agg_all, pre_all, node_tiles, w_self, requests)


def finish_kernel(node_in, summed, w_all, node_grad, rel_grad, w_in_grad, w_self_grad):
    node_grad[...] = node_in[...]
    for j in range(4):
        cols = slice(128 * j, 128 * j + 128)
        whole = summed[j].astype(F32).reshape(256, 128)
        rel_grad[:, cols] = whole[: rel_grad.shape[0]]
        for q in range(2):
            rows = slice(256 * q, 256 * q + 256)
            for at, target in ((q, w_in_grad), (2 + q, w_self_grad)):
                target[rows, cols] = w_all[j, at].astype(F32).reshape(256, 128)


def finish(node_grad, summed, w_all, relations):
    depth = node_grad.shape[2]
    return pl.pallas_call(
        finish_kernel,
        name="finish",
        out_shape=(
            jax.ShapeDtypeStruct(node_grad.shape, F32),
            jax.ShapeDtypeStruct((relations, depth), F32),
            jax.ShapeDtypeStruct((depth, depth), F32),
            jax.ShapeDtypeStruct((depth, depth), F32),
        ),
        in_specs=[VMEM_SPEC] * 3,
        out_specs=(VMEM_SPEC,) * 4,
    )(node_grad, summed, w_all)


def body(
    node_emb,
    rel_emb,
    w_in,
    w_self,
    rel_score,
    mirror_blocks,
    adj_values,
    adj_source,
    adj_target,
    adj_relation,
    live_blocks,
    query_head,
    query_rel,
    allowed,
    true_tail,
):
    wanted = mirror_blocks.reshape(1, 32)
    node_tiles = node_emb.reshape(4, 128, -1)
    mirrors, requests, self_part = fetch(node_tiles, wanted, w_self)
    partial, partial_low, query_part = forward(
        adj_source, adj_target, adj_relation, live_blocks, adj_values, mirrors, rel_emb,
        query_rel, rel_score,
    )
    h, loss, agg_all, pre_all, agg_tiles = middle(
        partial_low,
        partial,
        self_part,
        w_in,
        query_part,
        query_head.reshape(1, -1),
        true_tail.reshape(1, -1),
        allowed.T,
    )
    tiles, rel_part, h_out, loss = backward(
        adj_source, adj_target, adj_relation, live_blocks, adj_values, agg_tiles, h, loss
    )
    node_grad, summed, w_all = give_back(
        tiles.reshape(2, 8, 4, 128, 256),
        rel_part,
        agg_all,
        pre_all,
        node_tiles,
        w_self,
        requests,
    )
    node_grad, rel_grad, w_in_grad, w_self_grad = finish(
        node_grad, summed, w_all, rel_emb.shape[0]
    )
    return (h_out, loss.reshape(-1), node_grad, rel_grad, w_in_grad, w_self_grad)


def solution(mesh):
    return jax.shard_map(
        body,
        mesh=mesh,
        in_specs=(
            P("cand", None, None),
            P("grp", None),
            P(),
            P(),
            P(),
            P("grp", "cand", None, None),
            P("grp", "cand", None, None, None),
            P("grp", "cand", None),
            P("grp", "cand", None),
            P("grp", "cand", None),
            P("grp", "cand"),
            P(),
            P(),
            P(),
            P(),
        ),
        out_specs=(P("cand", "grp", None), P(), P("cand", "grp", None), P("grp", None), P(), P()),
        check_vma=False,
    )
```

```python
import functools

import jax
import jax.numpy as jnp
from jax import lax
from jax.experimental import pallas as pl
from jax.experimental.pallas import tpu as pltpu
from jax.sharding import PartitionSpec as P

NEG_FILL = -1e30
MESH = pl.DeviceIdType.MESH
BF = jnp.bfloat16
F32 = jnp.float32
NN = (((1,), (0,)), ((), ()))
NT = (((1,), (1,)), ((), ()))
TN = (((0,), (0,)), ((), ()))
VMEM_SPEC = pl.BlockSpec(memory_space=pltpu.VMEM)
SMEM_SPEC = pl.BlockSpec(memory_space=pltpu.SMEM)
ANY_SPEC = pl.BlockSpec(memory_space=pl.ANY)
MIB = 1024 * 1024
STAGES_CAND = (("z", "x"), ("x", "z"))


def dot(a, b, dims=NN):
    return lax.dot_general(a, b, dims, preferred_element_type=F32)


class Place:
    def __init__(self):
        self.g = lax.axis_index("grp")
        self.c = lax.axis_index("cand")
        self.x = self.c // 8
        self.zk = self.c % 8
        self.z = self.zk // 2
        self.k = self.c % 2
        self.xk = self.x * 2 + self.k

    def dev(self, g, c):
        return {"grp": g, "cand": c}

    def at(self, axis):
        return {"x": self.x, "z": self.z, "y": self.g}[axis]

    def peer(self, axis, other):
        if axis == "y":
            return self.dev(other, self.c)
        if axis == "x":
            return self.dev(self.g, other * 8 + self.zk)
        return self.dev(self.g, self.x * 8 + other * 2 + self.k)

    def sibling(self):
        return self.dev(self.g, self.c + 1 - 2 * self.k)


def enter(devices):
    barrier = pltpu.get_barrier_semaphore()
    for device in devices:
        pl.semaphore_signal(barrier, inc=1, device_id=device, device_id_type=MESH)
    pl.semaphore_wait(barrier, len(devices))


class Wire:
    def __init__(self, send_sem, recv_sem):
        self.send_sem, self.recv_sem, self.count, self.sent = send_sem, recv_sem, 0, []

    def put(self, src, dst, device):
        at = self.count
        self.count += 1
        copy = pltpu.make_async_remote_copy(
            src_ref=src,
            dst_ref=dst,
            send_sem=self.send_sem.at[at],
            recv_sem=self.recv_sem.at[at],
            device_id=device,
            device_id_type=MESH,
        )
        copy.start()
        self.sent.append(copy)
        return copy

    def drain(self):
        for copy in self.sent:
            copy.wait_send()


def add_up(read_terms, write, count):
    chunk = min(count, 8)

    def one(i, carry):
        at = pl.ds(i * chunk, chunk)
        terms = read_terms(at)
        total = terms[0].astype(F32)
        for term in terms[1:]:
            total = total + term.astype(F32)
        write(at, total)
        return carry

    if count == chunk:
        one(0, 0)
    else:
        lax.fori_loop(0, count // chunk, one, 0)


class AllReduce:
    @staticmethod
    def scratch(shards, stages, height):
        depth = len(stages[0])
        shapes = [
            pltpu.VMEM((4, shards, height, 128), BF),
            pltpu.VMEM((2, shards, height, 128), BF),
        ]
        for level in range(depth):
            shapes.append(pltpu.VMEM((2, shards // 4**level, height, 128), BF))
            shapes.append(pltpu.VMEM((2, 3, shards // 4 ** (level + 1), height, 128), BF))
        return shapes

    def __init__(self, me, wire, shards, stages, refs, summed, w_all):
        self.me, self.wire, self.shards, self.stages = me, wire, shards, stages
        self.part, self.rcore = refs[:2]
        self.summed, self.w_all = summed, w_all
        depth = len(stages[0])
        self.acc = refs[2 : 2 + 2 * depth : 2]
        self.recv = refs[3 : 3 + 2 * depth : 2]
        self.sizes = [shards // 4 ** (i + 1) for i in range(depth)]

    def steps(self):
        me, wire = self.me, self.wire
        mine = 2 * me.k
        copy = wire.put(self.part.at[pl.ds(2 - mine, 2)], self.rcore, me.sibling())
        yield
        copy.wait_recv()
        for col in range(2):

            def write(at, value, col=col):
                self.acc[0][col, at] = value.astype(BF)

            add_up(
                lambda at, col=col: (self.part[mine + col, at], self.rcore[col, at]),
                write,
                self.shards,
            )
        offsets = [0, 0]
        history = []
        depth = len(self.sizes)
        for level in range(depth):
            size = self.sizes[level]
            copies = []
            for d in (1, 3, 2):
                for col in range(2):
                    axis = self.stages[col][level]
                    other = (me.at(axis) + d) % 4
                    copies.append(
                        wire.put(
                            self.acc[level].at[col, pl.ds(other * size, size)],
                            self.recv[level].at[col, d - 1],
                            me.peer(axis, other),
                        )
                    )
            yield
            for copy in copies:
                copy.wait_recv()
            for col in range(2):
                own = me.at(self.stages[col][level]) * size
                offsets[col] = offsets[col] + own

                def terms(at, col=col, own=own, level=level):
                    base = pl.ds(own + at.start, at.size)
                    return [self.acc[level][col, base]] + [
                        self.recv[level][col, d, at] for d in range(3)
                    ]

                def write(at, value, col=col, level=level):
                    if level + 1 < depth:
                        self.acc[level + 1][col, at] = value.astype(BF)
                    else:
                        final = value.astype(BF)
                        place = pl.ds(offsets[col] + at.start, at.size)
                        self.w_all[me.g, mine + col, place] = final[:, 0:16]
                        self.summed[mine + col, place] = final[:, 16:32]

                add_up(terms, write, size)
            history.append(tuple(offsets))
        copies = []
        for d in (1, 3, 2):
            for col in range(2):
                place = self.w_all.at[me.g, mine + col, pl.ds(offsets[col], self.sizes[-1])]
                copies.append(wire.put(place, place, me.peer("y", (me.g + d) % 4)))
        yield
        for copy in copies:
            copy.wait_recv()
        for level in reversed(range(depth)):
            size = self.sizes[level]
            copies = []
            for d in (1, 3, 2):
                for col in range(2):
                    axis = self.stages[col][level]
                    other = (me.at(axis) + d) % 4
                    shards = pl.ds(history[level][col], size)
                    for place in (
                        self.summed.at[mine + col, shards],
                        self.w_all.at[:, mine + col, shards],
                    ):
                        copies.append(wire.put(place, place, me.peer(axis, other)))
            yield
            for copy in copies:
                copy.wait_recv()


def fetch_kernel(
    node, wanted_v, w_self,
    mirrors, requests, self_part,
    wanted_row, request_s, staged, send_sem, recv_sem, local_sem, *gathered,
):
    me = Place()
    devices = []
    for e in range(1, 8):
        devices.append(me.dev(me.g, me.x * 8 + (me.zk + e) % 8))
    for e in range(1, 8):
        other = (me.xk + e) % 8
        devices.append(me.dev(me.g, (other // 2) * 8 + me.z * 2 + other % 2))
    for d in (1, 2, 3):
        devices.append(me.peer("y", (me.g + d) % 4))
    enter(devices)
    wire = Wire(send_sem, recv_sem)
    wanted_row[...] = jnp.zeros_like(wanted_row)
    wanted_row[:, 0:32] = wanted_v[...]
    halves = (pl.ds(0, 256), pl.ds(256, 256))
    first = {}
    for d in (1, 3, 2):
        for col, axis in ((0, "x"), (1, "z")):
            other = (me.at(axis) + d) % 4
            first[col, d] = wire.put(
                node.at[me.g, :, halves[col]],
                gathered[3 * col + d - 1].at[me.g],
                me.peer(axis, other),
            )
    asks = []
    for e in range(1, 8):
        for col in range(2):
            asks.append(
                wire.put(
                    wanted_row,
                    requests.at[8 * col + (me.zk if col == 0 else me.xk)],
                    devices[7 * col + e - 1],
                )
            )
    requests[me.zk] = wanted_row[...]
    requests[8 + me.xk] = wanted_row[...]
    spread = {}

    def pass_on(d):
        for col in range(2):
            first[col, d].wait_recv()
            place = gathered[3 * col + d - 1].at[me.g]
            spread[col, d] = [
                wire.put(place, place, me.peer("y", (me.g + e) % 4)) for e in (1, 3, 2)
            ]

    pass_on(1)
    for copy in asks:
        copy.wait_recv()
    local = pltpu.make_async_copy(requests, request_s, local_sem)
    local.start()
    local.wait()
    moved = []
    for d in (0, 1, 3, 2):
        for col, axis in ((0, "x"), (1, "z")):
            if d:
                for copy in spread[col, d]:
                    copy.wait_recv()
            origin = (me.at(axis) + 4 - d) % 4
            own_slot = me.zk if col == 0 else me.xk
            owner = origin * 8 + me.zk if col == 0 else me.x * 8 + origin * 2 + me.k
            for e in range(8):
                slot = (own_slot + e) % 8
                index = request_s[8 * col + slot, 0, owner]
                if d:
                    tile = gathered[3 * col + d - 1][index]
                else:
                    tile = node[index, :, 256 * col : 256 * col + 256]
                if e == 0:
                    mirrors[col, own_slot, origin] = tile
                else:
                    staged[col, e - 1, d] = tile
                    moved.append(
                        wire.put(
                            staged.at[col, e - 1, d],
                            mirrors.at[col, own_slot, origin],
                            devices[7 * col + e - 1],
                        )
                    )
        if d == 0:
            pass_on(3)
            pass_on(2)
    self_part[...] = dot(node[me.g], w_self[...])
    for copy in moved:
        copy.wait_recv()
    wire.drain()


def fetch(node_tiles, wanted, w_self):
    depth = node_tiles.shape[2]
    copies = 6 + 14 + 56 + 18
    return pl.pallas_call(
        fetch_kernel,
        name="fetch",
        cost_estimate=pl.CostEstimate(flops=67108864, bytes_accessed=100000000, transcendentals=0),
        out_shape=(
            jax.ShapeDtypeStruct((2, 8, 4, 128, 256), BF),
            jax.ShapeDtypeStruct((16, 1, 128), jnp.int32),
            jax.ShapeDtypeStruct((128, depth), F32),
        ),
        in_specs=[VMEM_SPEC] * 3,
        out_specs=(VMEM_SPEC,) * 3,
        scratch_shapes=[
            pltpu.VMEM((1, 128), jnp.int32),
            pltpu.SMEM((16, 1, 128), jnp.int32),
            pltpu.VMEM((2, 7, 4, 128, 256), BF),
            pltpu.SemaphoreType.DMA((copies,)),
            pltpu.SemaphoreType.DMA((copies,)),
            pltpu.SemaphoreType.DMA,
            *[pltpu.VMEM((4, 128, 256), BF)] * 6,
        ],
        compiler_params=pltpu.CompilerParams(
            collective_id=0, has_side_effects=True, vmem_limit_bytes=16 * MIB
        ),
    )(node_tiles, wanted, w_self)


GROUP = 24


def slots_of(source):
    x, zk = source // 8, source % 8
    z, k = zk // 2, zk % 2
    return zk * 4 + x, (x * 2 + k) * 4 + z


def forward_kernel(
    source, target, relation, live, values, mirrors, rel_emb, query_rel, rel_score,
    out, out_low, query_part,
):
    step = pl.program_id(0)
    first = (lax.axis_index("grp") * 2 + lax.axis_index("cand") % 2) * 128

    for j in range(16):
        row = step * 16 + j
        query_part[pl.ds(row, 1), :] = rel_score[pl.ds(query_rel[first + row], 1), :]

    @pl.when(step == 0)
    def _():
        out[...] = jnp.zeros_like(out)

    count = live[0, 0]

    @pl.when(step * GROUP < count)
    def _():
        for j in range(GROUP):
            b = step * GROUP + j
            slots = slots_of(source[0, 0, b])
            t = target[0, 0, b]
            block = values[0, 0, j]
            block = jnp.where(b < count, block, jnp.zeros_like(block))
            row = rel_emb[pl.ds(relation[0, 0, b], 1), :]
            for col in range(2):
                part = slice(256 * col, 256 * col + 256)
                composed = (mirrors[col, slots[col]].astype(F32) - row[:, part]).astype(BF)
                out[t, :, part] += dot(block, composed)

    @pl.when(step == pl.num_programs(0) - 1)
    def _():
        for t in range(4):
            out_low[t] = out[t].astype(BF)


def adjacency_specs(blocks):
    return [SMEM_SPEC] * 4 + [
        pl.BlockSpec((1, 1, GROUP, 128, 128), lambda i: (0, 0, i, 0, 0)),
    ]


def forward(
    adj_source, adj_target, adj_relation, live_blocks, adj_values, mirrors, rel_emb, query_rel, rel_score
):
    blocks = adj_values.shape[2]
    depth = rel_score.shape[1]
    return pl.pallas_call(
        forward_kernel,
        name="forward_blocks",
        cost_estimate=pl.CostEstimate(flops=3221225472, bytes_accessed=30000000, transcendentals=0),
        grid=(blocks // GROUP,),
        out_shape=(
            jax.ShapeDtypeStruct((4, 128, depth), F32),
            jax.ShapeDtypeStruct((4, 128, depth), BF),
            jax.ShapeDtypeStruct((128, depth), F32),
        ),
        in_specs=adjacency_specs(blocks) + [VMEM_SPEC] * 2 + [SMEM_SPEC, VMEM_SPEC],
        out_specs=(VMEM_SPEC,) * 3,
        compiler_params=pltpu.CompilerParams(vmem_limit_bytes=16 * MIB),
    )(
        adj_source, adj_target, adj_relation, live_blocks, adj_values,
        mirrors.reshape(2, 32, 128, 256), rel_emb, query_rel, rel_score,
    )


def backward_kernel(
    source, target, relation, live, values, agg, h_in, loss_in,
    tiles_out, rel_out, h_out, loss_out, tiles,
):
    step = pl.program_id(0)

    @pl.when(step == 0)
    def _():
        def clear(i, carry):
            for col in range(2):
                tiles[col, i] = jnp.zeros((128, 256), F32)
            return carry

        lax.fori_loop(0, 32, clear, 0)
        rel_out[...] = jnp.zeros_like(rel_out)
        h_out[...] = h_in[...]
        for j in range(8):
            loss_out[j : j + 1, :] = loss_in[j]

    count = live[0, 0]

    @pl.when(step * GROUP < count)
    def _():
        for j in range(GROUP):
            b = step * GROUP + j
            slots = slots_of(source[0, 0, b])
            r = pl.ds(relation[0, 0, b], 1)
            block = values[0, 0, j]
            block = jnp.where(b < count, block, jnp.zeros_like(block))
            grad = dot(block, agg[target[0, 0, b]], TN)
            rel_out[r, :] -= jnp.sum(grad, axis=0, keepdims=True)
            for col in range(2):
                tiles[col, slots[col]] += grad[:, 256 * col : 256 * col + 256]

    @pl.when(step == pl.num_programs(0) - 1)
    def _():
        def store(i, carry):
            for col in range(2):
                tiles_out[col, i] = tiles[col, i].astype(BF)
            return carry

        lax.fori_loop(0, 32, store, 0)


def backward(adj_source, adj_target, adj_relation, live_blocks, adj_values, agg_tiles, h, loss):
    blocks = adj_values.shape[2]
    return pl.pallas_call(
        backward_kernel,
        name="backward_blocks",
        cost_estimate=pl.CostEstimate(flops=3221225472, bytes_accessed=30000000, transcendentals=0),
        grid=(blocks // GROUP,),
        out_shape=(
            jax.ShapeDtypeStruct((2, 32, 128, 256), BF),
            jax.ShapeDtypeStruct((256, 512), F32),
            jax.ShapeDtypeStruct(h.shape, h.dtype),
            jax.ShapeDtypeStruct((8, 128), F32),
        ),
        in_specs=adjacency_specs(blocks) + [VMEM_SPEC] * 3,
        out_specs=(VMEM_SPEC,) * 4,
        scratch_shapes=[pltpu.VMEM((2, 32, 128, 256), F32)],
        compiler_params=pltpu.CompilerParams(vmem_limit_bytes=24 * MIB),
    )(adj_source, adj_target, adj_relation, live_blocks, adj_values, agg_tiles, h, loss)


def exchange_sum(me, wire, send, recv, out, during=None):
    for level in range(2):
        copies = []
        for d in (1, 3, 2):
            for col in range(2):
                axis = STAGES_CAND[col][level]
                other = (me.at(axis) + d) % 4
                copies.append(
                    wire.put(
                        send.at[level, col], recv.at[level, col, d - 1], me.peer(axis, other)
                    )
                )
        if level == 0 and during is not None:
            during()
        for copy in copies:
            copy.wait_recv()
        for col in range(2):
            total = send[level, col].astype(F32)
            for d in range(3):
                total = total + recv[level, col, d].astype(F32)
            if level == 0:
                send[1, col] = total.astype(BF)
            else:
                out[:, 256 * col : 256 * col + 256] = total


class GatherY:
    def __init__(self, me, wire, ref, slot):
        self.me, self.wire, self.ref, self.slot = me, wire, ref, slot
        self.near = (me.peer("y", (me.g + 1) % 4), me.peer("y", (me.g + 3) % 4))
        self.first = [self.put(0, 0, 0), self.put(0, 1, 1)]
        self.second = [self.put(0, 1, 0), self.put(0, 0, 1)]

    def put(self, d, half, way):
        place = self.ref.at[self.slot(d), pl.ds(64 * half, 64)]
        return self.wire.put(place, place, self.near[way])

    def neighbours(self):
        self.first[0].wait_recv()
        far = [self.put(1, 0, 0)]
        self.first[1].wait_recv()
        far.append(self.put(3, 1, 1))
        for copy in self.second:
            copy.wait_recv()
        self.far = far

    def opposite(self):
        for copy in self.far:
            copy.wait_recv()


def middle_kernel(
    partial_low, partial, self_part, w_in, query_part, query_head, true_tail, allowed,
    h_out, loss, agg_all, pre_all, agg_tiles,
    share_recv, act, column, head_send, head_recv, queries, q_hi, q_lo, scores, stats,
    h_sq, grad_send, grad_recv, summed, g_hi, g_lo, rows, core_send, core_recv, y_send, y_recv,
    send_sem, recv_sem,
):
    me = Place()
    plane = []
    for dx, dz in sorted(
        [(i, j) for i in range(4) for j in range(4) if i or j],
        key=lambda p: -(min(p[0], 4 - p[0]) + min(p[1], 4 - p[1])),
    ):
        plane.append(
            me.dev(me.g, ((me.x + dx) % 4) * 8 + ((me.z + dz) % 4) * 2 + me.k)
        )
    enter(
        [me.sibling()] + [me.peer("y", (me.g + d) % 4) for d in (1, 2, 3)] + plane
    )
    wire = Wire(send_sem, recv_sem)
    count = true_tail.shape[1]
    scale = 512 ** (-0.5)
    group = me.g * 2 + me.k
    lanes = pl.ds(pl.multiple_of(group * 128, 128), 128)
    first_chip = me.x * 8 + me.z * 2
    base = first_chip * 512

    def to_y(ref, at, order=(1, 3, 2)):
        copies = {}
        for d in order:
            copies[d] = wire.put(ref.at[at], ref.at[at], me.peer("y", (me.g + d) % 4))
        return copies

    copies = []
    for d in (1, 3, 2):
        other = (me.g + d) % 4
        copies.append(wire.put(partial_low.at[other], share_recv.at[d - 1], me.peer("y", other)))
    for copy in copies:
        copy.wait_recv()
    total = partial[me.g]
    for d in range(3):
        total = total + share_recv[d].astype(F32)
    agg = total.astype(BF)
    activated = jnp.tanh(dot(agg, w_in[...]) + self_part[...])
    h = activated.astype(BF)
    own_chunk = me.k * 4 + me.g
    column[own_chunk] = h
    gather_h = GatherY(me, wire, column, lambda d: me.k * 4 + (me.g + 4 - d) % 4)
    from_sibling = [wire.put(column.at[own_chunk], column.at[own_chunk], me.sibling())]
    h_out[0] = h
    act[...] = activated
    agg_all[me.g] = agg
    gather_h.neighbours()
    for d in (1, 3, 2):
        if d == 2:
            gather_h.opposite()
        chunk = me.k * 4 + (me.g + 4 - d) % 4
        from_sibling.append(wire.put(column.at[chunk], column.at[chunk], me.sibling()))

    agg_copies = to_y(agg_all, me.g)

    head_row = jnp.broadcast_to(query_head[:, lanes] - base, (128, 128))
    head_col = head_row.astype(F32).T
    lane_ids = lax.broadcasted_iota(jnp.int32, (128, 128), 1).astype(F32)
    row_ids = lax.broadcasted_iota(jnp.int32, (128, 128), 0)
    for copy in from_sibling:
        copy.wait_recv()
    part = jnp.zeros((128, 512), F32)
    for j in range(8):
        pick = jnp.where(head_col == lane_ids + 128.0 * j, 1.0, 0.0).astype(BF)
        part = part + dot(pick, column[j])
    for col in range(2):
        head_send[0, col] = part[:, 256 * col : 256 * col + 256].astype(BF)

    def squares():
        for j in range(8):
            h32 = column[j].astype(F32)
            h_sq[j] = jnp.broadcast_to(jnp.sum(h32 * h32, axis=1, keepdims=True), (128, 128))

    exchange_sum(me, wire, head_send, head_recv, summed, squares)

    q = summed[...] + query_part[...]
    queries[...] = q
    high = q.astype(BF)
    q_hi[...] = high
    q_lo[...] = (q - high.astype(F32)).astype(BF)
    square = jnp.zeros((128, 128), F32)
    for j in range(4):
        piece = q[:, 128 * j : 128 * j + 128]
        square = square + piece * piece
    q_sq = jnp.sum(square.T, axis=0, keepdims=True)
    tail_row = jnp.broadcast_to(true_tail[:, lanes] - base, (128, 128))
    kinds = allowed[:, lanes]

    def allowed_row(j):
        hit = jnp.where(kinds == first_chip * 4 + j, 1.0, 0.0)
        return jnp.max(hit, axis=0, keepdims=True)

    masks = [jnp.broadcast_to(allowed_row(j), (128, 128)) > 0.5 for j in range(8)]
    tops, truths = [], []
    for j in range(8):
        cross = dot(column[j], q_hi[...], NT) + dot(column[j], q_lo[...], NT)
        score = -scale * (q_sq + h_sq[j] - 2.0 * cross)
        scores[j] = score
        tops.append(jnp.max(jnp.where(masks[j], score, NEG_FILL), axis=0, keepdims=True))
        truths.append(
            jnp.sum(
                jnp.where(row_ids + 128 * j == tail_row, score, 0.0), axis=0, keepdims=True
            )
        )
    top = functools.reduce(jnp.maximum, tops)
    weight = jnp.zeros((1, 128), F32)
    for j in range(8):
        weight = weight + jnp.sum(
            jnp.exp(jnp.where(masks[j], scores[j] - top, NEG_FILL)), axis=0, keepdims=True
        )
    stats[0, 0:1, :] = top
    stats[0, 1:2, :] = weight
    stats[0, 2:3, :] = functools.reduce(lambda a, b: a + b, truths)

    copies = [wire.put(stats.at[0], stats.at[e + 1], plane[e]) for e in range(15)]
    for copy in copies:
        copy.wait_recv()
    members = [stats[m] for m in range(16)]
    tops = [m[0:1, :] for m in members]
    top = functools.reduce(jnp.maximum, tops)
    weight = jnp.zeros((1, 128), F32)
    truth = jnp.zeros((1, 128), F32)
    for m in range(16):
        weight = weight + members[m][1:2, :] * jnp.exp(tops[m] - top)
        truth = truth + members[m][2:3, :]
    log_norm = top + jnp.log(weight)
    loss[group] = log_norm - truth
    loss_copies = to_y(loss, group)
    rest_sum = (weight * jnp.exp(top - log_norm) - 1.0) / count
    rest_col = jnp.broadcast_to(rest_sum, (128, 128)).T

    part = jnp.zeros((128, 512), F32)
    for j in range(8):
        prob = jnp.exp(jnp.where(masks[j], scores[j] - log_norm, NEG_FILL))
        tail = jnp.where(row_ids + 128 * j == tail_row, 1.0, 0.0)
        grad = (prob - tail) / count
        scores[j] = grad
        high = grad.astype(BF)
        g_hi[j] = high
        g_lo[j] = (grad - high.astype(F32)).astype(BF)
        flipped = grad.T
        high = flipped.astype(BF)
        low = (flipped - high.astype(F32)).astype(BF)
        part = part + (dot(high, column[j]) + dot(low, column[j]))
    for col in range(2):
        grad_send[0, col] = part[:, 256 * col : 256 * col + 256].astype(BF)

    def candidates():
        for j in range(8):
            sums = jnp.sum(scores[j], axis=1, keepdims=True)
            rows[j] = (
                dot(g_hi[j], q_hi[...]) + dot(g_hi[j], q_lo[...]) + dot(g_lo[j], q_hi[...])
            ) - column[j].astype(F32) * sums

    exchange_sum(me, wire, grad_send, grad_recv, summed, candidates)

    query_grad = jnp.concatenate(
        [
            summed[:, 128 * j : 128 * j + 128] - queries[:, 128 * j : 128 * j + 128] * rest_col
            for j in range(4)
        ],
        axis=1,
    ).astype(BF)

    def row_part(chunk):
        pick = jnp.where(row_ids + 128 * chunk == head_row, 1.0, 0.0).astype(BF)
        return rows[chunk] + dot(pick, query_grad)

    order = (1, 3, 2, 0)
    core_copies = {}
    for at, d in enumerate(order):
        chunk = (1 - me.k) * 4 + (me.g + d) % 4
        core_send[d] = row_part(chunk).astype(BF)
        core_copies[d] = wire.put(core_send.at[d], core_recv.at[d], me.sibling())
    y_copies = []
    for d in order:
        own = row_part(me.k * 4 + (me.g + d) % 4)
        core_copies[d].wait_recv()
        total = own + core_recv[d].astype(F32)
        if d:
            y_send[d - 1] = total.astype(BF)
            y_copies.append(
                wire.put(y_send.at[d - 1], y_recv.at[d - 1], me.peer("y", (me.g + d) % 4))
            )
    for d in (1, 3, 2):
        loss_copies[d].wait_recv()
    loss_rows = []
    for d in range(4):
        row = ((me.g + d) % 4) * 2 + me.k
        loss_rows.append(wire.put(loss.at[row], loss.at[row], me.sibling()))
    for copy in y_copies:
        copy.wait_recv()
    for d in range(3):
        total = total + y_recv[d].astype(F32)
    activated = act[...]
    pre_grad = (((2.0 * scale) * total) * (1.0 - activated * activated)).astype(BF)
    pre_all[me.g] = pre_grad
    gather_pre = GatherY(me, wire, pre_all, lambda d: (me.g + 4 - d) % 4)
    agg_tiles[me.g] = dot(pre_grad, w_in[...], NT).astype(BF)
    gather_pre.neighbours()
    for d in (1, 3, 2):
        if d == 2:
            gather_pre.opposite()
        other = (me.g + 4 - d) % 4
        agg_tiles[other] = dot(pre_all[other], w_in[...], NT).astype(BF)
    for d in (1, 3, 2):
        agg_copies[d].wait_recv()
    for copy in loss_rows:
        copy.wait_recv()
    wire.drain()


def middle(partial_low, partial, self_part, w_in, query_part, query_head, true_tail, allowed):
    depth = w_in.shape[0]
    copies = 3 + 6 + 4 + 3 + 12 + 15 + 3 + 12 + 4 + 3 + 4 + 6
    tile_bf = jax.ShapeDtypeStruct((4, 128, depth), BF)
    return pl.pallas_call(
        middle_kernel,
        name="middle",
        cost_estimate=pl.CostEstimate(flops=2000000000, bytes_accessed=150000000, transcendentals=0),
        out_shape=(
            jax.ShapeDtypeStruct((1, 128, depth), BF),
            jax.ShapeDtypeStruct((8, 1, 128), F32),
            tile_bf,
            tile_bf,
            tile_bf,
        ),
        in_specs=[VMEM_SPEC] * 8,
        out_specs=(VMEM_SPEC,) * 5,
        scratch_shapes=[
            pltpu.VMEM((3, 128, depth), BF),
            pltpu.VMEM((128, depth), F32),
            pltpu.VMEM((8, 128, depth), BF),
            pltpu.VMEM((2, 2, 128, 256), BF),
            pltpu.VMEM((2, 2, 3, 128, 256), BF),
            pltpu.VMEM((128, depth), F32),
            pltpu.VMEM((128, depth), BF),
            pltpu.VMEM((128, depth), BF),
            pltpu.VMEM((8, 128, 128), F32),
            pltpu.VMEM((16, 8, 128), F32),
            pltpu.VMEM((8, 128, 128), F32),
            pltpu.VMEM((2, 2, 128, 256), BF),
            pltpu.VMEM((2, 2, 3, 128, 256), BF),
            pltpu.VMEM((128, depth), F32),
            pltpu.VMEM((8, 128, 128), BF),
            pltpu.VMEM((8, 128, 128), BF),
            pltpu.VMEM((8, 128, depth), F32),
            pltpu.VMEM((4, 128, depth), BF),
            pltpu.VMEM((4, 128, depth), BF),
            pltpu.VMEM((3, 128, depth), BF),
            pltpu.VMEM((3, 128, depth), BF),
            pltpu.SemaphoreType.DMA((copies,)),
            pltpu.SemaphoreType.DMA((copies,)),
        ],
        compiler_params=pltpu.CompilerParams(
            collective_id=1, has_side_effects=True, vmem_limit_bytes=22 * MIB
        ),
    )(partial_low, partial, self_part, w_in, query_part, query_head, true_tail, allowed)


def return_kernel(
    n_ar,
    tiles, rel_part, agg_all, pre_all, node, w_self, requests,
    node_grad, summed, w_all,
    arrived, shipped, y_recv, x_send, joined, self_grad, *rest,
):
    ar_refs = rest[:n_ar]
    send_sem, recv_sem, local_sem = rest[n_ar:]
    me = Place()
    devices = []
    for e in range(1, 8):
        devices.append(me.dev(me.g, me.x * 8 + (me.zk + e) % 8))
    for e in range(1, 8):
        other = (me.xk + e) % 8
        devices.append(me.dev(me.g, (other // 2) * 8 + me.z * 2 + other % 2))
    for d in (1, 2, 3):
        devices.append(me.peer("y", (me.g + d) % 4))
    enter(devices)
    wire = Wire(send_sem, recv_sem)
    reduce = AllReduce(me, wire, 16, STAGES_CAND, ar_refs, summed, w_all)
    steps = reduce.steps()

    def advance():
        next(steps, None)

    axes = ((0, "x"), (1, "z"))
    own_slots = (me.zk, me.xk)
    moved = {}

    rounds = ((1, 0, 128), (3, 0, 128), (2, 0, 128), (0, 0, 64), (0, 64, 64))

    def send_round(at):
        d, start, size = rounds[at]
        part = pl.ds(start, size)
        for col, axis in axes:
            place = (me.at(axis) + d) % 4
            for e in range(1, 8):
                slot = (own_slots[col] + e) % 8
                moved[at, col, e] = wire.put(
                    tiles.at[col, slot, place, part],
                    arrived.at[col, own_slots[col], place, part],
                    devices[7 * col + e - 1],
                )

    send_round(0)
    local = []
    for col in range(2):
        copy = pltpu.make_async_copy(
            tiles.at[col, own_slots[col]], arrived.at[col, own_slots[col]], local_sem.at[col]
        )
        copy.start()
        local.append(copy)
    cols = pl.ds(pl.multiple_of(me.g * 128, 128), 128)
    right = pre_all[:, :, cols].reshape(512, 128)
    for which, left in ((0, agg_all), (1, node)):
        for q in range(4):
            turned = left[:, :, 128 * q : 128 * q + 128].astype(F32).reshape(512, 128).T.astype(BF)
            reduce.part[2 * which + q // 2, 8 * (q % 2) : 8 * (q % 2) + 8, 0:16] = (
                dot(turned, right).reshape(8, 16, 128).astype(BF)
            )
    for q in range(2):
        for j in range(4):
            reduce.part[j, 8 * q : 8 * q + 8, 16:32] = (
                rel_part[128 * q : 128 * q + 128, 128 * j : 128 * j + 128]
                .reshape(8, 16, 128)
                .astype(BF)
            )
    advance()
    send_round(1)
    self_grad[...] = dot(pre_all[me.g], w_self[...], NT)
    advance()
    for copy in local:
        copy.wait()
    over_y = {}
    second = []

    def combine(d, col):
        for at in range(len(rounds)):
            if rounds[at][0] == d:
                for copy in over_y[at, col]:
                    copy.wait_recv()
        total = shipped[col, d, me.g].astype(F32)
        for m in range(3):
            total = total + y_recv[col, d, m].astype(F32)
        return total

    def send_combined(d):
        for col, axis in axes:
            x_send[col, d - 1] = combine(d, col).astype(BF)
            second.append(
                wire.put(
                    x_send.at[col, d - 1],
                    joined.at[col, d - 1],
                    me.peer(axis, (me.at(axis) + d) % 4),
                )
            )

    for at, (d, start, size) in enumerate(rounds):
        for col, axis in axes:
            place = (me.at(axis) + d) % 4
            owner = place * 8 + me.zk if col == 0 else me.x * 8 + place * 2 + me.k
            for e in range(1, 8):
                moved[at, col, e].wait_recv()
            index = [requests[8 * col + m, 0, owner] for m in range(8)]
            for part in range(size // 32):
                rows = pl.ds(start + part * 32, 32)
                values = [arrived[col, m, place, rows, :].astype(F32) for m in range(8)]
                for s in range(4):
                    total = jnp.zeros((32, 256), F32)
                    for m in range(8):
                        total = total + jnp.where(index[m] == s, values[m], 0.0)
                    shipped[col, d, s, rows, :] = total.astype(BF)
            over_y[at, col] = []
            rows = pl.ds(start, size)
            for e in (1, 3, 2):
                s = (me.g + e) % 4
                over_y[at, col].append(
                    wire.put(
                        shipped.at[col, d, s, rows],
                        y_recv.at[col, d, e - 1, rows],
                        me.peer("y", s),
                    )
                )
        advance()
        if at + 2 < len(rounds):
            send_round(at + 2)
        if at and rounds[at - 1][0]:
            send_combined(rounds[at - 1][0])
    advance()
    pair = pl.ds(2 * me.k, 2)
    last = [
        wire.put(summed.at[pair], summed.at[pair], me.sibling()),
        wire.put(w_all.at[:, pair], w_all.at[:, pair], me.sibling()),
    ]
    for copy in second:
        copy.wait_recv()
    for col in range(2):
        total = combine(0, col)
        for m in range(3):
            total = total + joined[col, m].astype(F32)
        node_grad[0, :, 256 * col : 256 * col + 256] = (
            total + self_grad[:, 256 * col : 256 * col + 256]
        )
    for copy in last:
        copy.wait_recv()
    wire.drain()


def give_back(tiles, rel_part, agg_all, pre_all, node_tiles, w_self, requests):
    depth = w_self.shape[0]
    ar = AllReduce.scratch(16, STAGES_CAND, 32)
    copies = 70 + 30 + 6 + (1 + 12 + 6 + 24) + 2
    return pl.pallas_call(
        functools.partial(return_kernel, len(ar)),
        name="give_back",
        cost_estimate=pl.CostEstimate(flops=1000000000, bytes_accessed=120000000, transcendentals=0),
        out_shape=(
            jax.ShapeDtypeStruct((1, 128, depth), F32),
            jax.ShapeDtypeStruct((4, 16, 16, 128), BF),
            jax.ShapeDtypeStruct((4, 4, 16, 16, 128), BF),
        ),
        in_specs=[ANY_SPEC] + [VMEM_SPEC] * 5 + [SMEM_SPEC],
        out_specs=(VMEM_SPEC,) * 3,
        scratch_shapes=[
            pltpu.VMEM((2, 8, 4, 128, 256), BF),
            pltpu.VMEM((2, 4, 4, 128, 256), BF),
            pltpu.VMEM((2, 4, 3, 128, 256), BF),
            pltpu.VMEM((2, 3, 128, 256), BF),
            pltpu.VMEM((2, 3, 128, 256), BF),
            pltpu.VMEM((128, depth), F32),
            *ar,
            pltpu.SemaphoreType.DMA((copies,)),
            pltpu.SemaphoreType.DMA((copies,)),
            pltpu.SemaphoreType.DMA((2,)),
        ],
        compiler_params=pltpu.CompilerParams(
            collective_id=2, has_side_effects=True, vmem_limit_bytes=20 * MIB
        ),
    )(tiles, rel_part, agg_all, pre_all, node_tiles, w_self, requests)


def finish_kernel(node_in, summed, w_all, node_grad, rel_grad, w_in_grad, w_self_grad):
    node_grad[...] = node_in[...]
    whole = summed[0].astype(F32).reshape(256, 128)
    rel_grad[...] = whole[: rel_grad.shape[0]]
    for q in range(2):
        rows = slice(256 * q, 256 * q + 256)
        for at, target in ((q, w_in_grad), (2 + q, w_self_grad)):
            target[rows, :] = w_all[0, at].astype(F32).reshape(256, 128)


def finish(node_grad, summed, w_all, relations):
    depth = node_grad.shape[2]
    tile = pl.BlockSpec((1, 128, 128), lambda j: (0, 0, j))
    whole = pl.BlockSpec((depth, 128), lambda j: (0, j))
    return pl.pallas_call(
        finish_kernel,
        name="finish",
        grid=(4,),
        out_shape=(
            jax.ShapeDtypeStruct(node_grad.shape, F32),
            jax.ShapeDtypeStruct((relations, depth), F32),
            jax.ShapeDtypeStruct((depth, depth), F32),
            jax.ShapeDtypeStruct((depth, depth), F32),
        ),
        in_specs=[
            tile,
            pl.BlockSpec((1, 16, 16, 128), lambda j: (j, 0, 0, 0)),
            pl.BlockSpec((1, 4, 16, 16, 128), lambda j: (j, 0, 0, 0, 0)),
        ],
        out_specs=(tile, pl.BlockSpec((relations, 128), lambda j: (0, j)), whole, whole),
        compiler_params=pltpu.CompilerParams(vmem_limit_bytes=8 * MIB),
    )(node_grad, summed, w_all)


def body(
    node_emb,
    rel_emb,
    w_in,
    w_self,
    rel_score,
    mirror_blocks,
    adj_values,
    adj_source,
    adj_target,
    adj_relation,
    live_blocks,
    query_head,
    query_rel,
    allowed,
    true_tail,
):
    wanted = mirror_blocks.reshape(1, 32)
    node_tiles = node_emb.reshape(4, 128, -1)
    mirrors, requests, self_part = fetch(node_tiles, wanted, w_self)
    partial, partial_low, query_part = forward(
        adj_source, adj_target, adj_relation, live_blocks,
        pltpu.with_memory_space_constraint(adj_values, pltpu.HBM),
        mirrors, rel_emb, query_rel, rel_score,
    )
    h, loss, agg_all, pre_all, agg_tiles = middle(
        partial_low,
        partial,
        self_part,
        w_in,
        query_part,
        query_head.reshape(1, -1),
        true_tail.reshape(1, -1),
        allowed.T,
    )
    tiles, rel_part, h_out, loss = backward(
        adj_source, adj_target, adj_relation, live_blocks, adj_values, agg_tiles, h, loss
    )
    node_grad, summed, w_all = give_back(
        tiles.reshape(2, 8, 4, 128, 256),
        rel_part,
        agg_all,
        pre_all,
        node_tiles,
        w_self,
        requests,
    )
    node_grad, rel_grad, w_in_grad, w_self_grad = finish(
        node_grad, summed, w_all, rel_emb.shape[0]
    )
    return (h_out, loss.reshape(-1), node_grad, rel_grad, w_in_grad, w_self_grad)


def solution(mesh):
    return jax.shard_map(
        body,
        mesh=mesh,
        in_specs=(
            P("cand", None, None),
            P("grp", None),
            P(),
            P(),
            P(),
            P("grp", "cand", None, None),
            P("grp", "cand", None, None, None),
            P("grp", "cand", None),
            P("grp", "cand", None),
            P("grp", "cand", None),
            P("grp", "cand"),
            P(),
            P(),
            P(),
            P(),
        ),
        out_specs=(P("cand", "grp", None), P(), P("cand", "grp", None), P("grp", None), P(), P()),
        check_vma=False,
    )
```

```python
import functools

import jax
import jax.numpy as jnp
from jax import lax
from jax.experimental import pallas as pl
from jax.experimental.pallas import tpu as pltpu
from jax.sharding import PartitionSpec as P

NEG_FILL = -1e30
MESH = pl.DeviceIdType.MESH
BF = jnp.bfloat16
F32 = jnp.float32
NN = (((1,), (0,)), ((), ()))
NT = (((1,), (1,)), ((), ()))
TN = (((0,), (0,)), ((), ()))
VMEM_SPEC = pl.BlockSpec(memory_space=pltpu.VMEM)
SMEM_SPEC = pl.BlockSpec(memory_space=pltpu.SMEM)
ANY_SPEC = pl.BlockSpec(memory_space=pl.ANY)
MIB = 1024 * 1024
STAGES_CAND = (("z", "x"), ("x", "z"))


def dot(a, b, dims=NN):
    return lax.dot_general(a, b, dims, preferred_element_type=F32)


class Place:
    def __init__(self):
        self.g = lax.axis_index("grp")
        self.c = lax.axis_index("cand")
        self.x = self.c // 8
        self.zk = self.c % 8
        self.z = self.zk // 2
        self.k = self.c % 2
        self.xk = self.x * 2 + self.k

    def dev(self, g, c):
        return {"grp": g, "cand": c}

    def at(self, axis):
        return {"x": self.x, "z": self.z, "y": self.g}[axis]

    def peer(self, axis, other):
        if axis == "y":
            return self.dev(other, self.c)
        if axis == "x":
            return self.dev(self.g, other * 8 + self.zk)
        return self.dev(self.g, self.x * 8 + other * 2 + self.k)

    def sibling(self):
        return self.dev(self.g, self.c + 1 - 2 * self.k)


def enter(devices):
    barrier = pltpu.get_barrier_semaphore()
    for device in devices:
        pl.semaphore_signal(barrier, inc=1, device_id=device, device_id_type=MESH)
    pl.semaphore_wait(barrier, len(devices))


class Wire:
    def __init__(self, send_sem, recv_sem):
        self.send_sem, self.recv_sem, self.count, self.sent = send_sem, recv_sem, 0, []

    def put(self, src, dst, device):
        at = self.count
        self.count += 1
        copy = pltpu.make_async_remote_copy(
            src_ref=src,
            dst_ref=dst,
            send_sem=self.send_sem.at[at],
            recv_sem=self.recv_sem.at[at],
            device_id=device,
            device_id_type=MESH,
        )
        copy.start()
        self.sent.append(copy)
        return copy

    def drain(self):
        for copy in self.sent:
            copy.wait_send()


def add_up(read_terms, write, count):
    chunk = min(count, 8)

    def one(i, carry):
        at = pl.ds(i * chunk, chunk)
        terms = read_terms(at)
        total = terms[0].astype(F32)
        for term in terms[1:]:
            total = total + term.astype(F32)
        write(at, total)
        return carry

    if count == chunk:
        one(0, 0)
    else:
        lax.fori_loop(0, count // chunk, one, 0)


class AllReduce:
    @staticmethod
    def scratch(shards, stages, height):
        depth = len(stages[0])
        shapes = [
            pltpu.VMEM((4, shards, height, 128), BF),
            pltpu.VMEM((2, shards, height, 128), BF),
        ]
        for level in range(depth):
            shapes.append(pltpu.VMEM((2, shards // 4**level, height, 128), BF))
            shapes.append(pltpu.VMEM((2, 3, shards // 4 ** (level + 1), height, 128), BF))
        return shapes

    def __init__(self, me, wire, shards, stages, refs, summed, w_all):
        self.me, self.wire, self.shards, self.stages = me, wire, shards, stages
        self.part, self.rcore = refs[:2]
        self.summed, self.w_all = summed, w_all
        depth = len(stages[0])
        self.acc = refs[2 : 2 + 2 * depth : 2]
        self.recv = refs[3 : 3 + 2 * depth : 2]
        self.sizes = [shards // 4 ** (i + 1) for i in range(depth)]

    def steps(self):
        me, wire = self.me, self.wire
        mine = 2 * me.k
        copy = wire.put(self.part.at[pl.ds(2 - mine, 2)], self.rcore, me.sibling())
        yield
        copy.wait_recv()
        for col in range(2):

            def write(at, value, col=col):
                self.acc[0][col, at] = value.astype(BF)

            add_up(
                lambda at, col=col: (self.part[mine + col, at], self.rcore[col, at]),
                write,
                self.shards,
            )
        offsets = [0, 0]
        history = []
        depth = len(self.sizes)
        for level in range(depth):
            size = self.sizes[level]
            copies = []
            for d in (1, 3, 2):
                for col in range(2):
                    axis = self.stages[col][level]
                    other = (me.at(axis) + d) % 4
                    copies.append(
                        wire.put(
                            self.acc[level].at[col, pl.ds(other * size, size)],
                            self.recv[level].at[col, d - 1],
                            me.peer(axis, other),
                        )
                    )
            yield
            for copy in copies:
                copy.wait_recv()
            for col in range(2):
                own = me.at(self.stages[col][level]) * size
                offsets[col] = offsets[col] + own

                def terms(at, col=col, own=own, level=level):
                    base = pl.ds(own + at.start, at.size)
                    return [self.acc[level][col, base]] + [
                        self.recv[level][col, d, at] for d in range(3)
                    ]

                def write(at, value, col=col, level=level):
                    if level + 1 < depth:
                        self.acc[level + 1][col, at] = value.astype(BF)
                    else:
                        final = value.astype(BF)
                        place = pl.ds(offsets[col] + at.start, at.size)
                        self.w_all[me.g, mine + col, place] = final[:, 0:16]
                        self.summed[mine + col, place] = final[:, 16:32]

                add_up(terms, write, size)
            history.append(tuple(offsets))
        copies = []
        for d in (1, 3, 2):
            for col in range(2):
                place = self.w_all.at[me.g, mine + col, pl.ds(offsets[col], self.sizes[-1])]
                copies.append(wire.put(place, place, me.peer("y", (me.g + d) % 4)))
        yield
        for copy in copies:
            copy.wait_recv()
        for level in reversed(range(depth)):
            size = self.sizes[level]
            copies = []
            for d in (1, 3, 2):
                for col in range(2):
                    axis = self.stages[col][level]
                    other = (me.at(axis) + d) % 4
                    shards = pl.ds(history[level][col], size)
                    for place in (
                        self.summed.at[mine + col, shards],
                        self.w_all.at[:, mine + col, shards],
                    ):
                        copies.append(wire.put(place, place, me.peer(axis, other)))
            yield
            for copy in copies:
                copy.wait_recv()


def fetch_kernel(
    node, wanted_v, w_self,
    mirrors, requests, self_part,
    wanted_row, request_s, staged, send_sem, recv_sem, local_sem, *gathered,
):
    me = Place()
    devices = []
    for e in range(1, 8):
        devices.append(me.dev(me.g, me.x * 8 + (me.zk + e) % 8))
    for e in range(1, 8):
        other = (me.xk + e) % 8
        devices.append(me.dev(me.g, (other // 2) * 8 + me.z * 2 + other % 2))
    for d in (1, 2, 3):
        devices.append(me.peer("y", (me.g + d) % 4))
    enter(devices)
    wire = Wire(send_sem, recv_sem)
    wanted_row[...] = jnp.zeros_like(wanted_row)
    wanted_row[:, 0:32] = wanted_v[...]
    halves = (pl.ds(0, 256), pl.ds(256, 256))
    first = {}
    for d in (1, 3, 2):
        for col, axis in ((0, "x"), (1, "z")):
            other = (me.at(axis) + d) % 4
            first[col, d] = wire.put(
                node.at[me.g, :, halves[col]],
                gathered[3 * col + d - 1].at[me.g],
                me.peer(axis, other),
            )
    asks = []
    for e in range(1, 8):
        for col in range(2):
            asks.append(
                wire.put(
                    wanted_row,
                    requests.at[8 * col + (me.zk if col == 0 else me.xk)],
                    devices[7 * col + e - 1],
                )
            )
    requests[me.zk] = wanted_row[...]
    requests[8 + me.xk] = wanted_row[...]
    spread = {}

    def pass_on(d):
        for col in range(2):
            first[col, d].wait_recv()
            place = gathered[3 * col + d - 1].at[me.g]
            spread[col, d] = [
                wire.put(place, place, me.peer("y", (me.g + e) % 4)) for e in (1, 3, 2)
            ]

    pass_on(1)
    for copy in asks:
        copy.wait_recv()
    local = pltpu.make_async_copy(requests, request_s, local_sem)
    local.start()
    local.wait()
    moved = []
    for d in (0, 1, 3, 2):
        for col, axis in ((0, "x"), (1, "z")):
            if d:
                for copy in spread[col, d]:
                    copy.wait_recv()
            origin = (me.at(axis) + 4 - d) % 4
            own_slot = me.zk if col == 0 else me.xk
            owner = origin * 8 + me.zk if col == 0 else me.x * 8 + origin * 2 + me.k
            for e in range(8):
                slot = (own_slot + e) % 8
                index = request_s[8 * col + slot, 0, owner]
                if d:
                    tile = gathered[3 * col + d - 1][index]
                else:
                    tile = node[index, :, 256 * col : 256 * col + 256]
                if e == 0:
                    mirrors[col, own_slot, origin] = tile
                else:
                    staged[col, e - 1, d] = tile
                    moved.append(
                        wire.put(
                            staged.at[col, e - 1, d],
                            mirrors.at[col, own_slot, origin],
                            devices[7 * col + e - 1],
                        )
                    )
        if d == 0:
            pass_on(3)
            pass_on(2)
    self_part[...] = dot(node[me.g], w_self[...])
    for copy in moved:
        copy.wait_recv()
    wire.drain()


def fetch(node_tiles, wanted, w_self):
    depth = node_tiles.shape[2]
    copies = 6 + 14 + 56 + 18
    return pl.pallas_call(
        fetch_kernel,
        name="fetch",
        cost_estimate=pl.CostEstimate(flops=67108864, bytes_accessed=100000000, transcendentals=0),
        out_shape=(
            jax.ShapeDtypeStruct((2, 8, 4, 128, 256), BF),
            jax.ShapeDtypeStruct((16, 1, 128), jnp.int32),
            jax.ShapeDtypeStruct((128, depth), F32),
        ),
        in_specs=[VMEM_SPEC] * 3,
        out_specs=(VMEM_SPEC,) * 3,
        scratch_shapes=[
            pltpu.VMEM((1, 128), jnp.int32),
            pltpu.SMEM((16, 1, 128), jnp.int32),
            pltpu.VMEM((2, 7, 4, 128, 256), BF),
            pltpu.SemaphoreType.DMA((copies,)),
            pltpu.SemaphoreType.DMA((copies,)),
            pltpu.SemaphoreType.DMA,
            *[pltpu.VMEM((4, 128, 256), BF)] * 6,
        ],
        compiler_params=pltpu.CompilerParams(
            collective_id=0, has_side_effects=True, vmem_limit_bytes=16 * MIB
        ),
    )(node_tiles, wanted, w_self)


GROUP = 24


def slots_of(source):
    x, zk = source // 8, source % 8
    z, k = zk // 2, zk % 2
    return zk * 4 + x, (x * 2 + k) * 4 + z


def forward_kernel(
    source, target, relation, live, values, mirrors, rel_emb, query_rel, rel_score,
    out, out_low, query_part,
):
    step = pl.program_id(0)
    first = (lax.axis_index("grp") * 2 + lax.axis_index("cand") % 2) * 128

    for j in range(16):
        row = step * 16 + j
        query_part[pl.ds(row, 1), :] = rel_score[pl.ds(query_rel[first + row], 1), :]

    @pl.when(step == 0)
    def _():
        out[...] = jnp.zeros_like(out)

    count = live[0, 0]

    @pl.when(step * GROUP < count)
    def _():
        for j in range(GROUP):
            b = step * GROUP + j
            slots = slots_of(source[0, 0, b])
            t = target[0, 0, b]
            block = values[0, 0, j]
            block = jnp.where(b < count, block, jnp.zeros_like(block))
            row = rel_emb[pl.ds(relation[0, 0, b], 1), :]
            for col in range(2):
                part = slice(256 * col, 256 * col + 256)
                composed = (mirrors[col, slots[col]].astype(F32) - row[:, part]).astype(BF)
                out[t, :, part] += dot(block, composed)

    @pl.when(step == pl.num_programs(0) - 1)
    def _():
        for t in range(4):
            out_low[t] = out[t].astype(BF)


def adjacency_specs(blocks):
    return [SMEM_SPEC] * 4 + [
        pl.BlockSpec((1, 1, GROUP, 128, 128), lambda i: (0, 0, i, 0, 0)),
    ]


def forward(
    adj_source, adj_target, adj_relation, live_blocks, adj_values, mirrors, rel_emb, query_rel, rel_score
):
    blocks = adj_values.shape[2]
    depth = rel_score.shape[1]
    return pl.pallas_call(
        forward_kernel,
        name="forward_blocks",
        cost_estimate=pl.CostEstimate(flops=3221225472, bytes_accessed=30000000, transcendentals=0),
        grid=(blocks // GROUP,),
        out_shape=(
            jax.ShapeDtypeStruct((4, 128, depth), F32),
            jax.ShapeDtypeStruct((4, 128, depth), BF),
            jax.ShapeDtypeStruct((128, depth), F32),
        ),
        in_specs=adjacency_specs(blocks) + [VMEM_SPEC] * 2 + [SMEM_SPEC, VMEM_SPEC],
        out_specs=(VMEM_SPEC,) * 3,
        compiler_params=pltpu.CompilerParams(vmem_limit_bytes=16 * MIB),
    )(
        adj_source, adj_target, adj_relation, live_blocks, adj_values,
        mirrors.reshape(2, 32, 128, 256), rel_emb, query_rel, rel_score,
    )


def backward_kernel(
    source, target, relation, live, values, agg, h_in, loss_in,
    tiles_out, rel_out, h_out, loss_out, tiles,
):
    step = pl.program_id(0)

    @pl.when(step == 0)
    def _():
        def clear(i, carry):
            for col in range(2):
                tiles[col, i] = jnp.zeros((128, 256), F32)
            return carry

        lax.fori_loop(0, 32, clear, 0)
        rel_out[...] = jnp.zeros_like(rel_out)
        h_out[...] = h_in[...]
        for j in range(8):
            loss_out[j : j + 1, :] = loss_in[j]

    count = live[0, 0]

    @pl.when(step * GROUP < count)
    def _():
        for j in range(GROUP):
            b = step * GROUP + j
            slots = slots_of(source[0, 0, b])
            r = pl.ds(relation[0, 0, b], 1)
            block = values[0, 0, j]
            block = jnp.where(b < count, block, jnp.zeros_like(block))
            grad = dot(block, agg[target[0, 0, b]], TN)
            rel_out[r, :] -= jnp.sum(grad, axis=0, keepdims=True)
            for col in range(2):
                tiles[col, slots[col]] += grad[:, 256 * col : 256 * col + 256]

    @pl.when(step == pl.num_programs(0) - 1)
    def _():
        def store(i, carry):
            for col in range(2):
                tiles_out[col, i] = tiles[col, i].astype(BF)
            return carry

        lax.fori_loop(0, 32, store, 0)


def backward(adj_source, adj_target, adj_relation, live_blocks, adj_values, agg_tiles, h, loss):
    blocks = adj_values.shape[2]
    return pl.pallas_call(
        backward_kernel,
        name="backward_blocks",
        cost_estimate=pl.CostEstimate(flops=3221225472, bytes_accessed=30000000, transcendentals=0),
        grid=(blocks // GROUP,),
        out_shape=(
            jax.ShapeDtypeStruct((2, 32, 128, 256), BF),
            jax.ShapeDtypeStruct((256, 512), F32),
            jax.ShapeDtypeStruct(h.shape, h.dtype),
            jax.ShapeDtypeStruct((8, 128), F32),
        ),
        in_specs=adjacency_specs(blocks) + [VMEM_SPEC] * 3,
        out_specs=(VMEM_SPEC,) * 4,
        scratch_shapes=[pltpu.VMEM((2, 32, 128, 256), F32)],
        compiler_params=pltpu.CompilerParams(vmem_limit_bytes=24 * MIB),
    )(adj_source, adj_target, adj_relation, live_blocks, adj_values, agg_tiles, h, loss)


def exchange_sum(me, wire, send, recv, out, during=None):
    for level in range(2):
        copies = []
        for d in (1, 3, 2):
            for col in range(2):
                axis = STAGES_CAND[col][level]
                other = (me.at(axis) + d) % 4
                copies.append(
                    wire.put(
                        send.at[level, col], recv.at[level, col, d - 1], me.peer(axis, other)
                    )
                )
        if level == 0 and during is not None:
            during()
        for copy in copies:
            copy.wait_recv()
        for col in range(2):
            total = send[level, col].astype(F32)
            for d in range(3):
                total = total + recv[level, col, d].astype(F32)
            if level == 0:
                send[1, col] = total.astype(BF)
            else:
                out[:, 256 * col : 256 * col + 256] = total


class GatherY:
    def __init__(self, me, wire, ref, slot):
        self.me, self.wire, self.ref, self.slot = me, wire, ref, slot
        self.near = (me.peer("y", (me.g + 1) % 4), me.peer("y", (me.g + 3) % 4))
        self.first = [self.put(0, 0, 0), self.put(0, 1, 1)]
        self.second = [self.put(0, 1, 0), self.put(0, 0, 1)]

    def put(self, d, half, way):
        place = self.ref.at[self.slot(d), pl.ds(64 * half, 64)]
        return self.wire.put(place, place, self.near[way])

    def neighbours(self):
        self.first[0].wait_recv()
        far = [self.put(1, 0, 0)]
        self.first[1].wait_recv()
        far.append(self.put(3, 1, 1))
        for copy in self.second:
            copy.wait_recv()
        self.far = far

    def opposite(self):
        for copy in self.far:
            copy.wait_recv()


def middle_kernel(
    partial_low, partial, self_part, w_in, query_part, query_head, true_tail, allowed,
    h_out, loss, agg_all, pre_all, agg_tiles,
    share_recv, act, column, head_send, head_recv, queries, q_hi, q_lo, scores, stats,
    h_sq, grad_send, grad_recv, summed, g_hi, g_lo, rows, core_send, core_recv, y_send, y_recv,
    send_sem, recv_sem,
):
    me = Place()
    plane = []
    for dx, dz in sorted(
        [(i, j) for i in range(4) for j in range(4) if i or j],
        key=lambda p: -(min(p[0], 4 - p[0]) + min(p[1], 4 - p[1])),
    ):
        plane.append(
            me.dev(me.g, ((me.x + dx) % 4) * 8 + ((me.z + dz) % 4) * 2 + me.k)
        )
    enter(
        [me.sibling()] + [me.peer("y", (me.g + d) % 4) for d in (1, 2, 3)] + plane
    )
    wire = Wire(send_sem, recv_sem)
    count = true_tail.shape[1]
    scale = 512 ** (-0.5)
    group = me.g * 2 + me.k
    lanes = pl.ds(pl.multiple_of(group * 128, 128), 128)
    first_chip = me.x * 8 + me.z * 2
    base = first_chip * 512

    def to_y(ref, at, order=(1, 3, 2)):
        copies = {}
        for d in order:
            copies[d] = wire.put(ref.at[at], ref.at[at], me.peer("y", (me.g + d) % 4))
        return copies

    copies = []
    for d in (1, 3, 2):
        other = (me.g + d) % 4
        copies.append(wire.put(partial_low.at[other], share_recv.at[d - 1], me.peer("y", other)))
    for copy in copies:
        copy.wait_recv()
    total = partial[me.g]
    for d in range(3):
        total = total + share_recv[d].astype(F32)
    agg = total.astype(BF)
    activated = jnp.tanh(dot(agg, w_in[...]) + self_part[...])
    h = activated.astype(BF)
    own_chunk = me.k * 4 + me.g
    column[own_chunk] = h
    gather_h = GatherY(me, wire, column, lambda d: me.k * 4 + (me.g + 4 - d) % 4)
    from_sibling = [wire.put(column.at[own_chunk], column.at[own_chunk], me.sibling())]
    h_out[0] = h
    act[...] = activated
    agg_all[me.g] = agg
    gather_h.neighbours()
    for d in (1, 3, 2):
        if d == 2:
            gather_h.opposite()
        chunk = me.k * 4 + (me.g + 4 - d) % 4
        from_sibling.append(wire.put(column.at[chunk], column.at[chunk], me.sibling()))

    agg_copies = to_y(agg_all, me.g)

    head_row = jnp.broadcast_to(query_head[:, lanes] - base, (128, 128))
    head_col = head_row.astype(F32).T
    lane_ids = lax.broadcasted_iota(jnp.int32, (128, 128), 1).astype(F32)
    row_ids = lax.broadcasted_iota(jnp.int32, (128, 128), 0)
    for copy in from_sibling:
        copy.wait_recv()
    part = jnp.zeros((128, 512), F32)
    for j in range(8):
        pick = jnp.where(head_col == lane_ids + 128.0 * j, 1.0, 0.0).astype(BF)
        part = part + dot(pick, column[j])
    for col in range(2):
        head_send[0, col] = part[:, 256 * col : 256 * col + 256].astype(BF)

    def squares():
        for j in range(8):
            h32 = column[j].astype(F32)
            h_sq[j] = jnp.broadcast_to(jnp.sum(h32 * h32, axis=1, keepdims=True), (128, 128))

    exchange_sum(me, wire, head_send, head_recv, summed, squares)

    q = summed[...] + query_part[...]
    queries[...] = q
    high = q.astype(BF)
    q_hi[...] = high
    q_lo[...] = (q - high.astype(F32)).astype(BF)
    square = jnp.zeros((128, 128), F32)
    for j in range(4):
        piece = q[:, 128 * j : 128 * j + 128]
        square = square + piece * piece
    q_sq = jnp.sum(square.T, axis=0, keepdims=True)
    tail_row = jnp.broadcast_to(true_tail[:, lanes] - base, (128, 128))
    kinds = allowed[:, lanes]

    def allowed_row(j):
        hit = jnp.where(kinds == first_chip * 4 + j, 1.0, 0.0)
        return jnp.max(hit, axis=0, keepdims=True)

    masks = [jnp.broadcast_to(allowed_row(j), (128, 128)) > 0.5 for j in range(8)]
    tops, truths = [], []
    for j in range(8):
        cross = dot(column[j], q_hi[...], NT) + dot(column[j], q_lo[...], NT)
        score = -scale * (q_sq + h_sq[j] - 2.0 * cross)
        scores[j] = score
        tops.append(jnp.max(jnp.where(masks[j], score, NEG_FILL), axis=0, keepdims=True))
        truths.append(
            jnp.sum(
                jnp.where(row_ids + 128 * j == tail_row, score, 0.0), axis=0, keepdims=True
            )
        )
    top = functools.reduce(jnp.maximum, tops)
    weight = jnp.zeros((1, 128), F32)
    for j in range(8):
        weight = weight + jnp.sum(
            jnp.exp(jnp.where(masks[j], scores[j] - top, NEG_FILL)), axis=0, keepdims=True
        )
    stats[0, 0:1, :] = top
    stats[0, 1:2, :] = weight
    stats[0, 2:3, :] = functools.reduce(lambda a, b: a + b, truths)

    copies = [wire.put(stats.at[0], stats.at[e + 1], plane[e]) for e in range(15)]
    for copy in copies:
        copy.wait_recv()
    members = [stats[m] for m in range(16)]
    tops = [m[0:1, :] for m in members]
    top = functools.reduce(jnp.maximum, tops)
    weight = jnp.zeros((1, 128), F32)
    truth = jnp.zeros((1, 128), F32)
    for m in range(16):
        weight = weight + members[m][1:2, :] * jnp.exp(tops[m] - top)
        truth = truth + members[m][2:3, :]
    log_norm = top + jnp.log(weight)
    loss[group] = log_norm - truth
    loss_copies = to_y(loss, group)
    rest_sum = (weight * jnp.exp(top - log_norm) - 1.0) / count
    rest_col = jnp.broadcast_to(rest_sum, (128, 128)).T

    part = jnp.zeros((128, 512), F32)
    for j in range(8):
        prob = jnp.exp(jnp.where(masks[j], scores[j] - log_norm, NEG_FILL))
        tail = jnp.where(row_ids + 128 * j == tail_row, 1.0, 0.0)
        grad = (prob - tail) / count
        scores[j] = grad
        high = grad.astype(BF)
        g_hi[j] = high
        g_lo[j] = (grad - high.astype(F32)).astype(BF)
        flipped = grad.T
        high = flipped.astype(BF)
        low = (flipped - high.astype(F32)).astype(BF)
        part = part + (dot(high, column[j]) + dot(low, column[j]))
    for col in range(2):
        grad_send[0, col] = part[:, 256 * col : 256 * col + 256].astype(BF)

    def candidates():
        for j in range(8):
            sums = jnp.sum(scores[j], axis=1, keepdims=True)
            rows[j] = (
                dot(g_hi[j], q_hi[...]) + dot(g_hi[j], q_lo[...]) + dot(g_lo[j], q_hi[...])
            ) - column[j].astype(F32) * sums

    exchange_sum(me, wire, grad_send, grad_recv, summed, candidates)

    query_grad = jnp.concatenate(
        [
            summed[:, 128 * j : 128 * j + 128] - queries[:, 128 * j : 128 * j + 128] * rest_col
            for j in range(4)
        ],
        axis=1,
    ).astype(BF)

    def row_part(chunk):
        pick = jnp.where(row_ids + 128 * chunk == head_row, 1.0, 0.0).astype(BF)
        return rows[chunk] + dot(pick, query_grad)

    order = (1, 3, 2, 0)
    core_copies = {}
    for at, d in enumerate(order):
        chunk = (1 - me.k) * 4 + (me.g + d) % 4
        core_send[d] = row_part(chunk).astype(BF)
        core_copies[d] = wire.put(core_send.at[d], core_recv.at[d], me.sibling())
    y_copies = []
    for d in order:
        own = row_part(me.k * 4 + (me.g + d) % 4)
        core_copies[d].wait_recv()
        total = own + core_recv[d].astype(F32)
        if d:
            y_send[d - 1] = total.astype(BF)
            y_copies.append(
                wire.put(y_send.at[d - 1], y_recv.at[d - 1], me.peer("y", (me.g + d) % 4))
            )
    for d in (1, 3, 2):
        loss_copies[d].wait_recv()
    loss_rows = []
    for d in range(4):
        row = ((me.g + d) % 4) * 2 + me.k
        loss_rows.append(wire.put(loss.at[row], loss.at[row], me.sibling()))
    for copy in y_copies:
        copy.wait_recv()
    for d in range(3):
        total = total + y_recv[d].astype(F32)
    activated = act[...]
    pre_grad = (((2.0 * scale) * total) * (1.0 - activated * activated)).astype(BF)
    pre_all[me.g] = pre_grad
    gather_pre = GatherY(me, wire, pre_all, lambda d: (me.g + 4 - d) % 4)
    agg_tiles[me.g] = dot(pre_grad, w_in[...], NT).astype(BF)
    gather_pre.neighbours()
    for d in (1, 3, 2):
        if d == 2:
            gather_pre.opposite()
        other = (me.g + 4 - d) % 4
        agg_tiles[other] = dot(pre_all[other], w_in[...], NT).astype(BF)
    for d in (1, 3, 2):
        agg_copies[d].wait_recv()
    for copy in loss_rows:
        copy.wait_recv()
    wire.drain()


def middle(partial_low, partial, self_part, w_in, query_part, query_head, true_tail, allowed):
    depth = w_in.shape[0]
    copies = 3 + 6 + 4 + 3 + 12 + 15 + 3 + 12 + 4 + 3 + 4 + 6
    tile_bf = jax.ShapeDtypeStruct((4, 128, depth), BF)
    return pl.pallas_call(
        middle_kernel,
        name="middle",
        cost_estimate=pl.CostEstimate(flops=2000000000, bytes_accessed=150000000, transcendentals=0),
        out_shape=(
            jax.ShapeDtypeStruct((1, 128, depth), BF),
            jax.ShapeDtypeStruct((8, 1, 128), F32),
            tile_bf,
            tile_bf,
            tile_bf,
        ),
        in_specs=[VMEM_SPEC] * 8,
        out_specs=(VMEM_SPEC,) * 5,
        scratch_shapes=[
            pltpu.VMEM((3, 128, depth), BF),
            pltpu.VMEM((128, depth), F32),
            pltpu.VMEM((8, 128, depth), BF),
            pltpu.VMEM((2, 2, 128, 256), BF),
            pltpu.VMEM((2, 2, 3, 128, 256), BF),
            pltpu.VMEM((128, depth), F32),
            pltpu.VMEM((128, depth), BF),
            pltpu.VMEM((128, depth), BF),
            pltpu.VMEM((8, 128, 128), F32),
            pltpu.VMEM((16, 8, 128), F32),
            pltpu.VMEM((8, 128, 128), F32),
            pltpu.VMEM((2, 2, 128, 256), BF),
            pltpu.VMEM((2, 2, 3, 128, 256), BF),
            pltpu.VMEM((128, depth), F32),
            pltpu.VMEM((8, 128, 128), BF),
            pltpu.VMEM((8, 128, 128), BF),
            pltpu.VMEM((8, 128, depth), F32),
            pltpu.VMEM((4, 128, depth), BF),
            pltpu.VMEM((4, 128, depth), BF),
            pltpu.VMEM((3, 128, depth), BF),
            pltpu.VMEM((3, 128, depth), BF),
            pltpu.SemaphoreType.DMA((copies,)),
            pltpu.SemaphoreType.DMA((copies,)),
        ],
        compiler_params=pltpu.CompilerParams(
            collective_id=1, has_side_effects=True, vmem_limit_bytes=22 * MIB
        ),
    )(partial_low, partial, self_part, w_in, query_part, query_head, true_tail, allowed)


def return_kernel(
    n_ar,
    tiles, rel_part, agg_all, pre_all, node, w_self, requests,
    node_grad, summed, w_all,
    arrived, shipped, y_recv, x_send, joined, self_grad, *rest,
):
    ar_refs = rest[:n_ar]
    send_sem, recv_sem, local_sem = rest[n_ar:]
    me = Place()
    devices = []
    for e in range(1, 8):
        devices.append(me.dev(me.g, me.x * 8 + (me.zk + e) % 8))
    for e in range(1, 8):
        other = (me.xk + e) % 8
        devices.append(me.dev(me.g, (other // 2) * 8 + me.z * 2 + other % 2))
    for d in (1, 2, 3):
        devices.append(me.peer("y", (me.g + d) % 4))
    enter(devices)
    wire = Wire(send_sem, recv_sem)
    reduce = AllReduce(me, wire, 16, STAGES_CAND, ar_refs, summed, w_all)
    steps = reduce.steps()

    def advance():
        next(steps, None)

    axes = ((0, "x"), (1, "z"))
    own_slots = (me.zk, me.xk)
    moved = {}

    rounds = ((1, 0, 128), (3, 0, 128), (2, 0, 128), (0, 0, 64), (0, 64, 64))

    def send_round(at):
        d, start, size = rounds[at]
        part = pl.ds(start, size)
        for col, axis in axes:
            place = (me.at(axis) + d) % 4
            for e in range(1, 8):
                slot = (own_slots[col] + e) % 8
                moved[at, col, e] = wire.put(
                    tiles.at[col, slot, place, part],
                    arrived.at[col, own_slots[col], place, part],
                    devices[7 * col + e - 1],
                )

    send_round(0)
    local = []
    for col in range(2):
        copy = pltpu.make_async_copy(
            tiles.at[col, own_slots[col]], arrived.at[col, own_slots[col]], local_sem.at[col]
        )
        copy.start()
        local.append(copy)
    cols = pl.ds(pl.multiple_of(me.g * 128, 128), 128)
    right = pre_all[:, :, cols].reshape(512, 128)
    for which, left in ((0, agg_all), (1, node)):
        for q in range(4):
            turned = left[:, :, 128 * q : 128 * q + 128].astype(F32).reshape(512, 128).T.astype(BF)
            reduce.part[2 * which + q // 2, 8 * (q % 2) : 8 * (q % 2) + 8, 0:16] = (
                dot(turned, right).reshape(8, 16, 128).astype(BF)
            )
    for q in range(2):
        for j in range(4):
            reduce.part[j, 8 * q : 8 * q + 8, 16:32] = (
                rel_part[128 * q : 128 * q + 128, 128 * j : 128 * j + 128]
                .reshape(8, 16, 128)
                .astype(BF)
            )
    advance()
    send_round(1)
    self_grad[...] = dot(pre_all[me.g], w_self[...], NT)
    advance()
    for copy in local:
        copy.wait()
    over_y = {}
    second = []

    def combine(d, col):
        for at in range(len(rounds)):
            if rounds[at][0] == d:
                for copy in over_y[at, col]:
                    copy.wait_recv()
        total = shipped[col, d, me.g].astype(F32)
        for m in range(3):
            total = total + y_recv[col, d, m].astype(F32)
        return total

    def send_combined(d):
        for col, axis in axes:
            x_send[col, d - 1] = combine(d, col).astype(BF)
            second.append(
                wire.put(
                    x_send.at[col, d - 1],
                    joined.at[col, d - 1],
                    me.peer(axis, (me.at(axis) + d) % 4),
                )
            )

    for at, (d, start, size) in enumerate(rounds):
        for col, axis in axes:
            place = (me.at(axis) + d) % 4
            owner = place * 8 + me.zk if col == 0 else me.x * 8 + place * 2 + me.k
            for e in range(1, 8):
                moved[at, col, e].wait_recv()
            index = [requests[8 * col + m, 0, owner] for m in range(8)]
            for part in range(size // 32):
                rows = pl.ds(start + part * 32, 32)
                values = [arrived[col, m, place, rows, :].astype(F32) for m in range(8)]
                for s in range(4):
                    total = jnp.zeros((32, 256), F32)
                    for m in range(8):
                        total = total + jnp.where(index[m] == s, values[m], 0.0)
                    shipped[col, d, s, rows, :] = total.astype(BF)
            over_y[at, col] = []
            rows = pl.ds(start, size)
            for e in (1, 3, 2):
                s = (me.g + e) % 4
                over_y[at, col].append(
                    wire.put(
                        shipped.at[col, d, s, rows],
                        y_recv.at[col, d, e - 1, rows],
                        me.peer("y", s),
                    )
                )
        advance()
        if at + 2 < len(rounds):
            send_round(at + 2)
        if at and rounds[at - 1][0]:
            send_combined(rounds[at - 1][0])
    advance()
    pair = pl.ds(2 * me.k, 2)
    last = [
        wire.put(summed.at[pair], summed.at[pair], me.sibling()),
        wire.put(w_all.at[:, pair], w_all.at[:, pair], me.sibling()),
    ]
    for copy in second:
        copy.wait_recv()
    for col in range(2):
        total = combine(0, col)
        for m in range(3):
            total = total + joined[col, m].astype(F32)
        node_grad[0, :, 256 * col : 256 * col + 256] = (
            total + self_grad[:, 256 * col : 256 * col + 256]
        )
    for copy in last:
        copy.wait_recv()
    wire.drain()


def give_back(tiles, rel_part, agg_all, pre_all, node_tiles, w_self, requests):
    depth = w_self.shape[0]
    ar = AllReduce.scratch(16, STAGES_CAND, 32)
    copies = 70 + 30 + 6 + (1 + 12 + 6 + 24) + 2
    return pl.pallas_call(
        functools.partial(return_kernel, len(ar)),
        name="give_back",
        cost_estimate=pl.CostEstimate(flops=1000000000, bytes_accessed=120000000, transcendentals=0),
        out_shape=(
            jax.ShapeDtypeStruct((1, 128, depth), F32),
            jax.ShapeDtypeStruct((4, 16, 16, 128), BF),
            jax.ShapeDtypeStruct((4, 4, 16, 16, 128), BF),
        ),
        in_specs=[ANY_SPEC] + [VMEM_SPEC] * 5 + [SMEM_SPEC],
        out_specs=(VMEM_SPEC,) * 3,
        scratch_shapes=[
            pltpu.VMEM((2, 8, 4, 128, 256), BF),
            pltpu.VMEM((2, 4, 4, 128, 256), BF),
            pltpu.VMEM((2, 4, 3, 128, 256), BF),
            pltpu.VMEM((2, 3, 128, 256), BF),
            pltpu.VMEM((2, 3, 128, 256), BF),
            pltpu.VMEM((128, depth), F32),
            *ar,
            pltpu.SemaphoreType.DMA((copies,)),
            pltpu.SemaphoreType.DMA((copies,)),
            pltpu.SemaphoreType.DMA((2,)),
        ],
        compiler_params=pltpu.CompilerParams(
            collective_id=2, has_side_effects=True, vmem_limit_bytes=20 * MIB
        ),
    )(tiles, rel_part, agg_all, pre_all, node_tiles, w_self, requests)


def finish_kernel(node_in, summed, w_all, node_grad, rel_grad, w_in_grad, w_self_grad):
    node_grad[...] = node_in[...]
    whole = summed[0].astype(F32).reshape(256, 128)
    rel_grad[...] = whole[: rel_grad.shape[0]]
    for q in range(2):
        rows = slice(256 * q, 256 * q + 256)
        for at, target in ((q, w_in_grad), (2 + q, w_self_grad)):
            target[rows, :] = w_all[0, at].astype(F32).reshape(256, 128)


def finish(node_grad, summed, w_all, relations):
    depth = node_grad.shape[2]
    tile = pl.BlockSpec((1, 128, 128), lambda j: (0, 0, j))
    whole = pl.BlockSpec((depth, 128), lambda j: (0, j))
    return pl.pallas_call(
        finish_kernel,
        name="finish",
        grid=(4,),
        out_shape=(
            jax.ShapeDtypeStruct(node_grad.shape, F32),
            jax.ShapeDtypeStruct((relations, depth), F32),
            jax.ShapeDtypeStruct((depth, depth), F32),
            jax.ShapeDtypeStruct((depth, depth), F32),
        ),
        in_specs=[
            tile,
            pl.BlockSpec((1, 16, 16, 128), lambda j: (j, 0, 0, 0)),
            pl.BlockSpec((1, 4, 16, 16, 128), lambda j: (j, 0, 0, 0, 0)),
        ],
        out_specs=(tile, pl.BlockSpec((relations, 128), lambda j: (0, j)), whole, whole),
        compiler_params=pltpu.CompilerParams(vmem_limit_bytes=8 * MIB),
    )(node_grad, summed, w_all)


def stay(array):
    return pltpu.with_memory_space_constraint(array, pltpu.HBM)


def body(
    node_emb,
    rel_emb,
    w_in,
    w_self,
    rel_score,
    mirror_blocks,
    adj_values,
    adj_source,
    adj_target,
    adj_relation,
    live_blocks,
    query_head,
    query_rel,
    allowed,
    true_tail,
):
    wanted = mirror_blocks.reshape(1, 32)
    node_tiles = node_emb.reshape(4, 128, -1)
    mirrors, requests, self_part = fetch(stay(node_tiles), stay(wanted), stay(w_self))
    partial, partial_low, query_part = forward(
        stay(adj_source), stay(adj_target), stay(adj_relation), live_blocks, stay(adj_values),
        mirrors, stay(rel_emb), stay(query_rel), stay(rel_score),
    )
    h, loss, agg_all, pre_all, agg_tiles = middle(
        partial_low,
        partial,
        self_part,
        w_in,
        query_part,
        query_head.reshape(1, -1),
        true_tail.reshape(1, -1),
        allowed.T,
    )
    tiles, rel_part, h_out, loss = backward(
        adj_source, adj_target, adj_relation, live_blocks, adj_values, agg_tiles, h, loss
    )
    node_grad, summed, w_all = give_back(
        tiles.reshape(2, 8, 4, 128, 256),
        rel_part,
        agg_all,
        pre_all,
        node_tiles,
        w_self,
        requests,
    )
    node_grad, rel_grad, w_in_grad, w_self_grad = finish(
        node_grad, summed, w_all, rel_emb.shape[0]
    )
    return (h_out, loss.reshape(-1), node_grad, rel_grad, w_in_grad, w_self_grad)


def solution(mesh):
    return jax.shard_map(
        body,
        mesh=mesh,
        in_specs=(
            P("cand", None, None),
            P("grp", None),
            P(),
            P(),
            P(),
            P("grp", "cand", None, None),
            P("grp", "cand", None, None, None),
            P("grp", "cand", None),
            P("grp", "cand", None),
            P("grp", "cand", None),
            P("grp", "cand"),
            P(),
            P(),
            P(),
            P(),
        ),
        out_specs=(P("cand", "grp", None), P(), P("cand", "grp", None), P("grp", None), P(), P()),
        check_vma=False,
    )
```
